256 devices in a mesh: dp: 32 (over z, y), mp: 8 (over x, core).
Axes of the slice: x: 4, y: 4, z: 8, core: 2. Of those that a mesh axis runs over, the one named last changes fastest.
Arguments:
- tokens: bfloat16 [8192, 4096], P('dp', 'mp'), may hold values from -24 to 24
- cotangent: bfloat16 [8192, 4096], P('dp', 'mp'), may hold values from -6 to 6
- gain_dec: float32 [4096], replicated, may hold values from 0.1 to 1.9
- w_query: bfloat16 [4096, 4096], P(None, 'mp'), may hold values from -1 to 1
- w_out: bfloat16 [4096, 4096], P('mp'), may hold values from -0.5 to 0.5
- encodings: bfloat16 [256, 128, 896], P('dp', 'mp'), may hold values from -24 to 24
- gain_enc: float32 [896], replicated, may hold values from 0.1 to 1.9
- w_key: bfloat16 [896, 4096], P(None, 'mp'), may hold values from -1 to 1
- w_value: bfloat16 [896, 4096], P(None, 'mp'), may hold values from -0.1875 to 0.1875
- gain_post: float32 [4096], replicated, may hold values from 0.1 to 1.9
- neighbour_ids: int32 [128, 2], P('dp'), may hold values from 0 to 255, as said below
Outputs:
- mixed: bfloat16 [8192, 4096], P('dp', 'mp')
- ffn_input: bfloat16 [8192, 4096], P('dp', 'mp')
- d_encodings: bfloat16 [256, 128, 896], P('dp', 'mp')
The draws below stay inside these ranges and needn't reach their ends.
Inputs may be any that keep to these rules, and one draw needn't show every extreme that they name: `neighbour_ids`: encoder row g is held by index g // 8 of dp. Every encoder row is retrieved by exactly one block. The blocks of one index of dp retrieve at most 1 row held by any one index of dp, and exactly 1 from some.
All inputs are finite; a program needn't handle non-finite values.
Results may differ from the reference program's by a relative error of at most 0.02.
The reference program's roundings to bfloat16 on the way count: a program that leaves them out, or rounds other values in their place, can miss the bound.
Values may be sent and summed in bfloat16 or wider, within the bound.
No kernel may reach another device: no remote copies, remote signals or barrier semaphores. Data moves between devices by JAX's collectives and lax.ppermute only.
A program may use at most 64 MiB of HBM per device.

```python
import math
import jax
import jax.numpy as jnp
from jax import lax

D = 4096
HEADS = 32
HD = 128
EW = 896
BLOCK = 64
NLEN = 128
NEIGH = 2
TOK_DEV = 256
BLOCKS_DEV = 4
REFS = 8
TOKENS = 8192
ROWS = 256
N_DP = 32
N_MP = 8


def scaled_field(key, shape):
    k_base, k_rows, k_cols = jax.random.split(key, 3)
    base = jnp.clip(jax.random.normal(k_base, shape, jnp.float32), -4.0, 4.0)
    row_scale = jnp.exp(jax.random.uniform(k_rows, shape[:-1] + (1,), jnp.float32, math.log(0.3), math.log(3.0)))
    col_scale = jnp.exp(jax.random.uniform(k_cols, (shape[-1],), jnp.float32, math.log(0.5), math.log(2.0)))
    return base * row_scale * col_scale


def draw_tokens(key, part):
    return scaled_field(jax.random.fold_in(key, 1), (TOKENS, D)).astype(jnp.bfloat16)


def draw_encodings(key, part):
    return scaled_field(jax.random.fold_in(key, 2), (ROWS, NLEN, EW)).astype(jnp.bfloat16)


def draw_w_query(key, part):
    base = jnp.clip(jax.random.normal(jax.random.fold_in(key, 3), (D, HEADS * HD), jnp.float32), -4.0, 4.0) / math.sqrt(D)
    return jnp.clip(base, -1.0, 1.0).astype(jnp.bfloat16)


def draw_w_key(key, part):
    base = jnp.clip(jax.random.normal(jax.random.fold_in(key, 5), (EW, HEADS * HD), jnp.float32), -4.0, 4.0) / math.sqrt(EW)
    return jnp.clip(base, -1.0, 1.0).astype(jnp.bfloat16)


def draw_neighbour_ids(key, part):
    k_shift, k_own, k_read = jax.random.split(jax.random.fold_in(key, 9), 3)
    spread = min(N_DP, REFS)
    shuffled = jax.random.permutation(k_shift, N_DP).astype(jnp.int32)
    places = jnp.arange(N_DP, dtype=jnp.int32)
    front = jnp.where(shuffled == 1, 0, jnp.where(shuffled == N_DP // 2, 1, jnp.where(shuffled == N_DP - 1, 2, 3 + places)))
    shuffled = shuffled[jnp.argsort(front).astype(jnp.int32)]
    shifts = shuffled[jnp.arange(REFS, dtype=jnp.int32) % spread]
    owners = jnp.arange(N_DP, dtype=jnp.int32)
    targets = (owners[:, None] + shifts[None, :]) % N_DP
    row_perm = jax.vmap(lambda subkey: jax.random.permutation(subkey, REFS))(jax.random.split(k_own, N_DP))
    targets = jnp.take_along_axis(targets, row_perm.astype(jnp.int32), axis=1)
    flat_targets = targets.reshape(N_DP * REFS)
    row_ids = jnp.arange(N_DP * REFS, dtype=jnp.int32)
    by_reader = jnp.argsort(flat_targets * (N_DP * REFS) + row_ids).astype(jnp.int32).reshape(N_DP, REFS)
    read_perm = jax.vmap(lambda subkey: jax.random.permutation(subkey, REFS))(jax.random.split(k_read, N_DP))
    chosen = jnp.take_along_axis(by_reader, read_perm.astype(jnp.int32), axis=1)
    return chosen.reshape(N_DP * BLOCKS_DEV, NEIGH)


def block_scale(own_key, extent, shards, low, high):
    factor_of = 1.0
    for position, shards_of in shards:
        steps = jax.random.uniform(jax.random.fold_in(jax.random.fold_in(own_key, 6), position), (shards_of,), jnp.float32, low / len(shards), high / len(shards))
        factor_of = factor_of * jnp.repeat(jnp.exp(steps), extent[position] // shards_of).reshape((-1,) + (1,) * (len(extent) - 1 - position))
    return factor_of


def normal_values(key, dims, deviation, limit, cuts=(), held_as=jnp.bfloat16):
    loudness = block_scale(key, dims, cuts, -0.22, 0.18) if cuts else 1.0
    entries = jax.random.normal(key, dims, jnp.float32) * deviation * loudness
    return jnp.minimum(jnp.maximum(entries, -limit), limit).astype(held_as)


def setup_inputs(seed: int = 0) -> dict:
    streams_of = jax.random.split(jax.random.key(seed), 12)
    return {
        "tokens": draw_tokens(jax.random.fold_in(streams_of[11], 71), 0),
        "cotangent": normal_values(streams_of[1], (TOKENS, D), 1.0, 6.0, ((0, 32), (1, 8))),
        "gain_dec": jnp.clip(1.0 + 0.18 * jax.random.normal(streams_of[2], (D,), jnp.float32), 0.1, 1.9),
        "w_query": draw_w_query(jax.random.fold_in(streams_of[11], 71), 0),
        "w_out": normal_values(streams_of[4], (HEADS * HD, D), (HEADS * HD // 32) ** -0.5, 0.5, ((0, 8),)),
        "encodings": draw_encodings(jax.random.fold_in(streams_of[11], 71), 0),
        "gain_enc": jnp.clip(1.0 + 0.18 * jax.random.normal(streams_of[6], (EW,), jnp.float32), 0.1, 1.9),
        "w_key": draw_w_key(jax.random.fold_in(streams_of[11], 71), 0),
        "w_value": normal_values(streams_of[8], (EW, HEADS * HD), EW ** -0.5, 0.1875, ((1, 8),)),
        "gain_post": jnp.clip(1.0 + 0.18 * jax.random.normal(streams_of[9], (D,), jnp.float32), 0.1, 1.9),
        "neighbour_ids": draw_neighbour_ids(jax.random.fold_in(streams_of[11], 71), 0),
    }


EPS = 1e-06

def rms_scale(values):
    return lax.rsqrt(lax.optimization_barrier(jnp.mean(values * values, axis=-1, keepdims=True)) + EPS)

def rounded(values):
    return lax.optimization_barrier(values.astype(jnp.bfloat16)).astype(jnp.float32)

def reference(tokens, cotangent, gain_dec, w_query, w_out, encodings, gain_enc, w_key, w_value, gain_post, neighbour_ids):
    head_cols = HEADS * HD
    group_cols = head_cols // N_MP
    lead_in = BLOCK - 1
    score_scale = HD ** (-0.5)
    enc_wide = encodings.astype(jnp.float32)
    row_scale = rms_scale(enc_wide)
    normed_enc = (enc_wide * row_scale * gain_enc).astype(jnp.bfloat16)
    key_weights = w_key.astype(jnp.float32)
    value_weights = w_value.astype(jnp.float32)
    out_groups = w_out.astype(jnp.float32).reshape(N_MP, group_cols, D)
    key_groups = key_weights.reshape(EW, N_MP, group_cols)
    value_groups = value_weights.reshape(EW, N_MP, group_cols)

    def one_sequence(seq):
        rows_in = lax.dynamic_slice_in_dim(tokens, seq * TOK_DEV, TOK_DEV, 0)
        rows_grad = lax.dynamic_slice_in_dim(cotangent, seq * TOK_DEV, TOK_DEV, 0)
        chosen = lax.dynamic_slice_in_dim(neighbour_ids, seq * BLOCKS_DEV, BLOCKS_DEV, 0).reshape(REFS)
        tok_wide = rows_in.astype(jnp.float32)
        normed = (tok_wide * rms_scale(tok_wide) * gain_dec).astype(jnp.bfloat16)
        queries = rounded(jnp.dot(normed, w_query, preferred_element_type=jnp.float32))
        memory = normed_enc[chosen].astype(jnp.float32)
        key_rows = rounded(jnp.einsum('ate,ej->atj', memory, key_weights))
        value_rows = rounded(jnp.einsum('ate,ej->atj', memory, value_weights))
        key_blocks = key_rows.reshape(BLOCKS_DEV, NEIGH * NLEN, HEADS, HD)
        value_blocks = value_rows.reshape(BLOCKS_DEV, NEIGH * NLEN, HEADS, HD)
        shifted = jnp.concatenate([queries[lead_in:], jnp.zeros((lead_in, head_cols), jnp.float32)], axis=0)
        shifted = shifted.reshape(BLOCKS_DEV, BLOCK, HEADS, HD)
        scores = jnp.einsum('cqhd,ckhd->chqk', shifted, key_blocks) * score_scale
        probability = jax.nn.softmax(scores, axis=-1)
        weights = rounded(probability)
        attended = rounded(jnp.einsum('chqk,ckhd->cqhd', weights, value_blocks)).reshape(TOK_DEV, head_cols)
        attended = jnp.concatenate([jnp.zeros((lead_in, head_cols), jnp.float32), attended[:TOK_DEV - lead_in]], axis=0)
        branch = rounded(jnp.einsum('tgj,gjd->tgd', attended.reshape(TOK_DEV, N_MP, group_cols), out_groups))
        mixed = (tok_wide + lax.optimization_barrier(jnp.sum(branch, axis=1))).astype(jnp.bfloat16)
        mixed_wide = mixed.astype(jnp.float32)
        ffn_input = (mixed_wide * rms_scale(mixed_wide) * gain_post).astype(jnp.bfloat16)
        d_attended = rounded(jnp.dot(rows_grad, w_out.T, preferred_element_type=jnp.float32))
        d_shifted = jnp.concatenate([d_attended[lead_in:], jnp.zeros((lead_in, head_cols), jnp.float32)], axis=0)
        d_shifted = d_shifted.reshape(BLOCKS_DEV, BLOCK, HEADS, HD)
        value_grad = rounded(jnp.einsum('chqk,cqhd->ckhd', weights, d_shifted))
        d_probability = jnp.einsum('cqhd,ckhd->chqk', d_shifted, value_blocks)
        d_scores = rounded(probability * (d_probability - lax.optimization_barrier(jnp.sum(probability * d_probability, axis=-1, keepdims=True))) * score_scale)
        key_grad = rounded(jnp.einsum('chqk,cqhd->ckhd', d_scores, shifted))
        key_parts = key_grad.reshape(REFS, NLEN, N_MP, group_cols)
        value_parts = value_grad.reshape(REFS, NLEN, N_MP, group_cols)
        terms = rounded(jnp.einsum('atgj,egj->atge', key_parts, key_groups) + jnp.einsum('atgj,egj->atge', value_parts, value_groups))
        return (mixed, ffn_input, lax.optimization_barrier(jnp.sum(terms, axis=2)), chosen)
    mixed, ffn_input, d_normed, chosen = lax.map(one_sequence, jnp.arange(N_DP, dtype=jnp.int32))
    mixed = mixed.reshape(TOKENS, D)
    ffn_input = ffn_input.reshape(TOKENS, D)
    grad_rows = jnp.zeros((ROWS, NLEN, EW), jnp.float32).at[chosen.reshape(ROWS)].add(d_normed.reshape(ROWS, NLEN, EW))
    enc_hat = enc_wide * row_scale
    upstream = gain_enc * grad_rows
    d_encodings = (row_scale * (upstream - enc_hat * lax.optimization_barrier(jnp.mean(upstream * enc_hat, axis=-1, keepdims=True)))).astype(jnp.bfloat16)
    return (mixed, ffn_input, d_encodings)
```

```python
import jax
import jax.numpy as jnp
from jax import lax
from jax.experimental import pallas as pl
from jax.experimental.pallas import tpu as pltpu
from jax.sharding import PartitionSpec as P

HD = 128
BLOCK = 64
NLEN = 128
NEIGH = 2

EPS = 1e-06
F32 = jnp.float32
BF16 = jnp.bfloat16
VMEM_LIMIT = 48 * 1024 * 1024


def rms_scale(values):
    return lax.rsqrt(jnp.mean(values * values, axis=-1, keepdims=True) + EPS)


def params():
    return pltpu.CompilerParams(vmem_limit_bytes=VMEM_LIMIT)


def vmem():
    return pl.BlockSpec(memory_space=pltpu.VMEM)


def hbm():
    return pl.BlockSpec(memory_space=pl.ANY)


def smem():
    return pl.BlockSpec(memory_space=pltpu.SMEM)


def chip_shift(count, k):
    return [(i, (i + 2 * k) % count) for i in range(count)]


def core_swap(count):
    return [(i, i ^ 1) for i in range(count)]


def gather_pieces(x, count):
    own = [x] + [lax.ppermute(x, "mp", chip_shift(count, k)) for k in range(1, count // 2)]
    return own + [lax.ppermute(p, "mp", core_swap(count)) for p in own]


def scatter_sum(send, keep, count):
    both = keep.astype(F32) + lax.ppermute(send, "mp", core_swap(count)).astype(F32)
    pair = both.astype(BF16)
    total = pair[0].astype(F32)
    for k in range(1, count // 2):
        total = total + lax.ppermute(pair[k], "mp", chip_shift(count, -k)).astype(F32)
    return total


def shift_matrix(n, lead, transpose):
    r = lax.broadcasted_iota(jnp.int32, (n, n), 0)
    c = lax.broadcasted_iota(jnp.int32, (n, n), 1)
    hit = (r == c + lead) if transpose else (c == r + lead)
    return jnp.where(hit, 1.0, 0.0).astype(BF16)


def dot(a, b):
    return lax.dot_general(a, b, (((1,), (0,)), ((), ())), preferred_element_type=F32)


def dot_nt(a, b):
    return lax.dot_general(a, b, (((1,), (1,)), ((), ())), preferred_element_type=F32)


def dot_tn(a, b):
    return lax.dot_general(a, b, (((0,), (0,)), ((), ())), preferred_element_type=F32)


def query_kernel(count, src, *refs):
    pieces = refs[:count]
    gain, w_hbm, out, w_buf, sems = refs[count:]
    share = pieces[0].shape[1]
    copies = []
    for k in range(count):
        start = pl.multiple_of(src[k] * share, share)
        cp = pltpu.make_async_copy(w_hbm.at[pl.ds(start, share), :], w_buf.at[k], sems.at[k])
        cp.start()
        copies.append(cp)
    squares = jnp.zeros((pieces[0].shape[0], 1), F32)
    for k in range(count):
        wide = pieces[k][...].astype(F32)
        squares = squares + jnp.sum(wide * wide, axis=1, keepdims=True)
    scale = lax.rsqrt(squares / (share * count) + EPS)
    acc = jnp.zeros(out.shape, F32)
    for k in range(count):
        g = gain[pl.ds(src[k], 1), :]
        normed = (pieces[k][...].astype(F32) * scale * g).astype(BF16)
        copies[k].wait()
        acc = acc + dot(normed, w_buf[k])
    out[...] = dot(shift_matrix(out.shape[0], BLOCK - 1, False), acc.astype(BF16)).astype(BF16)


def run_query(src, pieces, gain, w_query):
    count = len(pieces)
    rows, share = pieces[0].shape
    cols = w_query.shape[1]
    return pl.pallas_call(
        lambda *r: query_kernel(count, *r),
        out_shape=jax.ShapeDtypeStruct((rows, cols), BF16),
        in_specs=[smem()] + [vmem()] * count + [vmem(), hbm()],
        out_specs=vmem(),
        scratch_shapes=[pltpu.VMEM((count, share, cols), BF16), pltpu.SemaphoreType.DMA((count,))],
        compiler_params=params(),
        name="queries",
    )(src, *pieces, gain.reshape(count, share), w_query)


def back_kernel(count, src, *refs):
    pieces = refs[:count]
    w_hbm, out, w_buf, sems = refs[count:]
    share = pieces[0].shape[1]
    copies = []
    for k in range(count):
        start = pl.multiple_of(src[k] * share, share)
        cp = pltpu.make_async_copy(w_hbm.at[:, pl.ds(start, share)], w_buf.at[k], sems.at[k])
        cp.start()
        copies.append(cp)
    acc = jnp.zeros(out.shape, F32)
    for k in range(count):
        copies[k].wait()
        acc = acc + dot_nt(pieces[k][...], w_buf[k])
    out[...] = dot(shift_matrix(out.shape[0], BLOCK - 1, False), acc.astype(BF16)).astype(BF16)


def run_back(src, pieces, w_out):
    count = len(pieces)
    rows, share = pieces[0].shape
    cols = w_out.shape[0]
    return pl.pallas_call(
        lambda *r: back_kernel(count, *r),
        out_shape=jax.ShapeDtypeStruct((rows, cols), BF16),
        in_specs=[smem()] + [vmem()] * count + [hbm()],
        out_specs=vmem(),
        scratch_shapes=[pltpu.VMEM((count, cols, share), BF16), pltpu.SemaphoreType.DMA((count,))],
        compiler_params=params(),
        name="d_attended",
    )(src, *pieces, w_out)


def branch_kernel(count, src, att, w_hbm, send, keep, w_buf, sems):
    share = send.shape[2]
    half = count // 2
    copies = []
    order = list(range(half, count)) + list(range(half))
    for k in order:
        start = pl.multiple_of(src[k] * share, share)
        cp = pltpu.make_async_copy(w_hbm.at[:, pl.ds(start, share)], w_buf.at[k], sems.at[k])
        cp.start()
        copies.append(cp)
    a = att[...]
    for k, cp in zip(order, copies):
        cp.wait()
        part = dot(a, w_buf[k]).astype(BF16)
        if k < half:
            keep[k] = part
        else:
            send[k - half] = part


def run_branch(src, att, w_out, count):
    rows, cols = att.shape
    share = w_out.shape[1] // count
    shape = jax.ShapeDtypeStruct((count // 2, rows, share), BF16)
    return pl.pallas_call(
        lambda *r: branch_kernel(count, *r),
        out_shape=(shape, shape),
        in_specs=[smem(), vmem(), hbm()],
        out_specs=(vmem(), vmem()),
        scratch_shapes=[pltpu.VMEM((count, cols, share), BF16), pltpu.SemaphoreType.DMA((count,))],
        compiler_params=params(),
        name="branches",
    )(src, att, w_out)


def attention_kernel(count, blocks, *refs):
    pieces = refs[:count]
    q_ref, d_ref, wk, wv, send, keep, att_out, mem, keys, values, k_grad, v_grad, att = refs[count:]
    heads = q_ref.shape[1] // HD
    part = pieces[0].shape[0] // blocks
    span = part * count
    half = count // 2
    scale = HD ** (-0.5)
    for b in range(blocks):
        for k in range(count):
            mem[b * span + k * part : b * span + (k + 1) * part, :] = pieces[k][
                b * part : (b + 1) * part, :
            ]
    keys[...] = dot(mem[...], wk[...]).astype(BF16)
    values[...] = dot(mem[...], wv[...]).astype(BF16)
    for b in range(blocks):
        rows = slice(b * BLOCK, (b + 1) * BLOCK)
        ctx = slice(b * span, (b + 1) * span)
        for h in range(heads):
            cols = slice(h * HD, (h + 1) * HD)
            q = q_ref[rows, cols]
            d = d_ref[rows, cols]
            kk = keys[ctx, cols]
            vv = values[ctx, cols]
            scores = dot_nt(q, kk) * scale
            lifted = jnp.exp(scores - jnp.max(scores, axis=-1, keepdims=True))
            prob = lifted / jnp.sum(lifted, axis=-1, keepdims=True)
            weights = prob.astype(BF16)
            att[rows, cols] = dot(weights, vv).astype(BF16)
            d_prob = dot_nt(d, vv)
            d_scores = (
                prob * (d_prob - jnp.sum(prob * d_prob, axis=-1, keepdims=True)) * scale
            ).astype(BF16)
            v_grad[ctx, cols] = dot_tn(weights, d).astype(BF16)
            k_grad[ctx, cols] = dot_tn(d_scores, q).astype(BF16)
    att_out[...] = dot(shift_matrix(att.shape[0], BLOCK - 1, True), att[...]).astype(BF16)
    for b in range(blocks):
        ctx = slice(b * span, (b + 1) * span)
        terms = (dot_nt(k_grad[ctx, :], wk[...]) + dot_nt(v_grad[ctx, :], wv[...])).astype(BF16)
        for k in range(count):
            rows = terms[k * part : (k + 1) * part, :]
            if k < half:
                keep[k, b * part : (b + 1) * part, :] = rows
            else:
                send[k - half, b * part : (b + 1) * part, :] = rows


def run_attention(pieces, q, d, w_key, w_value, blocks):
    count = len(pieces)
    rows, width = pieces[0].shape
    cols = q.shape[1]
    shape = jax.ShapeDtypeStruct((count // 2, rows, width), BF16)
    total = rows * count
    return pl.pallas_call(
        lambda *r: attention_kernel(count, blocks, *r),
        out_shape=(shape, shape, jax.ShapeDtypeStruct(q.shape, BF16)),
        in_specs=[vmem()] * (count + 4),
        out_specs=(vmem(), vmem(), vmem()),
        scratch_shapes=[pltpu.VMEM((total, width), BF16)]
        + [pltpu.VMEM((total, cols), BF16)] * 4
        + [pltpu.VMEM(q.shape, BF16)],
        compiler_params=params(),
        name="attention",
    )(*pieces, q, d, w_key, w_value)


def outgoing_kernel(req, enc, gain, out, normed):
    wide = enc[...].astype(F32)
    normed[...] = (wide * rms_scale(wide) * gain[...]).astype(BF16)
    for s in range(out.shape[0]):
        out[s] = normed[jnp.maximum(req[s], 0)]


def run_outgoing(requested, encodings, gain):
    slots = requested.shape[0]
    return pl.pallas_call(
        outgoing_kernel,
        out_shape=jax.ShapeDtypeStruct((slots,) + encodings.shape[1:], BF16),
        in_specs=[smem(), vmem(), vmem()],
        out_specs=vmem(),
        scratch_shapes=[pltpu.VMEM(encodings.shape, BF16)],
        compiler_params=params(),
        name="outgoing_rows",
    )(requested, encodings, gain.reshape(1, 1, -1))


def pick_kernel(owner, rows, out, sems):
    copies = []
    for a in range(out.shape[0]):
        cp = pltpu.make_async_copy(rows.at[owner[a]], out.at[a], sems.at[a])
        cp.start()
        copies.append(cp)
    for cp in copies:
        cp.wait()


def run_pick(owner, rows):
    n = owner.shape[0]
    return pl.pallas_call(
        pick_kernel,
        out_shape=jax.ShapeDtypeStruct((n,) + rows.shape[1:], rows.dtype),
        in_specs=[smem(), hbm()],
        out_specs=vmem(),
        scratch_shapes=[pltpu.SemaphoreType.DMA((n,))],
        compiler_params=params(),
        name="picked_rows",
    )(owner, rows)


def place_kernel(reading, own, r1, r2, r3, out, total):
    total[...] = (
        own[...].astype(F32) + r1[...].astype(F32) + r2[...].astype(F32) + r3[...].astype(F32)
    ).astype(BF16)
    for s in range(out.shape[0]):
        out[s] = total[reading[s]]


def run_place(reading, parts):
    slots = reading.shape[0]
    shape = parts[0].shape
    return pl.pallas_call(
        place_kernel,
        out_shape=jax.ShapeDtypeStruct((slots,) + shape[1:], BF16),
        in_specs=[smem()] + [vmem()] * 4,
        out_specs=vmem(),
        scratch_shapes=[pltpu.VMEM(shape, BF16)],
        compiler_params=params(),
        name="placed_grads",
    )(reading, *parts)


def finish_kernel(slot, back, enc, gain, out, buf, sems):
    copies = []
    for j in range(out.shape[0]):
        cp = pltpu.make_async_copy(back.at[slot[j]], buf.at[j], sems.at[j])
        cp.start()
        copies.append(cp)
    wide = enc[...].astype(F32)
    scale = rms_scale(wide)
    hat = wide * scale
    for cp in copies:
        cp.wait()
    up = gain[...] * buf[...].astype(F32)
    out[...] = (scale * (up - hat * jnp.mean(up * hat, axis=-1, keepdims=True))).astype(BF16)


def run_finish(slot, back, encodings, gain):
    rows = encodings.shape[0]
    return pl.pallas_call(
        finish_kernel,
        out_shape=jax.ShapeDtypeStruct(encodings.shape, BF16),
        in_specs=[smem(), hbm(), vmem(), vmem()],
        out_specs=vmem(),
        scratch_shapes=[pltpu.VMEM(encodings.shape, BF16), pltpu.SemaphoreType.DMA((rows,))],
        compiler_params=params(),
        name="d_encodings",
    )(slot, back, encodings, gain.reshape(1, 1, -1))


def shards(
    tokens,
    cotangent,
    gain_dec,
    w_query,
    w_out,
    encodings,
    gain_enc,
    w_key,
    w_value,
    gain_post,
    neighbour_ids,
):
    dp_count = lax.axis_size("dp")
    count = lax.axis_size("mp")
    half = count // 2
    share_cols = tokens.shape[1]
    own_rows, own_tokens, width = encodings.shape
    blocks = neighbour_ids.shape[0]
    readings = blocks * neighbour_ids.shape[1]
    here = lax.axis_index("mp")
    steps = jnp.arange(half, dtype=jnp.int32)
    same = (here - 2 * steps) % count
    src = jnp.concatenate([same, same ^ 1]).astype(jnp.int32)

    chosen = neighbour_ids.reshape(readings)
    owner = chosen // own_rows
    local_row = chosen % own_rows
    slots = jnp.arange(dp_count, dtype=jnp.int32)
    matches = owner[:, None] == slots[None, :]
    wanted = jnp.sum(jnp.where(matches, local_row[:, None] + 1, 0), axis=0) - 1
    reading = jnp.sum(
        jnp.where(matches, jnp.arange(readings, dtype=jnp.int32)[:, None], 0), axis=0
    )
    requested = lax.all_to_all(
        wanted.reshape(dp_count, 1), "dp", split_axis=0, concat_axis=0, tiled=True
    ).reshape(dp_count)
    serves = requested[:, None] == jnp.arange(own_rows, dtype=jnp.int32)[None, :]
    slot = jnp.sum(jnp.where(serves, slots[:, None], 0), axis=0)

    tok_pieces = gather_pieces(tokens, count)
    cot_pieces = gather_pieces(cotangent, count)
    outgoing = run_outgoing(requested, encodings, gain_enc)
    incoming = lax.all_to_all(outgoing, "dp", split_axis=0, concat_axis=0, tiled=True)
    picked = run_pick(owner, incoming)
    row_pieces = gather_pieces(picked.reshape(readings * own_tokens, width), count)
    q = run_query(src, tok_pieces, gain_dec, w_query)
    d = run_back(src, cot_pieces, w_out)
    send, keep, attended = run_attention(row_pieces, q, d, w_key, w_value, blocks)

    swapped = lax.ppermute(send, "mp", core_swap(count))
    pair = (keep.astype(F32) + swapped.astype(F32)).astype(BF16)
    parts = [pair[0]] + [
        lax.ppermute(pair[k], "mp", chip_shift(count, -k)) for k in range(1, half)
    ]
    back_out = run_place(
        reading, [p.reshape(readings, own_tokens, width) for p in parts]
    )
    back_in = lax.all_to_all(back_out, "dp", split_axis=0, concat_axis=0, tiled=True)

    b_send, b_keep = run_branch(src, attended, w_out, count)
    summed = scatter_sum(b_send, b_keep, count)
    mixed = (tokens.astype(F32) + summed).astype(BF16)
    mixed_wide = mixed.astype(F32)
    squares = jnp.sum(mixed_wide * mixed_wide, axis=1)
    squares = squares + lax.ppermute(squares, "mp", core_swap(count))
    total = squares
    for k in range(1, half):
        total = total + lax.ppermute(squares, "mp", chip_shift(count, k))
    post = lax.rsqrt(total / (share_cols * count) + EPS)[:, None]
    gain_here = lax.dynamic_slice_in_dim(gain_post, here * share_cols, share_cols, 0)
    ffn = (mixed_wide * post * gain_here).astype(BF16)

    d_encodings = run_finish(slot, back_in, encodings, gain_enc)
    return (mixed, ffn, d_encodings)


def solution(mesh):
    in_specs = (
        P("dp", "mp"),
        P("dp", "mp"),
        P(),
        P(None, "mp"),
        P("mp", None),
        P("dp", "mp", None),
        P(),
        P(None, "mp"),
        P(None, "mp"),
        P(),
        P("dp", None),
    )
    out_specs = (P("dp", "mp"), P("dp", "mp"), P("dp", "mp", None))
    return jax.shard_map(shards, mesh=mesh, in_specs=in_specs, out_specs=out_specs, check_vma=False)
```

```python
import jax
import jax.numpy as jnp
from jax import lax
from jax.experimental import pallas as pl
from jax.experimental.pallas import tpu as pltpu
from jax.sharding import PartitionSpec as P

HD = 128
BLOCK = 64
NLEN = 128
NEIGH = 2

EPS = 1e-06
F32 = jnp.float32
BF16 = jnp.bfloat16
VMEM_LIMIT = 48 * 1024 * 1024


def rms_scale(values):
    return lax.rsqrt(jnp.mean(values * values, axis=-1, keepdims=True) + EPS)


def params():
    return pltpu.CompilerParams(vmem_limit_bytes=VMEM_LIMIT)


def cost(micros):
    return pl.CostEstimate(flops=int(micros * 1.1e9), bytes_accessed=0, transcendentals=0)


def vmem():
    return pl.BlockSpec(memory_space=pltpu.VMEM)


def hbm():
    return pl.BlockSpec(memory_space=pl.ANY)


def smem():
    return pl.BlockSpec(memory_space=pltpu.SMEM)


def chip_shift(count, k):
    return [(i, (i + 2 * k) % count) for i in range(count)]


def core_swap(count):
    return [(i, i ^ 1) for i in range(count)]


def over_chips(x, count):
    return [x] + [lax.ppermute(x, "mp", chip_shift(count, k)) for k in range(1, count // 2)]


def with_other_core(own, count):
    return own + [lax.ppermute(p, "mp", core_swap(count)) for p in own]


def pair_sum(send, keep, count):
    return [
        (mine.astype(F32) + lax.ppermute(s, "mp", core_swap(count)).astype(F32)).astype(BF16)
        for s, mine in zip(send, keep)
    ]


def pair_shares(pair, count):
    return [pair[0]] + [
        lax.ppermute(pair[k], "mp", chip_shift(count, -k)) for k in range(1, count // 2)
    ]


def shift_matrix(n, lead, transpose):
    r = lax.broadcasted_iota(jnp.int32, (n, n), 0)
    c = lax.broadcasted_iota(jnp.int32, (n, n), 1)
    hit = (r == c + lead) if transpose else (c == r + lead)
    return jnp.where(hit, 1.0, 0.0).astype(BF16)


def dot(a, b):
    return lax.dot_general(a, b, (((1,), (0,)), ((), ())), preferred_element_type=F32)


def dot_nt(a, b):
    return lax.dot_general(a, b, (((1,), (1,)), ((), ())), preferred_element_type=F32)


def dot_tn(a, b):
    return lax.dot_general(a, b, (((0,), (0,)), ((), ())), preferred_element_type=F32)


def query_kernel(count, src, *refs):
    pieces = refs[:count]
    gain, w_hbm, out, w_buf, sems = refs[count:]
    share = pieces[0].shape[1]
    copies = []
    for k in range(count):
        start = pl.multiple_of(src[k] * share, share)
        cp = pltpu.make_async_copy(w_hbm.at[pl.ds(start, share), :], w_buf.at[k], sems.at[k])
        cp.start()
        copies.append(cp)
    squares = jnp.zeros((pieces[0].shape[0], 1), F32)
    for k in range(count):
        wide = pieces[k][...].astype(F32)
        squares = squares + jnp.sum(wide * wide, axis=1, keepdims=True)
    scale = lax.rsqrt(squares / (share * count) + EPS)
    acc = jnp.zeros(out.shape, F32)
    for k in range(count):
        g = gain[pl.ds(src[k], 1), :]
        normed = (pieces[k][...].astype(F32) * scale * g).astype(BF16)
        copies[k].wait()
        acc = acc + dot(normed, w_buf[k])
    out[...] = dot(shift_matrix(out.shape[0], BLOCK - 1, False), acc.astype(BF16)).astype(BF16)


def run_query(src, pieces, gain, w_query):
    count = len(pieces)
    rows, share = pieces[0].shape
    cols = w_query.shape[1]
    return pl.pallas_call(
        lambda *r: query_kernel(count, *r),
        out_shape=jax.ShapeDtypeStruct((rows, cols), BF16),
        in_specs=[smem()] + [vmem()] * count + [vmem(), hbm()],
        out_specs=vmem(),
        scratch_shapes=[pltpu.VMEM((count, share, cols), BF16), pltpu.SemaphoreType.DMA((count,))],
        compiler_params=params(),
        cost_estimate=cost(4.5),
        name="queries",
    )(src, *pieces, gain.reshape(count, share), w_query)


def back_kernel(count, src, *refs):
    pieces = refs[:count]
    w_hbm, out, w_buf, sems = refs[count:]
    share = pieces[0].shape[1]
    copies = []
    for k in range(count):
        start = pl.multiple_of(src[k] * share, share)
        cp = pltpu.make_async_copy(w_hbm.at[:, pl.ds(start, share)], w_buf.at[k], sems.at[k])
        cp.start()
        copies.append(cp)
    acc = jnp.zeros(out.shape, F32)
    for k in range(count):
        copies[k].wait()
        acc = acc + dot_nt(pieces[k][...], w_buf[k])
    out[...] = dot(shift_matrix(out.shape[0], BLOCK - 1, False), acc.astype(BF16)).astype(BF16)


def run_back(src, pieces, w_out):
    count = len(pieces)
    rows, share = pieces[0].shape
    cols = w_out.shape[0]
    return pl.pallas_call(
        lambda *r: back_kernel(count, *r),
        out_shape=jax.ShapeDtypeStruct((rows, cols), BF16),
        in_specs=[smem()] + [vmem()] * count + [hbm()],
        out_specs=vmem(),
        scratch_shapes=[pltpu.VMEM((count, cols, share), BF16), pltpu.SemaphoreType.DMA((count,))],
        compiler_params=params(),
        cost_estimate=cost(4.5),
        name="d_attended",
    )(src, *pieces, w_out)


def branch_kernel(count, src, att_a, att_b, w_hbm, *refs):
    outs, w_buf, sems = refs[:count], refs[count], refs[count + 1]
    share = outs[0].shape[1]
    half = count // 2
    copies = []
    order = list(range(half, count)) + list(range(half))
    for k in order:
        start = pl.multiple_of(src[k] * share, share)
        cp = pltpu.make_async_copy(w_hbm.at[:, pl.ds(start, share)], w_buf.at[k], sems.at[k])
        cp.start()
        copies.append(cp)
    shifted = jnp.concatenate([att_a[...], att_b[...]], axis=0)
    a = dot(shift_matrix(shifted.shape[0], BLOCK - 1, True), shifted).astype(BF16)
    for k, cp in zip(order, copies):
        cp.wait()
        outs[k][...] = dot(a, w_buf[k]).astype(BF16)


def run_branch(src, att_a, att_b, w_out, count):
    rows, cols = 2 * att_a.shape[0], att_a.shape[1]
    share = w_out.shape[1] // count
    outs = pl.pallas_call(
        lambda *r: branch_kernel(count, *r),
        out_shape=[jax.ShapeDtypeStruct((rows, share), BF16)] * count,
        in_specs=[smem(), vmem(), vmem(), hbm()],
        out_specs=[vmem()] * count,
        scratch_shapes=[pltpu.VMEM((count, cols, share), BF16), pltpu.SemaphoreType.DMA((count,))],
        compiler_params=params(),
        cost_estimate=cost(4),
        name="branches",
    )(src, att_a, att_b, w_out)
    return outs[count // 2 :], outs[: count // 2]


def attention_kernel(count, blocks, *refs):
    pieces = refs[:count]
    q_ref, d_ref, wk, wv = refs[count : count + 4]
    terms_out = refs[count + 4 : 2 * count + 4]
    att, mem, keys, values, k_grad, v_grad = refs[2 * count + 4 :]
    heads = q_ref.shape[1] // HD
    part = pieces[0].shape[0] // blocks
    span = part * count
    scale = HD ** (-0.5)
    for b in range(blocks):
        for k in range(count):
            mem[b * span + k * part : b * span + (k + 1) * part, :] = pieces[k][
                b * part : (b + 1) * part, :
            ]
    keys[...] = dot(mem[...], wk[...]).astype(BF16)
    values[...] = dot(mem[...], wv[...]).astype(BF16)
    for b in range(blocks):
        rows = slice(b * BLOCK, (b + 1) * BLOCK)
        ctx = slice(b * span, (b + 1) * span)
        for h in range(heads):
            cols = slice(h * HD, (h + 1) * HD)
            q = q_ref[rows, cols]
            d = d_ref[rows, cols]
            kk = keys[ctx, cols]
            vv = values[ctx, cols]
            scores = dot_nt(q, kk) * scale
            lifted = jnp.exp(scores - jnp.max(scores, axis=-1, keepdims=True))
            prob = lifted / jnp.sum(lifted, axis=-1, keepdims=True)
            weights = prob.astype(BF16)
            att[rows, cols] = dot(weights, vv).astype(BF16)
            d_prob = dot_nt(d, vv)
            d_scores = (
                prob * (d_prob - jnp.sum(prob * d_prob, axis=-1, keepdims=True)) * scale
            ).astype(BF16)
            v_grad[ctx, cols] = dot_tn(weights, d).astype(BF16)
            k_grad[ctx, cols] = dot_tn(d_scores, q).astype(BF16)
    for b in range(blocks):
        ctx = slice(b * span, (b + 1) * span)
        terms = (dot_nt(k_grad[ctx, :], wk[...]) + dot_nt(v_grad[ctx, :], wv[...])).astype(BF16)
        for k in range(count):
            terms_out[k][b * part : (b + 1) * part, :] = terms[k * part : (k + 1) * part, :]


def run_attention(pieces, q, d, w_key, w_value, blocks):
    count = len(pieces)
    rows, width = pieces[0].shape
    cols = q.shape[1]
    total = rows * count
    outs = pl.pallas_call(
        lambda *r: attention_kernel(count, blocks, *r),
        out_shape=[jax.ShapeDtypeStruct((rows, width), BF16)] * count
        + [jax.ShapeDtypeStruct(q.shape, BF16)],
        in_specs=[vmem()] * (count + 4),
        out_specs=[vmem()] * (count + 1),
        scratch_shapes=[pltpu.VMEM((total, width), BF16)]
        + [pltpu.VMEM((total, cols), BF16)] * 4,
        compiler_params=params(),
        cost_estimate=cost(7),
        name="attention",
    )(*pieces, q, d, w_key, w_value)
    return outs[count // 2 : count], outs[: count // 2], outs[count]


def outgoing_kernel(req, enc, gain, out, normed):
    wide = enc[...].astype(F32)
    normed[...] = (wide * rms_scale(wide) * gain[...]).astype(BF16)
    for s in range(out.shape[0]):
        out[s] = normed[jnp.maximum(req[s], 0)]


def run_outgoing(requested, encodings, gain):
    slots = requested.shape[0]
    return pl.pallas_call(
        outgoing_kernel,
        out_shape=jax.ShapeDtypeStruct((slots,) + encodings.shape[1:], BF16),
        in_specs=[smem(), vmem(), vmem()],
        out_specs=vmem(),
        scratch_shapes=[pltpu.VMEM(encodings.shape, BF16)],
        compiler_params=params(),
        cost_estimate=cost(1.7),
        name="outgoing_rows",
    )(requested, encodings, gain.reshape(1, 1, -1))


def pick_kernel(owner, rows, out, sems):
    copies = []
    for a in range(out.shape[0]):
        cp = pltpu.make_async_copy(rows.at[owner[a]], out.at[a], sems.at[a])
        cp.start()
        copies.append(cp)
    for cp in copies:
        cp.wait()


def run_pick(owner, rows):
    n = owner.shape[0]
    return pl.pallas_call(
        pick_kernel,
        out_shape=jax.ShapeDtypeStruct((n,) + rows.shape[1:], rows.dtype),
        in_specs=[smem(), hbm()],
        out_specs=vmem(),
        scratch_shapes=[pltpu.SemaphoreType.DMA((n,))],
        compiler_params=params(),
        cost_estimate=cost(1),
        name="picked_rows",
    )(owner, rows)


def place_kernel(reading, *refs):
    parts, out, total = refs[:-2], refs[-2], refs[-1]
    half = len(parts) // 2
    rows = parts[0].shape[0]
    for i in range(2):
        group = [p[...].astype(F32) for p in parts[i * half : (i + 1) * half]]
        total[i * rows : (i + 1) * rows] = sum(group).astype(BF16)
    for s in range(out.shape[0]):
        out[s] = total[reading[s]]


def run_place(reading, parts):
    slots = reading.shape[0]
    rows, *rest = parts[0].shape
    return pl.pallas_call(
        place_kernel,
        out_shape=jax.ShapeDtypeStruct((slots, *rest), BF16),
        in_specs=[smem()] + [vmem()] * len(parts),
        out_specs=vmem(),
        scratch_shapes=[pltpu.VMEM((2 * rows, *rest), BF16)],
        compiler_params=params(),
        cost_estimate=cost(1.7),
        name="placed_grads",
    )(reading, *parts)


def finish_kernel(slot, back, enc, gain, out, buf, sems):
    copies = []
    for j in range(out.shape[0]):
        cp = pltpu.make_async_copy(back.at[slot[j]], buf.at[j], sems.at[j])
        cp.start()
        copies.append(cp)
    wide = enc[...].astype(F32)
    scale = rms_scale(wide)
    hat = wide * scale
    for cp in copies:
        cp.wait()
    up = gain[...] * buf[...].astype(F32)
    out[...] = (scale * (up - hat * jnp.mean(up * hat, axis=-1, keepdims=True))).astype(BF16)


def run_finish(slot, back, encodings, gain):
    rows = encodings.shape[0]
    return pl.pallas_call(
        finish_kernel,
        out_shape=jax.ShapeDtypeStruct(encodings.shape, BF16),
        in_specs=[smem(), hbm(), vmem(), vmem()],
        out_specs=vmem(),
        scratch_shapes=[pltpu.VMEM(encodings.shape, BF16), pltpu.SemaphoreType.DMA((rows,))],
        compiler_params=params(),
        cost_estimate=cost(1.9),
        name="d_encodings",
    )(slot, back, encodings, gain.reshape(1, 1, -1))


def shards(
    tokens,
    cotangent,
    gain_dec,
    w_query,
    w_out,
    encodings,
    gain_enc,
    w_key,
    w_value,
    gain_post,
    neighbour_ids,
):
    dp_count = lax.axis_size("dp")
    count = lax.axis_size("mp")
    half = count // 2
    share_cols = tokens.shape[1]
    own_rows, own_tokens, width = encodings.shape
    blocks = neighbour_ids.shape[0]
    readings = blocks * neighbour_ids.shape[1]
    here = lax.axis_index("mp")
    steps = jnp.arange(half, dtype=jnp.int32)
    same = (here - 2 * steps) % count
    src = jnp.concatenate([same, same ^ 1]).astype(jnp.int32)

    chosen = neighbour_ids.reshape(readings)
    owner = chosen // own_rows
    local_row = chosen % own_rows
    slots = jnp.arange(dp_count, dtype=jnp.int32)
    matches = owner[:, None] == slots[None, :]
    wanted = jnp.sum(jnp.where(matches, local_row[:, None] + 1, 0), axis=0) - 1
    reading = jnp.sum(
        jnp.where(matches, jnp.arange(readings, dtype=jnp.int32)[:, None], 0), axis=0
    )
    requested = lax.all_to_all(
        wanted.reshape(dp_count, 1), "dp", split_axis=0, concat_axis=0, tiled=True
    ).reshape(dp_count)
    serves = requested[:, None] == jnp.arange(own_rows, dtype=jnp.int32)[None, :]
    slot = jnp.sum(jnp.where(serves, slots[:, None], 0), axis=0)

    tok_own = over_chips(tokens, count)
    cot_pieces = with_other_core(over_chips(cotangent, count), count)
    enc_in, tok_own = lax.optimization_barrier((encodings, tok_own))
    tok_pieces = with_other_core(tok_own, count)
    outgoing = run_outgoing(requested, enc_in, gain_enc)
    incoming = lax.all_to_all(outgoing, "dp", split_axis=0, concat_axis=0, tiled=True)
    q = run_query(src, tok_pieces, gain_dec, w_query)
    d = run_back(src, cot_pieces, w_out)
    split = (blocks // 2) * BLOCK
    picked = run_pick(owner, incoming).reshape(2, readings // 2 * own_tokens, width)
    own_a = over_chips(picked[0], count)
    own_b = over_chips(picked[1], count)
    own_a, q, d = lax.optimization_barrier((own_a, q, d))
    send_a, keep_a, att_a = run_attention(
        with_other_core(own_a, count), q[:split], d[:split], w_key, w_value, blocks // 2
    )
    own_b, att_a = lax.optimization_barrier((own_b, att_a))
    row_b = with_other_core(own_b, count)
    pair_a = pair_sum(send_a, keep_a, count)
    row_b, pair_a = lax.optimization_barrier((row_b, pair_a))
    parts_a = pair_shares(pair_a, count)
    send_b, keep_b, att_b = run_attention(
        row_b, q[split:], d[split:], w_key, w_value, blocks // 2
    )
    send_b, parts_a = lax.optimization_barrier((send_b, parts_a))
    pair_b = pair_sum(send_b, keep_b, count)
    att_b, pair_b = lax.optimization_barrier((att_b, pair_b))
    parts_b = pair_shares(pair_b, count)
    b_send, b_keep = run_branch(src, att_a, att_b, w_out, count)
    b_send, parts_b = lax.optimization_barrier((b_send, parts_b))
    b_pair = pair_sum(b_send, b_keep, count)
    b_parts = pair_shares(b_pair, count)
    back_out = run_place(
        reading,
        [p.reshape(readings // 2, own_tokens, width) for p in parts_a + parts_b],
    )
    back_in = lax.all_to_all(back_out, "dp", split_axis=0, concat_axis=0, tiled=True)

    summed = sum(p.astype(F32) for p in b_parts)
    mixed = (tokens.astype(F32) + summed).astype(BF16)
    mixed_wide = mixed.astype(F32)
    squares = jnp.sum(mixed_wide * mixed_wide, axis=1)
    squares = squares + lax.ppermute(squares, "mp", core_swap(count))
    total = squares
    for k in range(1, half):
        total = total + lax.ppermute(squares, "mp", chip_shift(count, k))
    post = lax.rsqrt(total / (share_cols * count) + EPS)[:, None]
    gain_here = lax.dynamic_slice_in_dim(gain_post, here * share_cols, share_cols, 0)
    ffn = (mixed_wide * post * gain_here).astype(BF16)

    d_encodings = run_finish(slot, back_in, encodings, gain_enc)
    return (mixed, ffn, d_encodings)


def solution(mesh):
    in_specs = (
        P("dp", "mp"),
        P("dp", "mp"),
        P(),
        P(None, "mp"),
        P("mp", None),
        P("dp", "mp", None),
        P(),
        P(None, "mp"),
        P(None, "mp"),
        P(),
        P("dp", None),
    )
    out_specs = (P("dp", "mp"), P("dp", "mp"), P("dp", "mp", None))
    return jax.shard_map(shards, mesh=mesh, in_specs=in_specs, out_specs=out_specs, check_vma=False)
```

```python
import jax
import jax.numpy as jnp
from jax import lax
from jax.experimental import pallas as pl
from jax.experimental.pallas import tpu as pltpu
from jax.sharding import PartitionSpec as P

HD = 128
BLOCK = 64
NLEN = 128
NEIGH = 2

EPS = 1e-06
F32 = jnp.float32
BF16 = jnp.bfloat16
IDS_WIDTH = 128
VMEM_LIMIT = 48 * 1024 * 1024


def rms_scale(values):
    return lax.rsqrt(jnp.mean(values * values, axis=-1, keepdims=True) + EPS)


def params():
    return pltpu.CompilerParams(vmem_limit_bytes=VMEM_LIMIT)


def cost(micros):
    return pl.CostEstimate(flops=int(micros * 1.1e9), bytes_accessed=0, transcendentals=0)


def vmem():
    return pl.BlockSpec(memory_space=pltpu.VMEM)


def hbm():
    return pl.BlockSpec(memory_space=pl.ANY)


def smem():
    return pl.BlockSpec(memory_space=pltpu.SMEM)


def chip_shift(count, k):
    return [(i, (i + 2 * k) % count) for i in range(count)]


def core_swap(count):
    return [(i, i ^ 1) for i in range(count)]


def over_chips(x, count):
    return [x] + [lax.ppermute(x, "mp", chip_shift(count, k)) for k in range(1, count // 2)]


def swap(x, count):
    return lax.ppermute(x, "mp", core_swap(count))


def pair_sum(send, keep, count):
    return (keep.astype(F32) + swap(send, count).astype(F32)).astype(BF16)


def pair_shares(pair, count):
    return [pair[0]] + [
        lax.ppermute(pair[k], "mp", chip_shift(count, -k)) for k in range(1, count // 2)
    ]


def shift_matrix(n, lead, transpose):
    r = lax.broadcasted_iota(jnp.int32, (n, n), 0)
    c = lax.broadcasted_iota(jnp.int32, (n, n), 1)
    hit = (r == c + lead) if transpose else (c == r + lead)
    return jnp.where(hit, 1.0, 0.0).astype(BF16)


def dot(a, b):
    return lax.dot_general(a, b, (((1,), (0,)), ((), ())), preferred_element_type=F32)


def dot_nt(a, b):
    return lax.dot_general(a, b, (((1,), (1,)), ((), ())), preferred_element_type=F32)


def dot_tn(a, b):
    return lax.dot_general(a, b, (((0,), (0,)), ((), ())), preferred_element_type=F32)


def views(count, refs):
    half = count // 2
    return list(refs[:half]) + [refs[half].at[k] for k in range(half)], refs[half + 1 :]


def query_kernel(count, src, *refs):
    pieces, rest = views(count, refs)
    gain, w_hbm, out, w_buf, sems = rest
    share = pieces[0].shape[1]
    copies = []
    for k in range(count):
        start = pl.multiple_of(src[k] * share, share)
        cp = pltpu.make_async_copy(w_hbm.at[pl.ds(start, share), :], w_buf.at[k], sems.at[k])
        cp.start()
        copies.append(cp)
    squares = jnp.zeros((pieces[0].shape[0], 1), F32)
    for k in range(count):
        wide = pieces[k][...].astype(F32)
        squares = squares + jnp.sum(wide * wide, axis=1, keepdims=True)
    scale = lax.rsqrt(squares / (share * count) + EPS)
    acc = jnp.zeros(out.shape, F32)
    for k in range(count):
        g = gain[pl.ds(src[k], 1), :]
        normed = (pieces[k][...].astype(F32) * scale * g).astype(BF16)
        copies[k].wait()
        acc = acc + dot(normed, w_buf[k])
    out[...] = dot(shift_matrix(out.shape[0], BLOCK - 1, False), acc.astype(BF16)).astype(BF16)


def run_query(src, pieces, gain, w_query):
    count = 2 * (len(pieces) - 1)
    rows, share = pieces[0].shape
    cols = w_query.shape[1]
    return pl.pallas_call(
        lambda *r: query_kernel(count, *r),
        out_shape=jax.ShapeDtypeStruct((rows, cols), BF16),
        in_specs=[smem()] + [vmem()] * (len(pieces) + 1) + [hbm()],
        out_specs=vmem(),
        scratch_shapes=[pltpu.VMEM((count, share, cols), BF16), pltpu.SemaphoreType.DMA((count,))],
        compiler_params=params(),
        cost_estimate=cost(4.5),
        name="queries",
    )(src, *pieces, gain.reshape(count, share), w_query)


def back_kernel(count, src, *refs):
    pieces, rest = views(count, refs)
    w_hbm, out, w_buf, sems = rest
    share = pieces[0].shape[1]
    copies = []
    for k in range(count):
        start = pl.multiple_of(src[k] * share, share)
        cp = pltpu.make_async_copy(w_hbm.at[:, pl.ds(start, share)], w_buf.at[k], sems.at[k])
        cp.start()
        copies.append(cp)
    acc = jnp.zeros(out.shape, F32)
    for k in range(count):
        copies[k].wait()
        acc = acc + dot_nt(pieces[k][...], w_buf[k])
    out[...] = dot(shift_matrix(out.shape[0], BLOCK - 1, False), acc.astype(BF16)).astype(BF16)


def run_back(src, pieces, w_out):
    count = 2 * (len(pieces) - 1)
    rows, share = pieces[0].shape
    cols = w_out.shape[0]
    return pl.pallas_call(
        lambda *r: back_kernel(count, *r),
        out_shape=jax.ShapeDtypeStruct((rows, cols), BF16),
        in_specs=[smem()] + [vmem()] * len(pieces) + [hbm()],
        out_specs=vmem(),
        scratch_shapes=[pltpu.VMEM((count, cols, share), BF16), pltpu.SemaphoreType.DMA((count,))],
        compiler_params=params(),
        cost_estimate=cost(4.5),
        name="d_attended",
    )(src, *pieces, w_out)


def branch_kernel(count, src, att_a, att_b, w_hbm, send, keep, w_buf, sems):
    share = send.shape[2]
    half = count // 2
    copies = []
    order = list(range(half, count)) + list(range(half))
    for k in order:
        start = pl.multiple_of(src[k] * share, share)
        cp = pltpu.make_async_copy(w_hbm.at[:, pl.ds(start, share)], w_buf.at[k], sems.at[k])
        cp.start()
        copies.append(cp)
    shifted = jnp.concatenate([att_a[...], att_b[...]], axis=0)
    a = dot(shift_matrix(shifted.shape[0], BLOCK - 1, True), shifted).astype(BF16)
    for k, cp in zip(order, copies):
        cp.wait()
        out = keep.at[k] if k < half else send.at[k - half]
        out[...] = dot(a, w_buf[k]).astype(BF16)


def run_branch(src, att_a, att_b, w_out, count):
    rows, cols = 2 * att_a.shape[0], att_a.shape[1]
    share = w_out.shape[1] // count
    shape = jax.ShapeDtypeStruct((count // 2, rows, share), BF16)
    return pl.pallas_call(
        lambda *r: branch_kernel(count, *r),
        out_shape=(shape, shape),
        in_specs=[smem(), vmem(), vmem(), hbm()],
        out_specs=(vmem(), vmem()),
        scratch_shapes=[pltpu.VMEM((count, cols, share), BF16), pltpu.SemaphoreType.DMA((count,))],
        compiler_params=params(),
        cost_estimate=cost(4),
        name="branches",
    )(src, att_a, att_b, w_out)


def attention_kernel(count, first, blocks, *refs):
    half = count // 2
    pieces = list(refs[:half]) + [refs[half].at[0]] + [refs[half + 1].at[k] for k in range(half - 1)]
    q_ref, d_ref, wk, wv, send, keep, att, mem, keys, values, k_grad, v_grad = refs[half + 2 :]
    heads = q_ref.shape[1] // HD
    part = send.shape[1] // blocks
    span = part * count
    scale = HD ** (-0.5)
    for b in range(blocks):
        for k in range(count):
            mem[b * span + k * part : b * span + (k + 1) * part, :] = pieces[k][
                (first + b) * part : (first + b + 1) * part, :
            ]
    keys[...] = dot(mem[...], wk[...]).astype(BF16)
    values[...] = dot(mem[...], wv[...]).astype(BF16)
    for b in range(blocks):
        rows = slice(b * BLOCK, (b + 1) * BLOCK)
        ctx = slice(b * span, (b + 1) * span)
        for h in range(heads):
            cols = slice(h * HD, (h + 1) * HD)
            q = q_ref[first * BLOCK + b * BLOCK : first * BLOCK + (b + 1) * BLOCK, cols]
            d = d_ref[first * BLOCK + b * BLOCK : first * BLOCK + (b + 1) * BLOCK, cols]
            kk = keys[ctx, cols]
            vv = values[ctx, cols]
            scores = dot_nt(q, kk) * scale
            lifted = jnp.exp(scores - jnp.max(scores, axis=-1, keepdims=True))
            prob = lifted / jnp.sum(lifted, axis=-1, keepdims=True)
            weights = prob.astype(BF16)
            att[rows, cols] = dot(weights, vv).astype(BF16)
            d_prob = dot_nt(d, vv)
            d_scores = (
                prob * (d_prob - jnp.sum(prob * d_prob, axis=-1, keepdims=True)) * scale
            ).astype(BF16)
            v_grad[ctx, cols] = dot_tn(weights, d).astype(BF16)
            k_grad[ctx, cols] = dot_tn(d_scores, q).astype(BF16)
    for b in range(blocks):
        ctx = slice(b * span, (b + 1) * span)
        terms = (dot_nt(k_grad[ctx, :], wk[...]) + dot_nt(v_grad[ctx, :], wv[...])).astype(BF16)
        for k in range(count):
            out = keep.at[k] if k < half else send.at[k - half]
            out[b * part : (b + 1) * part, :] = terms[k * part : (k + 1) * part, :]


def run_attention(pieces, q, d, w_key, w_value, first, blocks, all_blocks):
    count = 2 * (len(pieces) - 2)
    rows, width = pieces[0].shape
    rows = rows // all_blocks * blocks
    cols = q.shape[1]
    total = rows * count
    shape = jax.ShapeDtypeStruct((count // 2, rows, width), BF16)
    return pl.pallas_call(
        lambda *r: attention_kernel(count, first, blocks, *r),
        out_shape=(shape, shape, jax.ShapeDtypeStruct((blocks * BLOCK, cols), BF16)),
        in_specs=[vmem()] * (len(pieces) + 4),
        out_specs=(vmem(), vmem(), vmem()),
        scratch_shapes=[pltpu.VMEM((total, width), BF16)]
        + [pltpu.VMEM((total, cols), BF16)] * 4,
        compiler_params=params(),
        cost_estimate=cost(7),
        name="attention",
    )(*pieces, q, d, w_key, w_value)


def outgoing_kernel(req, enc, gain, out, normed):
    wide = enc[...].astype(F32)
    normed[...] = (wide * rms_scale(wide) * gain[...]).astype(BF16)
    for s in range(out.shape[0]):
        out[s] = normed[jnp.maximum(req[s, 0], 0)]


def run_outgoing(requested, encodings, gain):
    slots = requested.shape[0]
    return pl.pallas_call(
        outgoing_kernel,
        out_shape=jax.ShapeDtypeStruct((slots,) + encodings.shape[1:], BF16),
        in_specs=[smem(), vmem(), vmem()],
        out_specs=vmem(),
        scratch_shapes=[pltpu.VMEM(encodings.shape, BF16)],
        compiler_params=params(),
        cost_estimate=cost(1.7),
        name="outgoing_rows",
    )(requested, encodings, gain.reshape(1, 1, -1))


def pick_kernel(owner, rows, out, sems):
    copies = []
    for a in range(out.shape[0]):
        cp = pltpu.make_async_copy(rows.at[owner[a]], out.at[a], sems.at[a])
        cp.start()
        copies.append(cp)
    for cp in copies:
        cp.wait()


def run_pick(owner, rows):
    n = owner.shape[0]
    return pl.pallas_call(
        pick_kernel,
        out_shape=jax.ShapeDtypeStruct((n,) + rows.shape[1:], rows.dtype),
        in_specs=[smem(), hbm()],
        out_specs=vmem(),
        scratch_shapes=[pltpu.SemaphoreType.DMA((n,))],
        compiler_params=params(),
        cost_estimate=cost(1),
        name="picked_rows",
    )(owner, rows)


def place_kernel(reading, *refs):
    parts, out, total = refs[:-2], refs[-2], refs[-1]
    half = len(parts) // 2
    rows = parts[0].shape[0]
    for i in range(2):
        group = [p[...].astype(F32) for p in parts[i * half : (i + 1) * half]]
        total[i * rows : (i + 1) * rows] = sum(group).astype(BF16)
    for s in range(out.shape[0]):
        out[s] = total[reading[s]]


def run_place(reading, parts):
    slots = reading.shape[0]
    rows, *rest = parts[0].shape
    return pl.pallas_call(
        place_kernel,
        out_shape=jax.ShapeDtypeStruct((slots, *rest), BF16),
        in_specs=[smem()] + [vmem()] * len(parts),
        out_specs=vmem(),
        scratch_shapes=[pltpu.VMEM((2 * rows, *rest), BF16)],
        compiler_params=params(),
        cost_estimate=cost(1.7),
        name="placed_grads",
    )(reading, *parts)


def finish_kernel(slot, back, enc, gain, out, buf, sems):
    copies = []
    for j in range(out.shape[0]):
        cp = pltpu.make_async_copy(back.at[slot[j]], buf.at[j], sems.at[j])
        cp.start()
        copies.append(cp)
    wide = enc[...].astype(F32)
    scale = rms_scale(wide)
    hat = wide * scale
    for cp in copies:
        cp.wait()
    up = gain[...] * buf[...].astype(F32)
    out[...] = (scale * (up - hat * jnp.mean(up * hat, axis=-1, keepdims=True))).astype(BF16)


def run_finish(slot, back, encodings, gain):
    rows = encodings.shape[0]
    return pl.pallas_call(
        finish_kernel,
        out_shape=jax.ShapeDtypeStruct(encodings.shape, BF16),
        in_specs=[smem(), hbm(), vmem(), vmem()],
        out_specs=vmem(),
        scratch_shapes=[pltpu.VMEM(encodings.shape, BF16), pltpu.SemaphoreType.DMA((rows,))],
        compiler_params=params(),
        cost_estimate=cost(1.9),
        name="d_encodings",
    )(slot, back, encodings, gain.reshape(1, 1, -1))


def shards(
    tokens,
    cotangent,
    gain_dec,
    w_query,
    w_out,
    encodings,
    gain_enc,
    w_key,
    w_value,
    gain_post,
    neighbour_ids,
):
    dp_count = lax.axis_size("dp")
    count = lax.axis_size("mp")
    half = count // 2
    share_cols = tokens.shape[1]
    own_rows, own_tokens, width = encodings.shape
    blocks = neighbour_ids.shape[0]
    readings = blocks * neighbour_ids.shape[1]
    here = lax.axis_index("mp")
    steps = jnp.arange(half, dtype=jnp.int32)
    same = (here - 2 * steps) % count
    src = jnp.concatenate([same, same ^ 1]).astype(jnp.int32)

    chosen = neighbour_ids.reshape(readings)
    owner = chosen // own_rows
    local_row = chosen % own_rows
    slots = jnp.arange(dp_count, dtype=jnp.int32)
    matches = owner[:, None] == slots[None, :]
    wanted = jnp.sum(jnp.where(matches, local_row[:, None] + 1, 0), axis=0) - 1
    reading = jnp.sum(
        jnp.where(matches, jnp.arange(readings, dtype=jnp.int32)[:, None], 0), axis=0
    )
    requested = lax.all_to_all(
        jnp.broadcast_to(wanted[:, None], (dp_count, IDS_WIDTH)),
        "dp",
        split_axis=0,
        concat_axis=0,
        tiled=True,
    )
    serves = requested[:, :1] == jnp.arange(own_rows, dtype=jnp.int32)[None, :]
    slot = jnp.sum(jnp.where(serves, slots[:, None], 0), axis=0)

    tok_own = over_chips(tokens, count)
    enc_in, tok_own = lax.optimization_barrier((encodings, tok_own))
    outgoing = run_outgoing(requested, enc_in, gain_enc)
    outgoing, cot_in = lax.optimization_barrier((outgoing, cotangent))
    cot_own = over_chips(cot_in, count)
    incoming = lax.all_to_all(outgoing, "dp", split_axis=0, concat_axis=0, tiled=True)
    q = run_query(src, tok_own + [swap(jnp.stack(tok_own), count)], gain_dec, w_query)
    d = run_back(src, cot_own + [swap(jnp.stack(cot_own), count)], w_out)
    incoming, q, d = lax.optimization_barrier((incoming, q, d))
    picked = run_pick(owner, incoming).reshape(readings * own_tokens, width)
    row_own = over_chips(picked, count)
    rows = row_own + [swap(picked, count)[None], swap(jnp.stack(row_own[1:]), count)]
    first = blocks // 2
    send_a, keep_a, att_a = run_attention(rows, q, d, w_key, w_value, 0, first, blocks)
    pair_a = pair_sum(send_a, keep_a, count)
    rows, pair_a = lax.optimization_barrier((rows, pair_a))
    parts_a = pair_shares(pair_a, count)
    send_b, keep_b, att_b = run_attention(
        rows, q, d, w_key, w_value, first, blocks - first, blocks
    )
    send_b, parts_a = lax.optimization_barrier((send_b, parts_a))
    pair_b = pair_sum(send_b, keep_b, count)
    att_b, pair_b = lax.optimization_barrier((att_b, pair_b))
    parts_b = pair_shares(pair_b, count)
    b_send, b_keep = run_branch(src, att_a, att_b, w_out, count)
    b_send, parts_b = lax.optimization_barrier((b_send, parts_b))
    b_pair = pair_sum(b_send, b_keep, count)
    b_parts = pair_shares(b_pair, count)
    back_out = run_place(
        reading,
        [p.reshape(readings // 2, own_tokens, width) for p in parts_a + parts_b],
    )
    back_in = lax.all_to_all(back_out, "dp", split_axis=0, concat_axis=0, tiled=True)

    summed = sum(p.astype(F32) for p in b_parts)
    mixed = (tokens.astype(F32) + summed).astype(BF16)
    mixed_wide = mixed.astype(F32)
    squares = jnp.sum(mixed_wide * mixed_wide, axis=1)
    total = jnp.sum(lax.all_gather(squares, "mp", axis=0), axis=0)
    post = lax.rsqrt(total / (share_cols * count) + EPS)[:, None]
    gain_here = lax.dynamic_slice_in_dim(gain_post, here * share_cols, share_cols, 0)
    ffn = (mixed_wide * post * gain_here).astype(BF16)

    d_encodings = run_finish(slot, back_in, encodings, gain_enc)
    return (mixed, ffn, d_encodings)


def solution(mesh):
    in_specs = (
        P("dp", "mp"),
        P("dp", "mp"),
        P(),
        P(None, "mp"),
        P("mp", None),
        P("dp", "mp", None),
        P(),
        P(None, "mp"),
        P(None, "mp"),
        P(),
        P("dp", None),
    )
    out_specs = (P("dp", "mp"), P("dp", "mp"), P("dp", "mp", None))
    return jax.shard_map(shards, mesh=mesh, in_specs=in_specs, out_specs=out_specs, check_vma=False)
```

```python
import jax
import jax.numpy as jnp
from jax import lax
from jax.experimental import pallas as pl
from jax.experimental.pallas import tpu as pltpu
from jax.sharding import PartitionSpec as P

HD = 128
BLOCK = 64
NLEN = 128
NEIGH = 2

EPS = 1e-06
F32 = jnp.float32
BF16 = jnp.bfloat16
IDS_WIDTH = 128
GROUP = 8
MIX_COST = 100
VMEM_LIMIT = 48 * 1024 * 1024


def rms_scale(values):
    return lax.rsqrt(jnp.mean(values * values, axis=-1, keepdims=True) + EPS)


def params():
    return pltpu.CompilerParams(vmem_limit_bytes=VMEM_LIMIT)


def cost(micros):
    return pl.CostEstimate(flops=int(micros * 1.1e9), bytes_accessed=0, transcendentals=0)


def vmem():
    return pl.BlockSpec(memory_space=pltpu.VMEM)


def hbm():
    return pl.BlockSpec(memory_space=pl.ANY)


def smem():
    return pl.BlockSpec(memory_space=pltpu.SMEM)


def chip_shift(count, k):
    return [(i, (i + 2 * k) % count) for i in range(count)]


def core_swap(count):
    return [(i, i ^ 1) for i in range(count)]


def over_chips(x, count):
    return [x] + [lax.ppermute(x, "mp", chip_shift(count, k)) for k in range(1, count // 2)]


def swap(x, count):
    return lax.ppermute(x, "mp", core_swap(count))


def pair_sum(send, keep, count):
    return (keep.astype(F32) + swap(send, count).astype(F32)).astype(BF16)


def pair_shares(pair, count):
    return [pair[0]] + [
        lax.ppermute(pair[k], "mp", chip_shift(count, -k)) for k in range(1, count // 2)
    ]


def shift_matrix(n, lead, transpose):
    r = lax.broadcasted_iota(jnp.int32, (n, n), 0)
    c = lax.broadcasted_iota(jnp.int32, (n, n), 1)
    hit = (r == c + lead) if transpose else (c == r + lead)
    return jnp.where(hit, 1.0, 0.0).astype(BF16)


def dot(a, b):
    return lax.dot_general(a, b, (((1,), (0,)), ((), ())), preferred_element_type=F32)


def dot_nt(a, b):
    return lax.dot_general(a, b, (((1,), (1,)), ((), ())), preferred_element_type=F32)


def dot_tn(a, b):
    return lax.dot_general(a, b, (((0,), (0,)), ((), ())), preferred_element_type=F32)


def views(count, refs):
    half = count // 2
    return list(refs[:half]) + [refs[half].at[k] for k in range(half)], refs[half + 1 :]


def query_kernel(count, src, *refs):
    pieces, rest = views(count, refs)
    gain, w_hbm, out, w_buf, sems = rest
    share = pieces[0].shape[1]
    copies = []
    for k in range(count):
        start = pl.multiple_of(src[k] * share, share)
        cp = pltpu.make_async_copy(w_hbm.at[pl.ds(start, share), :], w_buf.at[k], sems.at[k])
        cp.start()
        copies.append(cp)
    squares = jnp.zeros((pieces[0].shape[0], 1), F32)
    for k in range(count):
        wide = pieces[k][...].astype(F32)
        squares = squares + jnp.sum(wide * wide, axis=1, keepdims=True)
    scale = lax.rsqrt(squares / (share * count) + EPS)
    acc = jnp.zeros(out.shape, F32)
    for k in range(count):
        g = gain[pl.ds(src[k], 1), :]
        normed = (pieces[k][...].astype(F32) * scale * g).astype(BF16)
        copies[k].wait()
        acc = acc + dot(normed, w_buf[k])
    out[...] = dot(shift_matrix(out.shape[0], BLOCK - 1, False), acc.astype(BF16)).astype(BF16)


def run_query(src, pieces, gain, w_query):
    count = 2 * (len(pieces) - 1)
    rows, share = pieces[0].shape
    cols = w_query.shape[1]
    return pl.pallas_call(
        lambda *r: query_kernel(count, *r),
        out_shape=jax.ShapeDtypeStruct((rows, cols), BF16),
        in_specs=[smem()] + [vmem()] * (len(pieces) + 1) + [hbm()],
        out_specs=vmem(),
        scratch_shapes=[pltpu.VMEM((count, share, cols), BF16), pltpu.SemaphoreType.DMA((count,))],
        compiler_params=params(),
        cost_estimate=cost(2.25),
        name="queries",
    )(src, *pieces, gain.reshape(count, share), w_query)


def back_kernel(count, src, *refs):
    pieces, rest = views(count, refs)
    w_hbm, out, w_buf, sems = rest
    share = pieces[0].shape[1]
    copies = []
    for k in range(count):
        start = pl.multiple_of(src[k] * share, share)
        cp = pltpu.make_async_copy(w_hbm.at[:, pl.ds(start, share)], w_buf.at[k], sems.at[k])
        cp.start()
        copies.append(cp)
    acc = jnp.zeros(out.shape, F32)
    for k in range(count):
        copies[k].wait()
        acc = acc + dot_nt(pieces[k][...], w_buf[k])
    out[...] = dot(shift_matrix(out.shape[0], BLOCK - 1, False), acc.astype(BF16)).astype(BF16)


def run_back(src, pieces, w_out):
    count = 2 * (len(pieces) - 1)
    rows, share = pieces[0].shape
    cols = w_out.shape[0]
    return pl.pallas_call(
        lambda *r: back_kernel(count, *r),
        out_shape=jax.ShapeDtypeStruct((rows, cols), BF16),
        in_specs=[smem()] + [vmem()] * len(pieces) + [hbm()],
        out_specs=vmem(),
        scratch_shapes=[pltpu.VMEM((count, cols, share), BF16), pltpu.SemaphoreType.DMA((count,))],
        compiler_params=params(),
        cost_estimate=cost(2.25),
        name="d_attended",
    )(src, *pieces, w_out)


def branch_kernel(count, src, att, w_hbm, send, keep, w_buf, sems):
    share = send.shape[2]
    half = count // 2
    copies = []
    order = list(range(half, count)) + list(range(half))
    for k in order:
        start = pl.multiple_of(src[k] * share, share)
        cp = pltpu.make_async_copy(w_hbm.at[:, pl.ds(start, share)], w_buf.at[k], sems.at[k])
        cp.start()
        copies.append(cp)
    a = dot(shift_matrix(att.shape[0], BLOCK - 1, True), att[...]).astype(BF16)
    for k, cp in zip(order, copies):
        cp.wait()
        out = keep.at[k] if k < half else send.at[k - half]
        out[...] = dot(a, w_buf[k]).astype(BF16)


def run_branch(src, att, w_out, count):
    rows, cols = att.shape
    share = w_out.shape[1] // count
    shape = jax.ShapeDtypeStruct((count // 2, rows, share), BF16)
    return pl.pallas_call(
        lambda *r: branch_kernel(count, *r),
        out_shape=(shape, shape),
        in_specs=[smem(), vmem(), hbm()],
        out_specs=(vmem(), vmem()),
        scratch_shapes=[pltpu.VMEM((count, cols, share), BF16), pltpu.SemaphoreType.DMA((count,))],
        compiler_params=params(),
        cost_estimate=cost(4),
        name="branches",
    )(src, att, w_out)


def attention_kernel(count, blocks, *refs):
    half = count // 2
    pieces = list(refs[:half]) + [refs[half].at[0]] + [refs[half + 1].at[k] for k in range(half - 1)]
    q_ref, d_ref, wk, wv, send, keep, att, mem, keys, values, k_grad, v_grad = refs[half + 2 :]
    heads = q_ref.shape[1] // HD
    part = send.shape[1] // blocks
    span = part * count
    scale = HD ** (-0.5)

    def rows(b):
        return slice(b * BLOCK, (b + 1) * BLOCK)

    def ctx(b):
        return slice(b * span, (b + 1) * span)

    def cols(h):
        return slice(h * HD, (h + 1) * HD)

    def softmax(scores):
        scores = scores * scale
        lifted = jnp.exp(scores - jnp.max(scores, axis=-1, keepdims=True))
        return lifted / jnp.sum(lifted, axis=-1, keepdims=True)

    def score_grad(p, dp):
        return (p * (dp - jnp.sum(p * dp, axis=-1, keepdims=True)) * scale).astype(BF16)

    for b in range(blocks):
        for k in range(count):
            mem[b * span + k * part : b * span + (k + 1) * part, :] = pieces[k][
                b * part : (b + 1) * part, :
            ]
    keys[...] = dot(mem[...], wk[...]).astype(BF16)
    values[...] = dot(mem[...], wv[...]).astype(BF16)
    every = [(b, h) for b in range(blocks) for h in range(heads)]
    for start in range(0, len(every), GROUP):
        group = every[start : start + GROUP]
        scores = [dot_nt(q_ref[rows(b), cols(h)], keys[ctx(b), cols(h)]) for b, h in group]
        d_probs = [dot_nt(d_ref[rows(b), cols(h)], values[ctx(b), cols(h)]) for b, h in group]
        probs = [softmax(s) for s in scores]
        weights = [p.astype(BF16) for p in probs]
        d_scores = [score_grad(p, dp) for p, dp in zip(probs, d_probs)]
        for w, ds, (b, h) in zip(weights, d_scores, group):
            att[rows(b), cols(h)] = dot(w, values[ctx(b), cols(h)]).astype(BF16)
            v_grad[ctx(b), cols(h)] = dot_tn(w, d_ref[rows(b), cols(h)]).astype(BF16)
            k_grad[ctx(b), cols(h)] = dot_tn(ds, q_ref[rows(b), cols(h)]).astype(BF16)
    for b in range(blocks):
        terms = (dot_nt(k_grad[ctx(b), :], wk[...]) + dot_nt(v_grad[ctx(b), :], wv[...])).astype(
            BF16
        )
        for k in range(count):
            out = keep.at[k] if k < half else send.at[k - half]
            out[b * part : (b + 1) * part, :] = terms[k * part : (k + 1) * part, :]


def run_attention(pieces, q, d, w_key, w_value, blocks):
    count = 2 * (len(pieces) - 2)
    rows, width = pieces[0].shape
    cols = q.shape[1]
    total = rows * count
    shape = jax.ShapeDtypeStruct((count // 2, rows, width), BF16)
    return pl.pallas_call(
        lambda *r: attention_kernel(count, blocks, *r),
        out_shape=(shape, shape, jax.ShapeDtypeStruct((blocks * BLOCK, cols), BF16)),
        in_specs=[vmem()] * (len(pieces) + 4),
        out_specs=(vmem(), vmem(), vmem()),
        scratch_shapes=[pltpu.VMEM((total, width), BF16)]
        + [pltpu.VMEM((total, cols), BF16)] * 4,
        compiler_params=params(),
        cost_estimate=cost(9),
        name="attention",
    )(*pieces, q, d, w_key, w_value)


def outgoing_kernel(req, enc, gain, out, normed):
    wide = enc[...].astype(F32)
    normed[...] = (wide * rms_scale(wide) * gain[...]).astype(BF16)
    for s in range(out.shape[0]):
        out[s] = normed[jnp.maximum(req[s, 0], 0)]


def run_outgoing(requested, encodings, gain):
    slots = requested.shape[0]
    return pl.pallas_call(
        outgoing_kernel,
        out_shape=jax.ShapeDtypeStruct((slots,) + encodings.shape[1:], BF16),
        in_specs=[smem(), vmem(), vmem()],
        out_specs=vmem(),
        scratch_shapes=[pltpu.VMEM(encodings.shape, BF16)],
        compiler_params=params(),
        cost_estimate=cost(1.7),
        name="outgoing_rows",
    )(requested, encodings, gain.reshape(1, 1, -1))


def pick_kernel(owner, rows, out, sems):
    copies = []
    for a in range(out.shape[0]):
        cp = pltpu.make_async_copy(rows.at[owner[a]], out.at[a], sems.at[a])
        cp.start()
        copies.append(cp)
    for cp in copies:
        cp.wait()


def run_pick(owner, rows):
    n = owner.shape[0]
    return pl.pallas_call(
        pick_kernel,
        out_shape=jax.ShapeDtypeStruct((n,) + rows.shape[1:], rows.dtype),
        in_specs=[smem(), hbm()],
        out_specs=vmem(),
        scratch_shapes=[pltpu.SemaphoreType.DMA((n,))],
        compiler_params=params(),
        cost_estimate=cost(2.25),
        name="picked_rows",
    )(owner, rows)


def place_kernel(reading, *refs):
    parts, out, total = refs[:-2], refs[-2], refs[-1]
    total[...] = sum(p[...].astype(F32) for p in parts).astype(BF16)
    for s in range(out.shape[0]):
        out[s] = total[reading[s]]


def run_place(reading, parts):
    slots = reading.shape[0]
    shape = parts[0].shape
    return pl.pallas_call(
        place_kernel,
        out_shape=jax.ShapeDtypeStruct((slots,) + shape[1:], BF16),
        in_specs=[smem()] + [vmem()] * len(parts),
        out_specs=vmem(),
        scratch_shapes=[pltpu.VMEM(shape, BF16)],
        compiler_params=params(),
        cost_estimate=cost(1.7),
        name="placed_grads",
    )(reading, *parts)


def mix_kernel(tok, *refs):
    parts, mixed, squares = refs[:-2], refs[-2], refs[-1]
    summed = sum(p[...].astype(F32) for p in parts)
    out = (tok[...].astype(F32) + summed).astype(BF16)
    mixed[...] = out
    wide = out.astype(F32)
    squares[...] = jnp.sum(wide * wide, axis=1, keepdims=True)


def run_mix(tokens, parts):
    return pl.pallas_call(
        mix_kernel,
        out_shape=(
            jax.ShapeDtypeStruct(tokens.shape, BF16),
            jax.ShapeDtypeStruct((tokens.shape[0], 1), F32),
        ),
        in_specs=[vmem()] * (len(parts) + 1),
        out_specs=(vmem(), vmem()),
        compiler_params=params(),
        cost_estimate=cost(MIX_COST),
        name="mixed",
    )(tokens, *parts)


def finish_kernel(slot, back, enc, gain, out, buf, sems):
    copies = []
    for j in range(out.shape[0]):
        cp = pltpu.make_async_copy(back.at[slot[j]], buf.at[j], sems.at[j])
        cp.start()
        copies.append(cp)
    wide = enc[...].astype(F32)
    scale = rms_scale(wide)
    hat = wide * scale
    for cp in copies:
        cp.wait()
    up = gain[...] * buf[...].astype(F32)
    out[...] = (scale * (up - hat * jnp.mean(up * hat, axis=-1, keepdims=True))).astype(BF16)


def run_finish(slot, back, encodings, gain):
    rows = encodings.shape[0]
    return pl.pallas_call(
        finish_kernel,
        out_shape=jax.ShapeDtypeStruct(encodings.shape, BF16),
        in_specs=[smem(), hbm(), vmem(), vmem()],
        out_specs=vmem(),
        scratch_shapes=[pltpu.VMEM(encodings.shape, BF16), pltpu.SemaphoreType.DMA((rows,))],
        compiler_params=params(),
        cost_estimate=cost(1.9),
        name="d_encodings",
    )(slot, back, encodings, gain.reshape(1, 1, -1))


def shards(
    tokens,
    cotangent,
    gain_dec,
    w_query,
    w_out,
    encodings,
    gain_enc,
    w_key,
    w_value,
    gain_post,
    neighbour_ids,
):
    dp_count = lax.axis_size("dp")
    count = lax.axis_size("mp")
    half = count // 2
    share_cols = tokens.shape[1]
    own_rows, own_tokens, width = encodings.shape
    blocks = neighbour_ids.shape[0]
    readings = blocks * neighbour_ids.shape[1]
    here = lax.axis_index("mp")
    steps = jnp.arange(half, dtype=jnp.int32)
    same = (here - 2 * steps) % count
    src = jnp.concatenate([same, same ^ 1]).astype(jnp.int32)

    chosen = neighbour_ids.reshape(readings)
    owner = chosen // own_rows
    local_row = chosen % own_rows
    slots = jnp.arange(dp_count, dtype=jnp.int32)
    matches = owner[:, None] == slots[None, :]
    wanted = jnp.sum(jnp.where(matches, local_row[:, None] + 1, 0), axis=0) - 1
    reading = jnp.sum(
        jnp.where(matches, jnp.arange(readings, dtype=jnp.int32)[:, None], 0), axis=0
    )
    requested = lax.all_to_all(
        jnp.broadcast_to(wanted[:, None], (dp_count, IDS_WIDTH)),
        "dp",
        split_axis=0,
        concat_axis=0,
        tiled=True,
    )
    serves = requested[:, :1] == jnp.arange(own_rows, dtype=jnp.int32)[None, :]
    slot = jnp.sum(jnp.where(serves, slots[:, None], 0), axis=0)

    tok_own = over_chips(tokens, count)
    outgoing = run_outgoing(requested, encodings, gain_enc)
    outgoing, cot_in = lax.optimization_barrier((outgoing, cotangent))
    incoming = lax.all_to_all(outgoing, "dp", split_axis=0, concat_axis=0, tiled=True)
    cot_own = over_chips(cot_in, count)
    q = run_query(src, tok_own + [swap(jnp.stack(tok_own), count)], gain_dec, w_query)
    d = run_back(src, cot_own + [swap(jnp.stack(cot_own), count)], w_out)
    incoming, q, d = lax.optimization_barrier((incoming, q, d))
    picked = run_pick(owner, incoming).reshape(readings * own_tokens, width)
    row_own = over_chips(picked, count)
    rows = row_own + [swap(picked, count)[None], swap(jnp.stack(row_own[1:]), count)]
    send, keep, att = run_attention(rows, q, d, w_key, w_value, blocks)
    pair = pair_sum(send, keep, count)
    parts = pair_shares(pair, count)
    b_send, b_keep = run_branch(src, att, w_out, count)
    b_pair = pair_sum(b_send, b_keep, count)
    parts, b_pair = lax.optimization_barrier((parts, b_pair))
    b_parts = pair_shares(b_pair, count)
    back_out = run_place(reading, [p.reshape(readings, own_tokens, width) for p in parts])
    back_in = lax.all_to_all(back_out, "dp", split_axis=0, concat_axis=0, tiled=True)

    mixed, squares = run_mix(tokens, b_parts)
    mixed_wide = mixed.astype(F32)
    squares = squares[:, 0]
    total = jnp.sum(lax.all_gather(squares, "mp", axis=0), axis=0)
    post = lax.rsqrt(total / (share_cols * count) + EPS)[:, None]
    gain_here = lax.dynamic_slice_in_dim(gain_post, here * share_cols, share_cols, 0)
    ffn = (mixed_wide * post * gain_here).astype(BF16)

    d_encodings = run_finish(slot, back_in, encodings, gain_enc)
    return (mixed, ffn, d_encodings)


def solution(mesh):
    in_specs = (
        P("dp", "mp"),
        P("dp", "mp"),
        P(),
        P(None, "mp"),
        P("mp", None),
        P("dp", "mp", None),
        P(),
        P(None, "mp"),
        P(None, "mp"),
        P(),
        P("dp", None),
    )
    out_specs = (P("dp", "mp"), P("dp", "mp"), P("dp", "mp", None))
    return jax.shard_map(shards, mesh=mesh, in_specs=in_specs, out_specs=out_specs, check_vma=False)
```

```python
import jax
import jax.numpy as jnp
from jax import lax
from jax.experimental import pallas as pl
from jax.experimental.pallas import tpu as pltpu
from jax.sharding import PartitionSpec as P

HD = 128
BLOCK = 64
NLEN = 128
NEIGH = 2

EPS = 1e-06
F32 = jnp.float32
BF16 = jnp.bfloat16
IDS_WIDTH = 128
GROUP = 8
MIX_COST = 100
VMEM_LIMIT = 24 * 1024 * 1024


def rms_scale(values):
    return lax.rsqrt(jnp.mean(values * values, axis=-1, keepdims=True) + EPS)


def params():
    return pltpu.CompilerParams(vmem_limit_bytes=VMEM_LIMIT)


def cost(micros):
    return pl.CostEstimate(flops=int(micros * 1.1e9), bytes_accessed=0, transcendentals=0)


def vmem():
    return pl.BlockSpec(memory_space=pltpu.VMEM)


def hbm():
    return pl.BlockSpec(memory_space=pl.ANY)


def smem():
    return pl.BlockSpec(memory_space=pltpu.SMEM)


def chip_shift(count, k):
    return [(i, (i + 2 * k) % count) for i in range(count)]


def core_swap(count):
    return [(i, i ^ 1) for i in range(count)]


def over_chips(x, count):
    return [x] + [lax.ppermute(x, "mp", chip_shift(count, k)) for k in range(1, count // 2)]


def swap(x, count):
    return lax.ppermute(x, "mp", core_swap(count))


def pair_sum(send, keep, count):
    return (keep.astype(F32) + swap(send, count).astype(F32)).astype(BF16)


def pair_shares(pair, count):
    return [pair[0]] + [
        lax.ppermute(pair[k], "mp", chip_shift(count, -k)) for k in range(1, count // 2)
    ]


def shift_matrix(n, lead, transpose):
    r = lax.broadcasted_iota(jnp.int32, (n, n), 0)
    c = lax.broadcasted_iota(jnp.int32, (n, n), 1)
    hit = (r == c + lead) if transpose else (c == r + lead)
    return jnp.where(hit, 1.0, 0.0).astype(BF16)


def dot(a, b):
    return lax.dot_general(a, b, (((1,), (0,)), ((), ())), preferred_element_type=F32)


def dot_nt(a, b):
    return lax.dot_general(a, b, (((1,), (1,)), ((), ())), preferred_element_type=F32)


def dot_tn(a, b):
    return lax.dot_general(a, b, (((0,), (0,)), ((), ())), preferred_element_type=F32)


def views(count, refs):
    half = count // 2
    return list(refs[:half]) + [refs[half].at[k] for k in range(half)], refs[half + 1 :]


def query_kernel(count, src, *refs):
    pieces, rest = views(count, refs)
    gain, w_hbm, out, w_buf, sems = rest
    share = pieces[0].shape[1]
    copies = []
    for k in range(count):
        start = pl.multiple_of(src[k] * share, share)
        cp = pltpu.make_async_copy(w_hbm.at[pl.ds(start, share), :], w_buf.at[k], sems.at[k])
        cp.start()
        copies.append(cp)
    squares = jnp.zeros((pieces[0].shape[0], 1), F32)
    for k in range(count):
        wide = pieces[k][...].astype(F32)
        squares = squares + jnp.sum(wide * wide, axis=1, keepdims=True)
    scale = lax.rsqrt(squares / (share * count) + EPS)
    acc = jnp.zeros(out.shape, F32)
    for k in range(count):
        g = gain[pl.ds(src[k], 1), :]
        normed = (pieces[k][...].astype(F32) * scale * g).astype(BF16)
        copies[k].wait()
        acc = acc + dot(normed, w_buf[k])
    out[...] = dot(shift_matrix(out.shape[0], BLOCK - 1, False), acc.astype(BF16)).astype(BF16)


def run_query(src, pieces, gain, w_query):
    count = 2 * (len(pieces) - 1)
    rows, share = pieces[0].shape
    cols = w_query.shape[1]
    return pl.pallas_call(
        lambda *r: query_kernel(count, *r),
        out_shape=jax.ShapeDtypeStruct((rows, cols), BF16),
        in_specs=[smem()] + [vmem()] * (len(pieces) + 1) + [hbm()],
        out_specs=vmem(),
        scratch_shapes=[pltpu.VMEM((count, share, cols), BF16), pltpu.SemaphoreType.DMA((count,))],
        compiler_params=params(),
        cost_estimate=cost(2.25),
        name="queries",
    )(src, *pieces, gain.reshape(count, share), w_query)


def back_kernel(count, whole, w_hbm, out, w_buf, sems):
    share = whole.shape[1] // count
    copies = []
    for k in range(count):
        cols = slice(k * share, (k + 1) * share)
        cp = pltpu.make_async_copy(w_hbm.at[:, cols], w_buf.at[k], sems.at[k])
        cp.start()
        copies.append(cp)
    acc = jnp.zeros(out.shape, F32)
    for k in range(count):
        copies[k].wait()
        acc = acc + dot_nt(whole[:, k * share : (k + 1) * share], w_buf[k])
    out[...] = dot(shift_matrix(out.shape[0], BLOCK - 1, False), acc.astype(BF16)).astype(BF16)


def run_back(whole, w_out, count):
    cols = w_out.shape[0]
    share = whole.shape[1] // count
    return pl.pallas_call(
        lambda *r: back_kernel(count, *r),
        out_shape=jax.ShapeDtypeStruct((whole.shape[0], cols), BF16),
        in_specs=[vmem(), hbm()],
        out_specs=vmem(),
        scratch_shapes=[pltpu.VMEM((count, cols, share), BF16), pltpu.SemaphoreType.DMA((count,))],
        compiler_params=params(),
        cost_estimate=cost(2.25),
        name="d_attended",
    )(whole, w_out)


def branch_kernel(count, att, w_hbm, out, w_buf, sems):
    share = out.shape[1] // count
    copies = []
    for k in range(count):
        cols = slice(k * share, (k + 1) * share)
        cp = pltpu.make_async_copy(w_hbm.at[:, cols], w_buf.at[k], sems.at[k])
        cp.start()
        copies.append(cp)
    a = dot(shift_matrix(att.shape[0], BLOCK - 1, True), att[...]).astype(BF16)
    for k in range(count):
        copies[k].wait()
        out[:, k * share : (k + 1) * share] = dot(a, w_buf[k]).astype(BF16)


def run_branch(att, w_out, count):
    rows, cols = att.shape
    width = w_out.shape[1]
    return pl.pallas_call(
        lambda *r: branch_kernel(count, *r),
        out_shape=jax.ShapeDtypeStruct((rows, width), BF16),
        in_specs=[vmem(), hbm()],
        out_specs=vmem(),
        scratch_shapes=[
            pltpu.VMEM((count, cols, width // count), BF16),
            pltpu.SemaphoreType.DMA((count,)),
        ],
        compiler_params=params(),
        cost_estimate=cost(4),
        name="branches",
    )(att, w_out)


def attention_kernel(count, blocks, *refs):
    half = count // 2
    pieces = list(refs[:half]) + [refs[half].at[0]] + [refs[half + 1].at[k] for k in range(half - 1)]
    q_ref, d_ref, wk, wv, send, keep, att, mem, keys, values, k_grad, v_grad = refs[half + 2 :]
    heads = q_ref.shape[1] // HD
    part = send.shape[1] // blocks
    span = part * count
    scale = HD ** (-0.5)

    def rows(b):
        return slice(b * BLOCK, (b + 1) * BLOCK)

    def ctx(b):
        return slice(b * span, (b + 1) * span)

    def cols(h):
        return slice(h * HD, (h + 1) * HD)

    def softmax(scores):
        scores = scores * scale
        lifted = jnp.exp(scores - jnp.max(scores, axis=-1, keepdims=True))
        return lifted / jnp.sum(lifted, axis=-1, keepdims=True)

    def score_grad(p, dp):
        return (p * (dp - jnp.sum(p * dp, axis=-1, keepdims=True)) * scale).astype(BF16)

    for b in range(blocks):
        for k in range(count):
            mem[b * span + k * part : b * span + (k + 1) * part, :] = pieces[k][
                b * part : (b + 1) * part, :
            ]
    keys[...] = dot(mem[...], wk[...]).astype(BF16)
    values[...] = dot(mem[...], wv[...]).astype(BF16)
    every = [(b, h) for b in range(blocks) for h in range(heads)]
    for start in range(0, len(every), GROUP):
        group = every[start : start + GROUP]
        scores = [dot_nt(q_ref[rows(b), cols(h)], keys[ctx(b), cols(h)]) for b, h in group]
        d_probs = [dot_nt(d_ref[rows(b), cols(h)], values[ctx(b), cols(h)]) for b, h in group]
        probs = [softmax(s) for s in scores]
        weights = [p.astype(BF16) for p in probs]
        d_scores = [score_grad(p, dp) for p, dp in zip(probs, d_probs)]
        for w, ds, (b, h) in zip(weights, d_scores, group):
            att[rows(b), cols(h)] = dot(w, values[ctx(b), cols(h)]).astype(BF16)
            v_grad[ctx(b), cols(h)] = dot_tn(w, d_ref[rows(b), cols(h)]).astype(BF16)
            k_grad[ctx(b), cols(h)] = dot_tn(ds, q_ref[rows(b), cols(h)]).astype(BF16)
    for b in range(blocks):
        terms = (dot_nt(k_grad[ctx(b), :], wk[...]) + dot_nt(v_grad[ctx(b), :], wv[...])).astype(
            BF16
        )
        for k in range(count):
            out = keep.at[k] if k < half else send.at[k - half]
            out[b * part : (b + 1) * part, :] = terms[k * part : (k + 1) * part, :]


def run_attention(pieces, q, d, w_key, w_value, blocks):
    count = 2 * (len(pieces) - 2)
    rows, width = pieces[0].shape
    cols = q.shape[1]
    total = rows * count
    shape = jax.ShapeDtypeStruct((count // 2, rows, width), BF16)
    return pl.pallas_call(
        lambda *r: attention_kernel(count, blocks, *r),
        out_shape=(shape, shape, jax.ShapeDtypeStruct((blocks * BLOCK, cols), BF16)),
        in_specs=[vmem()] * (len(pieces) + 4),
        out_specs=(vmem(), vmem(), vmem()),
        scratch_shapes=[pltpu.VMEM((total, width), BF16)]
        + [pltpu.VMEM((total, cols), BF16)] * 4,
        compiler_params=params(),
        cost_estimate=cost(9),
        name="attention",
    )(*pieces, q, d, w_key, w_value)


def outgoing_kernel(req, enc, gain, out, normed):
    wide = enc[...].astype(F32)
    normed[...] = (wide * rms_scale(wide) * gain[...]).astype(BF16)
    for s in range(out.shape[0]):
        out[s] = normed[jnp.maximum(req[s, 0], 0)]


def run_outgoing(requested, encodings, gain):
    slots = requested.shape[0]
    return pl.pallas_call(
        outgoing_kernel,
        out_shape=jax.ShapeDtypeStruct((slots,) + encodings.shape[1:], BF16),
        in_specs=[smem(), vmem(), vmem()],
        out_specs=vmem(),
        scratch_shapes=[pltpu.VMEM(encodings.shape, BF16)],
        compiler_params=params(),
        cost_estimate=cost(1.7),
        name="outgoing_rows",
    )(requested, encodings, gain.reshape(1, 1, -1))


def pick_kernel(owner, rows, out, sems):
    copies = []
    for a in range(out.shape[0]):
        cp = pltpu.make_async_copy(rows.at[owner[a]], out.at[a], sems.at[a])
        cp.start()
        copies.append(cp)
    for cp in copies:
        cp.wait()


def run_pick(owner, rows):
    n = owner.shape[0]
    return pl.pallas_call(
        pick_kernel,
        out_shape=jax.ShapeDtypeStruct((n,) + rows.shape[1:], rows.dtype),
        in_specs=[smem(), hbm()],
        out_specs=vmem(),
        scratch_shapes=[pltpu.SemaphoreType.DMA((n,))],
        compiler_params=params(),
        cost_estimate=cost(2.25),
        name="picked_rows",
    )(owner, rows)


def place_kernel(reading, *refs):
    parts, out, total = refs[:-2], refs[-2], refs[-1]
    total[...] = sum(p[...].astype(F32) for p in parts).astype(BF16)
    for s in range(out.shape[0]):
        out[s] = total[reading[s]]


def run_place(reading, parts):
    slots = reading.shape[0]
    shape = parts[0].shape
    return pl.pallas_call(
        place_kernel,
        out_shape=jax.ShapeDtypeStruct((slots,) + shape[1:], BF16),
        in_specs=[smem()] + [vmem()] * len(parts),
        out_specs=vmem(),
        scratch_shapes=[pltpu.VMEM(shape, BF16)],
        compiler_params=params(),
        cost_estimate=cost(60),
        name="placed_grads",
    )(reading, *parts)


def mix_kernel(tok, *refs):
    parts, mixed, squares = refs[:-2], refs[-2], refs[-1]
    summed = sum(p[...].astype(F32) for p in parts)
    out = (tok[...].astype(F32) + summed).astype(BF16)
    mixed[...] = out
    wide = out.astype(F32)
    squares[...] = jnp.sum(wide * wide, axis=1, keepdims=True)


def run_mix(tokens, parts):
    return pl.pallas_call(
        mix_kernel,
        out_shape=(
            jax.ShapeDtypeStruct(tokens.shape, BF16),
            jax.ShapeDtypeStruct((tokens.shape[0], 1), F32),
        ),
        in_specs=[vmem()] * (len(parts) + 1),
        out_specs=(vmem(), vmem()),
        compiler_params=params(),
        cost_estimate=cost(MIX_COST),
        name="mixed",
    )(tokens, *parts)


def finish_kernel(slot, back, enc, gain, out, buf, sems):
    copies = []
    for j in range(out.shape[0]):
        cp = pltpu.make_async_copy(back.at[slot[j]], buf.at[j], sems.at[j])
        cp.start()
        copies.append(cp)
    wide = enc[...].astype(F32)
    scale = rms_scale(wide)
    hat = wide * scale
    for cp in copies:
        cp.wait()
    up = gain[...] * buf[...].astype(F32)
    out[...] = (scale * (up - hat * jnp.mean(up * hat, axis=-1, keepdims=True))).astype(BF16)


def run_finish(slot, back, encodings, gain):
    rows = encodings.shape[0]
    return pl.pallas_call(
        finish_kernel,
        out_shape=jax.ShapeDtypeStruct(encodings.shape, BF16),
        in_specs=[smem(), hbm(), vmem(), vmem()],
        out_specs=vmem(),
        scratch_shapes=[pltpu.VMEM(encodings.shape, BF16), pltpu.SemaphoreType.DMA((rows,))],
        compiler_params=params(),
        cost_estimate=cost(1.9),
        name="d_encodings",
    )(slot, back, encodings, gain.reshape(1, 1, -1))


def shards(
    tokens,
    cotangent,
    gain_dec,
    w_query,
    w_out,
    encodings,
    gain_enc,
    w_key,
    w_value,
    gain_post,
    neighbour_ids,
):
    dp_count = lax.axis_size("dp")
    count = lax.axis_size("mp")
    half = count // 2
    share_cols = tokens.shape[1]
    own_rows, own_tokens, width = encodings.shape
    blocks = neighbour_ids.shape[0]
    readings = blocks * neighbour_ids.shape[1]
    here = lax.axis_index("mp")
    steps = jnp.arange(half, dtype=jnp.int32)
    same = (here - 2 * steps) % count
    src = jnp.concatenate([same, same ^ 1]).astype(jnp.int32)

    chosen = neighbour_ids.reshape(readings)
    owner = chosen // own_rows
    local_row = chosen % own_rows
    slots = jnp.arange(dp_count, dtype=jnp.int32)
    matches = owner[:, None] == slots[None, :]
    wanted = jnp.sum(jnp.where(matches, local_row[:, None] + 1, 0), axis=0) - 1
    reading = jnp.sum(
        jnp.where(matches, jnp.arange(readings, dtype=jnp.int32)[:, None], 0), axis=0
    )
    requested = lax.all_to_all(
        jnp.broadcast_to(wanted[:, None], (dp_count, IDS_WIDTH)),
        "dp",
        split_axis=0,
        concat_axis=0,
        tiled=True,
    )
    serves = requested[:, :1] == jnp.arange(own_rows, dtype=jnp.int32)[None, :]
    slot = jnp.sum(jnp.where(serves, slots[:, None], 0), axis=0)

    tok_own = over_chips(tokens, count)
    outgoing = run_outgoing(requested, encodings, gain_enc)
    incoming = lax.all_to_all(outgoing, "dp", split_axis=0, concat_axis=0, tiled=True)
    q = run_query(src, tok_own + [swap(jnp.stack(tok_own), count)], gain_dec, w_query)
    d = run_back(lax.all_gather(cotangent, "mp", axis=1, tiled=True), w_out, count)
    incoming, q, d = lax.optimization_barrier((incoming, q, d))
    picked = run_pick(owner, incoming).reshape(readings * own_tokens, width)
    row_own = over_chips(picked, count)
    rows = row_own + [swap(picked, count)[None], swap(jnp.stack(row_own[1:]), count)]
    send, keep, att = run_attention(rows, q, d, w_key, w_value, blocks)
    pair = pair_sum(send, keep, count)
    branch = run_branch(att, w_out, count)
    pair, branch = lax.optimization_barrier((pair, branch))
    parts = pair_shares(pair, count)
    summed = lax.psum_scatter(branch, "mp", scatter_dimension=1, tiled=True)
    back_out = run_place(reading, [p.reshape(readings, own_tokens, width) for p in parts])
    back_in = lax.all_to_all(back_out, "dp", split_axis=0, concat_axis=0, tiled=True)

    mixed, squares = run_mix(tokens, [summed])
    mixed_wide = mixed.astype(F32)
    squares = squares[:, 0]
    squares = squares + swap(squares, count)
    total = squares
    for k in range(1, half):
        total = total + lax.ppermute(squares, "mp", chip_shift(count, k))
    post = lax.rsqrt(total / (share_cols * count) + EPS)[:, None]
    gain_here = lax.dynamic_slice_in_dim(gain_post, here * share_cols, share_cols, 0)
    ffn = (mixed_wide * post * gain_here).astype(BF16)

    d_encodings = run_finish(slot, back_in, encodings, gain_enc)
    return (mixed, ffn, d_encodings)


def solution(mesh):
    in_specs = (
        P("dp", "mp"),
        P("dp", "mp"),
        P(),
        P(None, "mp"),
        P("mp", None),
        P("dp", "mp", None),
        P(),
        P(None, "mp"),
        P(None, "mp"),
        P(),
        P("dp", None),
    )
    out_specs = (P("dp", "mp"), P("dp", "mp"), P("dp", "mp", None))
    return jax.shard_map(shards, mesh=mesh, in_specs=in_specs, out_specs=out_specs, check_vma=False)
```

```python
import jax
import jax.numpy as jnp
from jax import lax
from jax.experimental import pallas as pl
from jax.experimental.pallas import tpu as pltpu
from jax.sharding import PartitionSpec as P

HD = 128
BLOCK = 64
NLEN = 128
NEIGH = 2

EPS = 1e-06
F32 = jnp.float32
BF16 = jnp.bfloat16
IDS_WIDTH = 128
GROUP = 8
MIX_COST = 1
MIB = 1024 * 1024


def rms_scale(values):
    return lax.rsqrt(jnp.mean(values * values, axis=-1, keepdims=True) + EPS)


def params(mib=8):
    return pltpu.CompilerParams(vmem_limit_bytes=mib * MIB)


def cost(micros):
    return pl.CostEstimate(flops=int(micros * 1.1e9), bytes_accessed=0, transcendentals=0)


def vmem():
    return pl.BlockSpec(memory_space=pltpu.VMEM)


def hbm():
    return pl.BlockSpec(memory_space=pltpu.HBM)


def smem():
    return pl.BlockSpec(memory_space=pltpu.SMEM)


def chip_shift(count, k):
    return [(i, (i + 2 * k) % count) for i in range(count)]


def core_swap(count):
    return [(i, i ^ 1) for i in range(count)]


def over_chips(x, count):
    return [x] + [lax.ppermute(x, "mp", chip_shift(count, k)) for k in range(1, count // 2)]


def swap(x, count):
    return lax.ppermute(x, "mp", core_swap(count))


def pair_kernel(keep, other, *outs):
    for k, out in enumerate(outs):
        out[...] = (keep[k].astype(F32) + other[k].astype(F32)).astype(BF16)


def pair_sum(keep, other):
    return pl.pallas_call(
        pair_kernel,
        out_shape=[jax.ShapeDtypeStruct(keep.shape[1:], BF16)] * keep.shape[0],
        in_specs=[vmem(), vmem()],
        out_specs=[vmem()] * keep.shape[0],
        compiler_params=params(12),
        cost_estimate=cost(0.7),
        name="pair_sums",
    )(keep, other)


def pair_shares(pair, count):
    return [pair[0]] + [
        lax.ppermute(pair[k], "mp", chip_shift(count, -k)) for k in range(1, count // 2)
    ]


def shift_matrix(n, lead, transpose):
    r = lax.broadcasted_iota(jnp.int32, (n, n), 0)
    c = lax.broadcasted_iota(jnp.int32, (n, n), 1)
    hit = (r == c + lead) if transpose else (c == r + lead)
    return jnp.where(hit, 1.0, 0.0).astype(BF16)


def dot(a, b):
    return lax.dot_general(a, b, (((1,), (0,)), ((), ())), preferred_element_type=F32)


def dot_nt(a, b):
    return lax.dot_general(a, b, (((1,), (1,)), ((), ())), preferred_element_type=F32)


def dot_tn(a, b):
    return lax.dot_general(a, b, (((0,), (0,)), ((), ())), preferred_element_type=F32)


def views(count, refs):
    half = count // 2
    return list(refs[:half]) + [refs[half].at[k] for k in range(half)], refs[half + 1 :]


def query_kernel(count, src, *refs):
    pieces, rest = views(count, refs)
    gain, w_hbm, out, w_buf, sems = rest
    share = pieces[0].shape[1]
    copies = []
    for k in range(count):
        start = pl.multiple_of(src[k] * share, share)
        cp = pltpu.make_async_copy(w_hbm.at[pl.ds(start, share), :], w_buf.at[k], sems.at[k])
        cp.start()
        copies.append(cp)
    squares = jnp.zeros((pieces[0].shape[0], 1), F32)
    for k in range(count):
        wide = pieces[k][...].astype(F32)
        squares = squares + jnp.sum(wide * wide, axis=1, keepdims=True)
    scale = lax.rsqrt(squares / (share * count) + EPS)
    acc = jnp.zeros(out.shape, F32)
    for k in range(count):
        g = gain[pl.ds(src[k], 1), :]
        normed = (pieces[k][...].astype(F32) * scale * g).astype(BF16)
        copies[k].wait()
        acc = acc + dot(normed, w_buf[k])
    out[...] = dot(shift_matrix(out.shape[0], BLOCK - 1, False), acc.astype(BF16)).astype(BF16)


def run_query(src, pieces, gain, w_query):
    count = 2 * (len(pieces) - 1)
    rows, share = pieces[0].shape
    cols = w_query.shape[1]
    return pl.pallas_call(
        lambda *r: query_kernel(count, *r),
        out_shape=jax.ShapeDtypeStruct((rows, cols), BF16),
        in_specs=[smem()] + [vmem()] * (len(pieces) + 1) + [hbm()],
        out_specs=vmem(),
        scratch_shapes=[pltpu.VMEM((count, share, cols), BF16), pltpu.SemaphoreType.DMA((count,))],
        compiler_params=params(20),
        cost_estimate=cost(4.5),
        name="queries",
    )(src, *pieces, gain.reshape(count, share), w_query)


def back_kernel(count, src, *refs):
    pieces = refs[:count]
    w_hbm, out, w_buf, sems = refs[count:]
    share = pieces[0].shape[1]
    copies = []
    for k in range(count):
        start = pl.multiple_of(src[k] * share, share)
        cp = pltpu.make_async_copy(w_hbm.at[:, pl.ds(start, share)], w_buf.at[k], sems.at[k])
        cp.start()
        copies.append(cp)
    acc = jnp.zeros(out.shape, F32)
    for k in range(count):
        copies[k].wait()
        acc = acc + dot_nt(pieces[k][...], w_buf[k])
    out[...] = dot(shift_matrix(out.shape[0], BLOCK - 1, False), acc.astype(BF16)).astype(BF16)


def run_back(src, pieces, w_out):
    count = len(pieces)
    rows, share = pieces[0].shape
    cols = w_out.shape[0]
    return pl.pallas_call(
        lambda *r: back_kernel(count, *r),
        out_shape=jax.ShapeDtypeStruct((rows, cols), BF16),
        in_specs=[smem()] + [vmem()] * len(pieces) + [hbm()],
        out_specs=vmem(),
        scratch_shapes=[pltpu.VMEM((count, cols, share), BF16), pltpu.SemaphoreType.DMA((count,))],
        compiler_params=params(20),
        cost_estimate=cost(4.5),
        name="d_attended",
    )(src, *pieces, w_out)


def branch_kernel(count, src, att, w_hbm, send, keep, w_buf, sems):
    share = send.shape[2]
    half = count // 2
    copies = []
    order = list(range(half, count)) + list(range(half))
    for k in order:
        start = pl.multiple_of(src[k] * share, share)
        cp = pltpu.make_async_copy(w_hbm.at[:, pl.ds(start, share)], w_buf.at[k], sems.at[k])
        cp.start()
        copies.append(cp)
    a = dot(shift_matrix(att.shape[0], BLOCK - 1, True), att[...]).astype(BF16)
    for k, cp in zip(order, copies):
        cp.wait()
        out = keep.at[k] if k < half else send.at[k - half]
        out[...] = dot(a, w_buf[k]).astype(BF16)


def run_branch(src, att, w_out, count):
    rows, cols = att.shape
    share = w_out.shape[1] // count
    shape = jax.ShapeDtypeStruct((count // 2, rows, share), BF16)
    return pl.pallas_call(
        lambda *r: branch_kernel(count, *r),
        out_shape=(shape, shape),
        in_specs=[smem(), vmem(), hbm()],
        out_specs=(vmem(), vmem()),
        scratch_shapes=[pltpu.VMEM((count, cols, share), BF16), pltpu.SemaphoreType.DMA((count,))],
        compiler_params=params(20),
        cost_estimate=cost(4),
        name="branches",
    )(src, att, w_out)


def attention_kernel(count, blocks, *refs):
    half = count // 2
    pieces = refs[:count]
    q_ref, d_ref, wk, wv, send, keep, att, mem, keys, values, k_grad, v_grad = refs[count:]
    heads = q_ref.shape[1] // HD
    part = send.shape[1] // blocks
    span = part * count
    scale = HD ** (-0.5)

    def rows(b):
        return slice(b * BLOCK, (b + 1) * BLOCK)

    def ctx(b):
        return slice(b * span, (b + 1) * span)

    def cols(h):
        return slice(h * HD, (h + 1) * HD)

    def softmax(scores):
        scores = scores * scale
        lifted = jnp.exp(scores - jnp.max(scores, axis=-1, keepdims=True))
        return lifted / jnp.sum(lifted, axis=-1, keepdims=True)

    def score_grad(p, dp):
        return (p * (dp - jnp.sum(p * dp, axis=-1, keepdims=True)) * scale).astype(BF16)

    for b in range(blocks):
        for k in range(count):
            mem[b * span + k * part : b * span + (k + 1) * part, :] = pieces[k][
                b * part : (b + 1) * part, :
            ]
    keys[...] = dot(mem[...], wk[...]).astype(BF16)
    values[...] = dot(mem[...], wv[...]).astype(BF16)
    every = [(b, h) for b in range(blocks) for h in range(heads)]
    for start in range(0, len(every), GROUP):
        group = every[start : start + GROUP]
        scores = [dot_nt(q_ref[rows(b), cols(h)], keys[ctx(b), cols(h)]) for b, h in group]
        d_probs = [dot_nt(d_ref[rows(b), cols(h)], values[ctx(b), cols(h)]) for b, h in group]
        probs = [softmax(s) for s in scores]
        weights = [p.astype(BF16) for p in probs]
        d_scores = [score_grad(p, dp) for p, dp in zip(probs, d_probs)]
        for w, ds, (b, h) in zip(weights, d_scores, group):
            att[rows(b), cols(h)] = dot(w, values[ctx(b), cols(h)]).astype(BF16)
            v_grad[ctx(b), cols(h)] = dot_tn(w, d_ref[rows(b), cols(h)]).astype(BF16)
            k_grad[ctx(b), cols(h)] = dot_tn(ds, q_ref[rows(b), cols(h)]).astype(BF16)
    for b in range(blocks):
        terms = (dot_nt(k_grad[ctx(b), :], wk[...]) + dot_nt(v_grad[ctx(b), :], wv[...])).astype(
            BF16
        )
        for k in range(count):
            out = keep.at[k] if k < half else send.at[k - half]
            out[b * part : (b + 1) * part, :] = terms[k * part : (k + 1) * part, :]


def run_attention(pieces, q, d, w_key, w_value, blocks):
    count = len(pieces)
    rows, width = pieces[0].shape
    cols = q.shape[1]
    total = rows * count
    shape = jax.ShapeDtypeStruct((count // 2, rows, width), BF16)
    return pl.pallas_call(
        lambda *r: attention_kernel(count, blocks, *r),
        out_shape=(shape, shape, jax.ShapeDtypeStruct((blocks * BLOCK, cols), BF16)),
        in_specs=[vmem()] * (len(pieces) + 4),
        out_specs=(vmem(), vmem(), vmem()),
        scratch_shapes=[pltpu.VMEM((total, width), BF16)]
        + [pltpu.VMEM((total, cols), BF16)] * 4,
        compiler_params=params(24),
        cost_estimate=cost(9),
        name="attention",
    )(*pieces, q, d, w_key, w_value)


def outgoing_kernel(req, enc, gain, out, normed):
    wide = enc[...].astype(F32)
    normed[...] = (wide * rms_scale(wide) * gain[...]).astype(BF16)
    for s in range(out.shape[0]):
        out[s] = normed[jnp.maximum(req[s, 0], 0)]


def run_outgoing(requested, encodings, gain):
    slots = requested.shape[0]
    return pl.pallas_call(
        outgoing_kernel,
        out_shape=jax.ShapeDtypeStruct((slots,) + encodings.shape[1:], BF16),
        in_specs=[smem(), vmem(), vmem()],
        out_specs=vmem(),
        scratch_shapes=[pltpu.VMEM(encodings.shape, BF16)],
        compiler_params=params(12),
        cost_estimate=cost(1.7),
        name="outgoing_rows",
    )(requested, encodings, gain.reshape(1, 1, -1))


def pick_kernel(owner, rows, out, sems):
    copies = []
    for a in range(out.shape[0]):
        cp = pltpu.make_async_copy(rows.at[owner[a]], out.at[a], sems.at[a])
        cp.start()
        copies.append(cp)
    for cp in copies:
        cp.wait()


def run_pick(owner, rows):
    n = owner.shape[0]
    return pl.pallas_call(
        pick_kernel,
        out_shape=jax.ShapeDtypeStruct((n,) + rows.shape[1:], rows.dtype),
        in_specs=[smem(), hbm()],
        out_specs=vmem(),
        scratch_shapes=[pltpu.SemaphoreType.DMA((n,))],
        compiler_params=params(),
        cost_estimate=cost(4.5),
        name="picked_rows",
    )(owner, rows)


def place_kernel(reading, *refs):
    parts, out, total = refs[:-2], refs[-2], refs[-1]
    total[...] = sum(p[...].astype(F32) for p in parts).astype(BF16)
    for s in range(out.shape[0]):
        out[s] = total[reading[s]]


def run_place(reading, parts):
    slots = reading.shape[0]
    shape = parts[0].shape
    return pl.pallas_call(
        place_kernel,
        out_shape=jax.ShapeDtypeStruct((slots,) + shape[1:], BF16),
        in_specs=[smem()] + [vmem()] * len(parts),
        out_specs=vmem(),
        scratch_shapes=[pltpu.VMEM(shape, BF16)],
        compiler_params=params(12),
        cost_estimate=cost(1.7),
        name="placed_grads",
    )(reading, *parts)


def mix_kernel(tok, *refs):
    parts, mixed, squares = refs[:-2], refs[-2], refs[-1]
    summed = sum(p[...].astype(F32) for p in parts)
    out = (tok[...].astype(F32) + summed).astype(BF16)
    mixed[...] = out
    wide = out.astype(F32)
    squares[...] = jnp.sum(wide * wide, axis=1, keepdims=True)


def run_mix(tokens, parts):
    return pl.pallas_call(
        mix_kernel,
        out_shape=(
            jax.ShapeDtypeStruct(tokens.shape, BF16),
            jax.ShapeDtypeStruct((tokens.shape[0], 1), F32),
        ),
        in_specs=[vmem()] * (len(parts) + 1),
        out_specs=(vmem(), vmem()),
        compiler_params=params(12),
        cost_estimate=cost(MIX_COST),
        name="mixed",
    )(tokens, *parts)


def finish_kernel(slot, back, enc, gain, out, buf, sems):
    copies = []
    for j in range(out.shape[0]):
        cp = pltpu.make_async_copy(back.at[slot[j]], buf.at[j], sems.at[j])
        cp.start()
        copies.append(cp)
    wide = enc[...].astype(F32)
    scale = rms_scale(wide)
    hat = wide * scale
    for cp in copies:
        cp.wait()
    up = gain[...] * buf[...].astype(F32)
    out[...] = (scale * (up - hat * jnp.mean(up * hat, axis=-1, keepdims=True))).astype(BF16)


def run_finish(slot, back, encodings, gain):
    rows = encodings.shape[0]
    return pl.pallas_call(
        finish_kernel,
        out_shape=jax.ShapeDtypeStruct(encodings.shape, BF16),
        in_specs=[smem(), hbm(), vmem(), vmem()],
        out_specs=vmem(),
        scratch_shapes=[pltpu.VMEM(encodings.shape, BF16), pltpu.SemaphoreType.DMA((rows,))],
        compiler_params=params(12),
        cost_estimate=cost(1.9),
        name="d_encodings",
    )(slot, back, encodings, gain.reshape(1, 1, -1))


def shards(
    tokens,
    cotangent,
    gain_dec,
    w_query,
    w_out,
    encodings,
    gain_enc,
    w_key,
    w_value,
    gain_post,
    neighbour_ids,
):
    dp_count = lax.axis_size("dp")
    count = lax.axis_size("mp")
    half = count // 2
    share_cols = tokens.shape[1]
    own_rows, own_tokens, width = encodings.shape
    blocks = neighbour_ids.shape[0]
    readings = blocks * neighbour_ids.shape[1]
    here = lax.axis_index("mp")
    steps = jnp.arange(half, dtype=jnp.int32)
    same = (here - 2 * steps) % count
    src = jnp.concatenate([same, same ^ 1]).astype(jnp.int32)

    chosen = neighbour_ids.reshape(readings)
    owner = chosen // own_rows
    local_row = chosen % own_rows
    slots = jnp.arange(dp_count, dtype=jnp.int32)
    matches = owner[:, None] == slots[None, :]
    wanted = jnp.sum(jnp.where(matches, local_row[:, None] + 1, 0), axis=0) - 1
    reading = jnp.sum(
        jnp.where(matches, jnp.arange(readings, dtype=jnp.int32)[:, None], 0), axis=0
    )
    requested = lax.all_to_all(
        jnp.broadcast_to(wanted[:, None], (dp_count, IDS_WIDTH)),
        "dp",
        split_axis=0,
        concat_axis=0,
        tiled=True,
    )
    serves = requested[:, :1] == jnp.arange(own_rows, dtype=jnp.int32)[None, :]
    slot = jnp.sum(jnp.where(serves, slots[:, None], 0), axis=0)

    tok_own = over_chips(tokens, count)
    outgoing = run_outgoing(requested, encodings, gain_enc)
    outgoing, cot_in = lax.optimization_barrier((outgoing, cotangent))
    incoming = lax.all_to_all(outgoing, "dp", split_axis=0, concat_axis=0, tiled=True)
    cot_own = over_chips(cot_in, count)
    q = run_query(src, tok_own + [swap(jnp.stack(tok_own), count)], gain_dec, w_query)
    d = run_back(src, cot_own + [swap(p, count) for p in cot_own], w_out)
    incoming, q, d = lax.optimization_barrier((incoming, q, d))
    picked = run_pick(owner, incoming).reshape(readings * own_tokens, width)
    row_own = over_chips(picked, count)
    rows = row_own + [swap(p, count) for p in row_own]
    send, keep, att = run_attention(rows, q, d, w_key, w_value, blocks)
    pair = pair_sum(keep, swap(send, count))
    att, pair = lax.optimization_barrier((att, pair))
    parts = pair_shares(pair, count)
    b_send, b_keep = run_branch(src, att, w_out, count)
    b_send, parts = lax.optimization_barrier((b_send, parts))
    b_parts = pair_shares(pair_sum(b_keep, swap(b_send, count)), count)
    back_out = run_place(reading, [p.reshape(readings, own_tokens, width) for p in parts])
    back_in = lax.all_to_all(back_out, "dp", split_axis=0, concat_axis=0, tiled=True)

    mixed, squares = run_mix(tokens, b_parts)
    mixed_wide = mixed.astype(F32)
    squares = squares[:, 0]
    squares = squares + swap(squares, count)
    total = squares
    for k in range(1, half):
        total = total + lax.ppermute(squares, "mp", chip_shift(count, k))
    post = lax.rsqrt(total / (share_cols * count) + EPS)[:, None]
    gain_here = lax.dynamic_slice_in_dim(gain_post, here * share_cols, share_cols, 0)
    ffn = (mixed_wide * post * gain_here).astype(BF16)

    d_encodings = run_finish(slot, back_in, encodings, gain_enc)
    return (mixed, ffn, d_encodings)


def solution(mesh):
    in_specs = (
        P("dp", "mp"),
        P("dp", "mp"),
        P(),
        P(None, "mp"),
        P("mp", None),
        P("dp", "mp", None),
        P(),
        P(None, "mp"),
        P(None, "mp"),
        P(),
        P("dp", None),
    )
    out_specs = (P("dp", "mp"), P("dp", "mp"), P("dp", "mp", None))
    return jax.shard_map(shards, mesh=mesh, in_specs=in_specs, out_specs=out_specs, check_vma=False)
```

```python
import jax
import jax.numpy as jnp
from jax import lax
from jax.experimental import pallas as pl
from jax.experimental.pallas import tpu as pltpu
from jax.sharding import PartitionSpec as P

HD = 128
BLOCK = 64
NLEN = 128
NEIGH = 2

EPS = 1e-06
F32 = jnp.float32
BF16 = jnp.bfloat16
IDS_WIDTH = 128
GROUP = 8
MIX_COST = 1
MIB = 1024 * 1024


def rms_scale(values):
    return lax.rsqrt(jnp.mean(values * values, axis=-1, keepdims=True) + EPS)


def params(mib=8):
    return pltpu.CompilerParams(vmem_limit_bytes=mib * MIB)


def cost(micros):
    return pl.CostEstimate(flops=int(micros * 1.1e9), bytes_accessed=0, transcendentals=0)


def vmem():
    return pl.BlockSpec(memory_space=pltpu.VMEM)


def hbm():
    return pl.BlockSpec(memory_space=pltpu.HBM)


def smem():
    return pl.BlockSpec(memory_space=pltpu.SMEM)


def chip_shift(count, k):
    return [(i, (i + 2 * k) % count) for i in range(count)]


def core_swap(count):
    return [(i, i ^ 1) for i in range(count)]


def over_chips(x, count):
    return [x] + [lax.ppermute(x, "mp", chip_shift(count, k)) for k in range(1, count // 2)]


def swap(x, count):
    return lax.ppermute(x, "mp", core_swap(count))


def pair_kernel(keep, other, *outs):
    for k, out in enumerate(outs):
        out[...] = (keep[k].astype(F32) + other[k].astype(F32)).astype(BF16)


def pair_sum(keep, other):
    return pl.pallas_call(
        pair_kernel,
        out_shape=[jax.ShapeDtypeStruct(keep.shape[1:], BF16)] * keep.shape[0],
        in_specs=[vmem(), vmem()],
        out_specs=[vmem()] * keep.shape[0],
        compiler_params=params(12),
        cost_estimate=cost(0.7),
        name="pair_sums",
    )(keep, other)


def pair_shares(pair, count):
    return [pair[0]] + [
        lax.ppermute(pair[k], "mp", chip_shift(count, -k)) for k in range(1, count // 2)
    ]


def shift_matrix(n, lead, transpose):
    r = lax.broadcasted_iota(jnp.int32, (n, n), 0)
    c = lax.broadcasted_iota(jnp.int32, (n, n), 1)
    hit = (r == c + lead) if transpose else (c == r + lead)
    return jnp.where(hit, 1.0, 0.0).astype(BF16)


def dot(a, b):
    return lax.dot_general(a, b, (((1,), (0,)), ((), ())), preferred_element_type=F32)


def dot_nt(a, b):
    return lax.dot_general(a, b, (((1,), (1,)), ((), ())), preferred_element_type=F32)


def dot_tn(a, b):
    return lax.dot_general(a, b, (((0,), (0,)), ((), ())), preferred_element_type=F32)


def views(count, refs):
    half = count // 2
    return list(refs[:half]) + [refs[half].at[k] for k in range(half)], refs[half + 1 :]


def query_kernel(count, src, *refs):
    pieces, rest = views(count, refs)
    gain, w_hbm, out, w_buf, sems = rest
    share = pieces[0].shape[1]
    copies = []
    for k in range(count):
        start = pl.multiple_of(src[k] * share, share)
        cp = pltpu.make_async_copy(w_hbm.at[pl.ds(start, share), :], w_buf.at[k], sems.at[k])
        cp.start()
        copies.append(cp)
    squares = jnp.zeros((pieces[0].shape[0], 1), F32)
    for k in range(count):
        wide = pieces[k][...].astype(F32)
        squares = squares + jnp.sum(wide * wide, axis=1, keepdims=True)
    scale = lax.rsqrt(squares / (share * count) + EPS)
    acc = jnp.zeros(out.shape, F32)
    for k in range(count):
        g = gain[pl.ds(src[k], 1), :]
        normed = (pieces[k][...].astype(F32) * scale * g).astype(BF16)
        copies[k].wait()
        acc = acc + dot(normed, w_buf[k])
    out[...] = dot(shift_matrix(out.shape[0], BLOCK - 1, False), acc.astype(BF16)).astype(BF16)


def run_query(src, pieces, gain, w_query):
    count = 2 * (len(pieces) - 1)
    rows, share = pieces[0].shape
    cols = w_query.shape[1]
    return pl.pallas_call(
        lambda *r: query_kernel(count, *r),
        out_shape=jax.ShapeDtypeStruct((rows, cols), BF16),
        in_specs=[smem()] + [vmem()] * (len(pieces) + 1) + [hbm()],
        out_specs=vmem(),
        scratch_shapes=[pltpu.VMEM((count, share, cols), BF16), pltpu.SemaphoreType.DMA((count,))],
        compiler_params=params(48),
        cost_estimate=cost(4.5),
        name="queries",
    )(src, *pieces, gain.reshape(count, share), w_query)


def back_kernel(count, src, *refs):
    pieces = refs[:count]
    w_hbm, out, w_buf, sems = refs[count:]
    share = pieces[0].shape[1]
    copies = []
    for k in range(count):
        start = pl.multiple_of(src[k] * share, share)
        cp = pltpu.make_async_copy(w_hbm.at[:, pl.ds(start, share)], w_buf.at[k], sems.at[k])
        cp.start()
        copies.append(cp)
    acc = jnp.zeros(out.shape, F32)
    for k in range(count):
        copies[k].wait()
        acc = acc + dot_nt(pieces[k][...], w_buf[k])
    out[...] = dot(shift_matrix(out.shape[0], BLOCK - 1, False), acc.astype(BF16)).astype(BF16)


def run_back(src, pieces, w_out):
    count = len(pieces)
    rows, share = pieces[0].shape
    cols = w_out.shape[0]
    return pl.pallas_call(
        lambda *r: back_kernel(count, *r),
        out_shape=jax.ShapeDtypeStruct((rows, cols), BF16),
        in_specs=[smem()] + [vmem()] * len(pieces) + [hbm()],
        out_specs=vmem(),
        scratch_shapes=[pltpu.VMEM((count, cols, share), BF16), pltpu.SemaphoreType.DMA((count,))],
        compiler_params=params(48),
        cost_estimate=cost(4.5),
        name="d_attended",
    )(src, *pieces, w_out)


def branch_kernel(count, src, att, w_hbm, send, keep, w_buf, sems):
    share = send.shape[2]
    half = count // 2
    copies = []
    order = list(range(half, count)) + list(range(half))
    for k in order:
        start = pl.multiple_of(src[k] * share, share)
        cp = pltpu.make_async_copy(w_hbm.at[:, pl.ds(start, share)], w_buf.at[k], sems.at[k])
        cp.start()
        copies.append(cp)
    a = dot(shift_matrix(att.shape[0], BLOCK - 1, True), att[...]).astype(BF16)
    for k, cp in zip(order, copies):
        cp.wait()
        out = keep.at[k] if k < half else send.at[k - half]
        out[...] = dot(a, w_buf[k]).astype(BF16)


def run_branch(src, att, w_out, count):
    rows, cols = att.shape
    share = w_out.shape[1] // count
    shape = jax.ShapeDtypeStruct((count // 2, rows, share), BF16)
    return pl.pallas_call(
        lambda *r: branch_kernel(count, *r),
        out_shape=(shape, shape),
        in_specs=[smem(), vmem(), hbm()],
        out_specs=(vmem(), vmem()),
        scratch_shapes=[pltpu.VMEM((count, cols, share), BF16), pltpu.SemaphoreType.DMA((count,))],
        compiler_params=params(48),
        cost_estimate=cost(4),
        name="branches",
    )(src, att, w_out)


def attention_kernel(count, blocks, *refs):
    half = count // 2
    pieces = refs[:count]
    q_ref, d_ref, wk, wv, send, keep, att, mem, keys, values, k_grad, v_grad = refs[count:]
    heads = q_ref.shape[1] // HD
    part = send.shape[1] // blocks
    span = part * count
    scale = HD ** (-0.5)

    def rows(b):
        return slice(b * BLOCK, (b + 1) * BLOCK)

    def ctx(b):
        return slice(b * span, (b + 1) * span)

    def cols(h):
        return slice(h * HD, (h + 1) * HD)

    def softmax(scores):
        scores = scores * scale
        lifted = jnp.exp(scores - jnp.max(scores, axis=-1, keepdims=True))
        return lifted / jnp.sum(lifted, axis=-1, keepdims=True)

    def score_grad(p, dp):
        return (p * (dp - jnp.sum(p * dp, axis=-1, keepdims=True)) * scale).astype(BF16)

    for b in range(blocks):
        for k in range(count):
            mem[b * span + k * part : b * span + (k + 1) * part, :] = pieces[k][
                b * part : (b + 1) * part, :
            ]
    keys[...] = dot(mem[...], wk[...]).astype(BF16)
    values[...] = dot(mem[...], wv[...]).astype(BF16)
    every = [(b, h) for b in range(blocks) for h in range(heads)]
    for start in range(0, len(every), GROUP):
        group = every[start : start + GROUP]
        scores = [dot_nt(q_ref[rows(b), cols(h)], keys[ctx(b), cols(h)]) for b, h in group]
        d_probs = [dot_nt(d_ref[rows(b), cols(h)], values[ctx(b), cols(h)]) for b, h in group]
        probs = [softmax(s) for s in scores]
        weights = [p.astype(BF16) for p in probs]
        d_scores = [score_grad(p, dp) for p, dp in zip(probs, d_probs)]
        for w, ds, (b, h) in zip(weights, d_scores, group):
            att[rows(b), cols(h)] = dot(w, values[ctx(b), cols(h)]).astype(BF16)
            v_grad[ctx(b), cols(h)] = dot_tn(w, d_ref[rows(b), cols(h)]).astype(BF16)
            k_grad[ctx(b), cols(h)] = dot_tn(ds, q_ref[rows(b), cols(h)]).astype(BF16)
    for b in range(blocks):
        terms = (dot_nt(k_grad[ctx(b), :], wk[...]) + dot_nt(v_grad[ctx(b), :], wv[...])).astype(
            BF16
        )
        for k in range(count):
            out = keep.at[k] if k < half else send.at[k - half]
            out[b * part : (b + 1) * part, :] = terms[k * part : (k + 1) * part, :]


def run_attention(pieces, q, d, w_key, w_value, blocks):
    count = len(pieces)
    rows, width = pieces[0].shape
    cols = q.shape[1]
    total = rows * count
    shape = jax.ShapeDtypeStruct((count // 2, rows, width), BF16)
    return pl.pallas_call(
        lambda *r: attention_kernel(count, blocks, *r),
        out_shape=(shape, shape, jax.ShapeDtypeStruct((blocks * BLOCK, cols), BF16)),
        in_specs=[vmem()] * (len(pieces) + 4),
        out_specs=(vmem(), vmem(), vmem()),
        scratch_shapes=[pltpu.VMEM((total, width), BF16)]
        + [pltpu.VMEM((total, cols), BF16)] * 4,
        compiler_params=params(24),
        cost_estimate=cost(9),
        name="attention",
    )(*pieces, q, d, w_key, w_value)


def outgoing_kernel(req, enc, gain, out, normed):
    wide = enc[...].astype(F32)
    normed[...] = (wide * rms_scale(wide) * gain[...]).astype(BF16)
    for s in range(out.shape[0]):
        out[s] = normed[jnp.maximum(req[s, 0], 0)]


def run_outgoing(requested, encodings, gain):
    slots = requested.shape[0]
    return pl.pallas_call(
        outgoing_kernel,
        out_shape=jax.ShapeDtypeStruct((slots,) + encodings.shape[1:], BF16),
        in_specs=[smem(), vmem(), vmem()],
        out_specs=vmem(),
        scratch_shapes=[pltpu.VMEM(encodings.shape, BF16)],
        compiler_params=params(12),
        cost_estimate=cost(1.7),
        name="outgoing_rows",
    )(requested, encodings, gain.reshape(1, 1, -1))


def pick_kernel(owner, rows, out, sems):
    copies = []
    for a in range(out.shape[0]):
        cp = pltpu.make_async_copy(rows.at[owner[a]], out.at[a], sems.at[a])
        cp.start()
        copies.append(cp)
    for cp in copies:
        cp.wait()


def run_pick(owner, rows):
    n = owner.shape[0]
    return pl.pallas_call(
        pick_kernel,
        out_shape=jax.ShapeDtypeStruct((n,) + rows.shape[1:], rows.dtype),
        in_specs=[smem(), hbm()],
        out_specs=vmem(),
        scratch_shapes=[pltpu.SemaphoreType.DMA((n,))],
        compiler_params=params(),
        cost_estimate=cost(4.5),
        name="picked_rows",
    )(owner, rows)


def place_kernel(reading, *refs):
    parts, out, total = refs[:-2], refs[-2], refs[-1]
    total[...] = sum(p[...].astype(F32) for p in parts).astype(BF16)
    for s in range(out.shape[0]):
        out[s] = total[reading[s]]


def run_place(reading, parts):
    slots = reading.shape[0]
    shape = parts[0].shape
    return pl.pallas_call(
        place_kernel,
        out_shape=jax.ShapeDtypeStruct((slots,) + shape[1:], BF16),
        in_specs=[smem()] + [vmem()] * len(parts),
        out_specs=vmem(),
        scratch_shapes=[pltpu.VMEM(shape, BF16)],
        compiler_params=params(12),
        cost_estimate=cost(1.7),
        name="placed_grads",
    )(reading, *parts)


def mix_kernel(tok, *refs):
    parts, mixed, squares = refs[:-2], refs[-2], refs[-1]
    summed = sum(p[...].astype(F32) for p in parts)
    out = (tok[...].astype(F32) + summed).astype(BF16)
    mixed[...] = out
    wide = out.astype(F32)
    squares[...] = jnp.sum(wide * wide, axis=1, keepdims=True)


def run_mix(tokens, parts):
    return pl.pallas_call(
        mix_kernel,
        out_shape=(
            jax.ShapeDtypeStruct(tokens.shape, BF16),
            jax.ShapeDtypeStruct((tokens.shape[0], 1), F32),
        ),
        in_specs=[vmem()] * (len(parts) + 1),
        out_specs=(vmem(), vmem()),
        compiler_params=params(12),
        cost_estimate=cost(MIX_COST),
        name="mixed",
    )(tokens, *parts)


def finish_kernel(slot, back, enc, gain, out, buf, sems):
    copies = []
    for j in range(out.shape[0]):
        cp = pltpu.make_async_copy(back.at[slot[j]], buf.at[j], sems.at[j])
        cp.start()
        copies.append(cp)
    wide = enc[...].astype(F32)
    scale = rms_scale(wide)
    hat = wide * scale
    for cp in copies:
        cp.wait()
    up = gain[...] * buf[...].astype(F32)
    out[...] = (scale * (up - hat * jnp.mean(up * hat, axis=-1, keepdims=True))).astype(BF16)


def run_finish(slot, back, encodings, gain):
    rows = encodings.shape[0]
    return pl.pallas_call(
        finish_kernel,
        out_shape=jax.ShapeDtypeStruct(encodings.shape, BF16),
        in_specs=[smem(), hbm(), vmem(), vmem()],
        out_specs=vmem(),
        scratch_shapes=[pltpu.VMEM(encodings.shape, BF16), pltpu.SemaphoreType.DMA((rows,))],
        compiler_params=params(12),
        cost_estimate=cost(1.9),
        name="d_encodings",
    )(slot, back, encodings, gain.reshape(1, 1, -1))


def shards(
    tokens,
    cotangent,
    gain_dec,
    w_query,
    w_out,
    encodings,
    gain_enc,
    w_key,
    w_value,
    gain_post,
    neighbour_ids,
):
    dp_count = lax.axis_size("dp")
    count = lax.axis_size("mp")
    half = count // 2
    share_cols = tokens.shape[1]
    own_rows, own_tokens, width = encodings.shape
    blocks = neighbour_ids.shape[0]
    readings = blocks * neighbour_ids.shape[1]
    here = lax.axis_index("mp")
    steps = jnp.arange(half, dtype=jnp.int32)
    same = (here - 2 * steps) % count
    src = jnp.concatenate([same, same ^ 1]).astype(jnp.int32)

    chosen = neighbour_ids.reshape(readings)
    owner = chosen // own_rows
    local_row = chosen % own_rows
    slots = jnp.arange(dp_count, dtype=jnp.int32)
    matches = owner[:, None] == slots[None, :]
    wanted = jnp.sum(jnp.where(matches, local_row[:, None] + 1, 0), axis=0) - 1
    reading = jnp.sum(
        jnp.where(matches, jnp.arange(readings, dtype=jnp.int32)[:, None], 0), axis=0
    )
    requested = lax.all_to_all(
        jnp.broadcast_to(wanted[:, None], (dp_count, IDS_WIDTH)),
        "dp",
        split_axis=0,
        concat_axis=0,
        tiled=True,
    )
    serves = requested[:, :1] == jnp.arange(own_rows, dtype=jnp.int32)[None, :]
    slot = jnp.sum(jnp.where(serves, slots[:, None], 0), axis=0)

    tok_own = over_chips(tokens, count)
    outgoing = run_outgoing(requested, encodings, gain_enc)
    outgoing, cot_in = lax.optimization_barrier((outgoing, cotangent))
    incoming = lax.all_to_all(outgoing, "dp", split_axis=0, concat_axis=0, tiled=True)
    cot_own = over_chips(cot_in, count)
    q = run_query(src, tok_own + [swap(jnp.stack(tok_own), count)], gain_dec, w_query)
    cot_own, q = lax.optimization_barrier((cot_own, q))
    d = run_back(src, cot_own + [swap(p, count) for p in cot_own], w_out)
    picked = run_pick(owner, incoming).reshape(readings * own_tokens, width)
    row_own = over_chips(picked, count)
    rows = row_own + [swap(p, count) for p in row_own]
    send, keep, att = run_attention(rows, q, d, w_key, w_value, blocks)
    pair = pair_sum(keep, swap(send, count))
    att, pair = lax.optimization_barrier((att, pair))
    parts = pair_shares(pair, count)
    b_send, b_keep = run_branch(src, att, w_out, count)
    b_send, parts = lax.optimization_barrier((b_send, parts))
    b_parts = pair_shares(pair_sum(b_keep, swap(b_send, count)), count)
    back_out = run_place(reading, [p.reshape(readings, own_tokens, width) for p in parts])
    back_in = lax.all_to_all(back_out, "dp", split_axis=0, concat_axis=0, tiled=True)

    mixed, squares = run_mix(tokens, b_parts)
    mixed_wide = mixed.astype(F32)
    squares = squares[:, 0]
    squares = squares + swap(squares, count)
    total = squares
    for k in range(1, half):
        total = total + lax.ppermute(squares, "mp", chip_shift(count, k))
    d_encodings = run_finish(slot, back_in, encodings, gain_enc)
    total, d_encodings = lax.optimization_barrier((total, d_encodings))
    post = lax.rsqrt(total / (share_cols * count) + EPS)[:, None]
    gain_here = lax.dynamic_slice_in_dim(gain_post, here * share_cols, share_cols, 0)
    ffn = (mixed_wide * post * gain_here).astype(BF16)
    return (mixed, ffn, d_encodings)


def solution(mesh):
    in_specs = (
        P("dp", "mp"),
        P("dp", "mp"),
        P(),
        P(None, "mp"),
        P("mp", None),
        P("dp", "mp", None),
        P(),
        P(None, "mp"),
        P(None, "mp"),
        P(),
        P("dp", None),
    )
    out_specs = (P("dp", "mp"), P("dp", "mp"), P("dp", "mp", None))
    return jax.shard_map(shards, mesh=mesh, in_specs=in_specs, out_specs=out_specs, check_vma=False)
```

```python
import jax
import jax.numpy as jnp
from jax import lax
from jax.experimental import pallas as pl
from jax.experimental.pallas import tpu as pltpu
from jax.sharding import PartitionSpec as P

HD = 128
BLOCK = 64
NLEN = 128
NEIGH = 2

EPS = 1e-06
F32 = jnp.float32
BF16 = jnp.bfloat16
IDS_WIDTH = 128
GROUP = 8
MIX_COST = 1
MIB = 1024 * 1024


def rms_scale(values):
    return lax.rsqrt(jnp.mean(values * values, axis=-1, keepdims=True) + EPS)


def params(mib=8):
    return pltpu.CompilerParams(vmem_limit_bytes=mib * MIB)


def cost(micros):
    return pl.CostEstimate(flops=int(micros * 1.1e9), bytes_accessed=0, transcendentals=0)


def vmem():
    return pl.BlockSpec(memory_space=pltpu.VMEM)


def hbm():
    return pl.BlockSpec(memory_space=pltpu.HBM)


def smem():
    return pl.BlockSpec(memory_space=pltpu.SMEM)


def chip_shift(count, k):
    return [(i, (i + 2 * k) % count) for i in range(count)]


def core_swap(count):
    return [(i, i ^ 1) for i in range(count)]


def over_chips(x, count):
    return [x] + [lax.ppermute(x, "mp", chip_shift(count, k)) for k in range(1, count // 2)]


def swap(x, count):
    return lax.ppermute(x, "mp", core_swap(count))


def pair_kernel(keep, other, *outs):
    for k, out in enumerate(outs):
        out[...] = (keep[k].astype(F32) + other[k].astype(F32)).astype(BF16)


def pair_sum(keep, other):
    return pl.pallas_call(
        pair_kernel,
        out_shape=[jax.ShapeDtypeStruct(keep.shape[1:], BF16)] * keep.shape[0],
        in_specs=[vmem(), vmem()],
        out_specs=[vmem()] * keep.shape[0],
        compiler_params=params(12),
        cost_estimate=cost(0.7),
        name="pair_sums",
    )(keep, other)


def pair_shares(pair, count):
    return [pair[0]] + [
        lax.ppermute(pair[k], "mp", chip_shift(count, -k)) for k in range(1, count // 2)
    ]


def shift_matrix(n, lead, transpose):
    r = lax.broadcasted_iota(jnp.int32, (n, n), 0)
    c = lax.broadcasted_iota(jnp.int32, (n, n), 1)
    hit = (r == c + lead) if transpose else (c == r + lead)
    return jnp.where(hit, 1.0, 0.0).astype(BF16)


def dot(a, b):
    return lax.dot_general(a, b, (((1,), (0,)), ((), ())), preferred_element_type=F32)


def dot_nt(a, b):
    return lax.dot_general(a, b, (((1,), (1,)), ((), ())), preferred_element_type=F32)


def dot_tn(a, b):
    return lax.dot_general(a, b, (((0,), (0,)), ((), ())), preferred_element_type=F32)


def views(count, refs):
    half = count // 2
    return list(refs[:half]) + [refs[half].at[k] for k in range(half)], refs[half + 1 :]


def query_kernel(count, src, *refs):
    pieces, rest = views(count, refs)
    gain, w_hbm, out, w_buf, sems = rest
    share = pieces[0].shape[1]
    copies = []
    for k in range(count):
        start = pl.multiple_of(src[k] * share, share)
        cp = pltpu.make_async_copy(w_hbm.at[pl.ds(start, share), :], w_buf.at[k], sems.at[k])
        cp.start()
        copies.append(cp)
    squares = jnp.zeros((pieces[0].shape[0], 1), F32)
    for k in range(count):
        wide = pieces[k][...].astype(F32)
        squares = squares + jnp.sum(wide * wide, axis=1, keepdims=True)
    scale = lax.rsqrt(squares / (share * count) + EPS)
    acc = jnp.zeros(out.shape, F32)
    for k in range(count):
        g = gain[pl.ds(src[k], 1), :]
        normed = (pieces[k][...].astype(F32) * scale * g).astype(BF16)
        copies[k].wait()
        acc = acc + dot(normed, w_buf[k])
    out[...] = dot(shift_matrix(out.shape[0], BLOCK - 1, False), acc.astype(BF16)).astype(BF16)


def run_query(src, pieces, gain, w_query):
    count = 2 * (len(pieces) - 1)
    rows, share = pieces[0].shape
    cols = w_query.shape[1]
    return pl.pallas_call(
        lambda *r: query_kernel(count, *r),
        out_shape=jax.ShapeDtypeStruct((rows, cols), BF16),
        in_specs=[smem()] + [vmem()] * (len(pieces) + 1) + [hbm()],
        out_specs=vmem(),
        scratch_shapes=[pltpu.VMEM((count, share, cols), BF16), pltpu.SemaphoreType.DMA((count,))],
        compiler_params=params(48),
        cost_estimate=cost(3.4),
        name="queries",
    )(src, *pieces, gain.reshape(count, share), w_query)


def back_kernel(count, src, *refs):
    pieces = refs[:count]
    w_hbm, out, w_buf, sems = refs[count:]
    share = pieces[0].shape[1]
    copies = []
    for k in range(count):
        start = pl.multiple_of(src[k] * share, share)
        cp = pltpu.make_async_copy(w_hbm.at[:, pl.ds(start, share)], w_buf.at[k], sems.at[k])
        cp.start()
        copies.append(cp)
    acc = jnp.zeros(out.shape, F32)
    for k in range(count):
        copies[k].wait()
        acc = acc + dot_nt(pieces[k][...], w_buf[k])
    out[...] = dot(shift_matrix(out.shape[0], BLOCK - 1, False), acc.astype(BF16)).astype(BF16)


def run_back(src, pieces, w_out):
    count = len(pieces)
    rows, share = pieces[0].shape
    cols = w_out.shape[0]
    return pl.pallas_call(
        lambda *r: back_kernel(count, *r),
        out_shape=jax.ShapeDtypeStruct((rows, cols), BF16),
        in_specs=[smem()] + [vmem()] * len(pieces) + [hbm()],
        out_specs=vmem(),
        scratch_shapes=[pltpu.VMEM((count, cols, share), BF16), pltpu.SemaphoreType.DMA((count,))],
        compiler_params=params(48),
        cost_estimate=cost(3.4),
        name="d_attended",
    )(src, *pieces, w_out)


def branch_kernel(count, src, att, w_hbm, send, keep, w_buf, sems):
    share = send.shape[2]
    half = count // 2
    copies = []
    order = list(range(half, count)) + list(range(half))
    for k in order:
        start = pl.multiple_of(src[k] * share, share)
        cp = pltpu.make_async_copy(w_hbm.at[:, pl.ds(start, share)], w_buf.at[k], sems.at[k])
        cp.start()
        copies.append(cp)
    a = dot(shift_matrix(att.shape[0], BLOCK - 1, True), att[...]).astype(BF16)
    for k, cp in zip(order, copies):
        cp.wait()
        out = keep.at[k] if k < half else send.at[k - half]
        out[...] = dot(a, w_buf[k]).astype(BF16)


def run_branch(src, att, w_out, count):
    rows, cols = att.shape
    share = w_out.shape[1] // count
    shape = jax.ShapeDtypeStruct((count // 2, rows, share), BF16)
    return pl.pallas_call(
        lambda *r: branch_kernel(count, *r),
        out_shape=(shape, shape),
        in_specs=[smem(), vmem(), hbm()],
        out_specs=(vmem(), vmem()),
        scratch_shapes=[pltpu.VMEM((count, cols, share), BF16), pltpu.SemaphoreType.DMA((count,))],
        compiler_params=params(48),
        cost_estimate=cost(4),
        name="branches",
    )(src, att, w_out)


def attention_kernel(count, blocks, *refs):
    half = count // 2
    pieces = refs[:count]
    q_ref, d_ref, wk, wv, send, keep, att, mem, keys, values, k_grad, v_grad = refs[count:]
    heads = q_ref.shape[1] // HD
    part = send.shape[1] // blocks
    span = part * count
    scale = HD ** (-0.5)

    def rows(b):
        return slice(b * BLOCK, (b + 1) * BLOCK)

    def ctx(b):
        return slice(b * span, (b + 1) * span)

    def cols(h):
        return slice(h * HD, (h + 1) * HD)

    def softmax(scores):
        scores = scores * scale
        lifted = jnp.exp(scores - jnp.max(scores, axis=-1, keepdims=True))
        return lifted / jnp.sum(lifted, axis=-1, keepdims=True)

    def score_grad(p, dp):
        return (p * (dp - jnp.sum(p * dp, axis=-1, keepdims=True)) * scale).astype(BF16)

    for b in range(blocks):
        for k in range(count):
            mem[b * span + k * part : b * span + (k + 1) * part, :] = pieces[k][
                b * part : (b + 1) * part, :
            ]
    keys[...] = dot(mem[...], wk[...]).astype(BF16)
    values[...] = dot(mem[...], wv[...]).astype(BF16)
    every = [(b, h) for b in range(blocks) for h in range(heads)]
    for start in range(0, len(every), GROUP):
        group = every[start : start + GROUP]
        scores = [dot_nt(q_ref[rows(b), cols(h)], keys[ctx(b), cols(h)]) for b, h in group]
        d_probs = [dot_nt(d_ref[rows(b), cols(h)], values[ctx(b), cols(h)]) for b, h in group]
        probs = [softmax(s) for s in scores]
        weights = [p.astype(BF16) for p in probs]
        d_scores = [score_grad(p, dp) for p, dp in zip(probs, d_probs)]
        for w, ds, (b, h) in zip(weights, d_scores, group):
            att[rows(b), cols(h)] = dot(w, values[ctx(b), cols(h)]).astype(BF16)
            v_grad[ctx(b), cols(h)] = dot_tn(w, d_ref[rows(b), cols(h)]).astype(BF16)
            k_grad[ctx(b), cols(h)] = dot_tn(ds, q_ref[rows(b), cols(h)]).astype(BF16)
    for b in range(blocks):
        terms = (dot_nt(k_grad[ctx(b), :], wk[...]) + dot_nt(v_grad[ctx(b), :], wv[...])).astype(
            BF16
        )
        for k in range(count):
            out = keep.at[k] if k < half else send.at[k - half]
            out[b * part : (b + 1) * part, :] = terms[k * part : (k + 1) * part, :]


def run_attention(pieces, q, d, w_key, w_value, blocks):
    count = len(pieces)
    rows, width = pieces[0].shape
    cols = q.shape[1]
    total = rows * count
    shape = jax.ShapeDtypeStruct((count // 2, rows, width), BF16)
    return pl.pallas_call(
        lambda *r: attention_kernel(count, blocks, *r),
        out_shape=(shape, shape, jax.ShapeDtypeStruct((blocks * BLOCK, cols), BF16)),
        in_specs=[vmem()] * (len(pieces) + 4),
        out_specs=(vmem(), vmem(), vmem()),
        scratch_shapes=[pltpu.VMEM((total, width), BF16)]
        + [pltpu.VMEM((total, cols), BF16)] * 4,
        compiler_params=params(24),
        cost_estimate=cost(9),
        name="attention",
    )(*pieces, q, d, w_key, w_value)


def normed_kernel(enc, gain, out):
    wide = enc[...].astype(F32)
    out[...] = (wide * rms_scale(wide) * gain[...]).astype(BF16)


def run_normed(encodings, gain):
    return pl.pallas_call(
        normed_kernel,
        out_shape=jax.ShapeDtypeStruct(encodings.shape, BF16),
        in_specs=[vmem(), vmem()],
        out_specs=vmem(),
        compiler_params=params(8),
        cost_estimate=cost(0.1),
        name="normed_rows",
    )(encodings, gain.reshape(1, 1, -1))


def outgoing_kernel(req, normed, out):
    for s in range(out.shape[0]):
        out[s] = normed[jnp.maximum(req[s, 0], 0)]


def run_outgoing(requested, normed):
    slots = requested.shape[0]
    return pl.pallas_call(
        outgoing_kernel,
        out_shape=jax.ShapeDtypeStruct((slots,) + normed.shape[1:], BF16),
        in_specs=[smem(), vmem()],
        out_specs=vmem(),
        compiler_params=params(8),
        cost_estimate=cost(0.1),
        name="outgoing_rows",
    )(requested, normed)


def pick_kernel(owner, rows, out, sems):
    copies = []
    for a in range(out.shape[0]):
        cp = pltpu.make_async_copy(rows.at[owner[a]], out.at[a], sems.at[a])
        cp.start()
        copies.append(cp)
    for cp in copies:
        cp.wait()


def run_pick(owner, rows):
    n = owner.shape[0]
    return pl.pallas_call(
        pick_kernel,
        out_shape=jax.ShapeDtypeStruct((n,) + rows.shape[1:], rows.dtype),
        in_specs=[smem(), hbm()],
        out_specs=vmem(),
        scratch_shapes=[pltpu.SemaphoreType.DMA((n,))],
        compiler_params=params(),
        cost_estimate=cost(3.4),
        name="picked_rows",
    )(owner, rows)


def place_kernel(reading, *refs):
    parts, out, total = refs[:-2], refs[-2], refs[-1]
    total[...] = sum(p[...].astype(F32) for p in parts).astype(BF16)
    for s in range(out.shape[0]):
        out[s] = total[reading[s]]


def run_place(reading, parts):
    slots = reading.shape[0]
    shape = parts[0].shape
    return pl.pallas_call(
        place_kernel,
        out_shape=jax.ShapeDtypeStruct((slots,) + shape[1:], BF16),
        in_specs=[smem()] + [vmem()] * len(parts),
        out_specs=vmem(),
        scratch_shapes=[pltpu.VMEM(shape, BF16)],
        compiler_params=params(12),
        cost_estimate=cost(1.7),
        name="placed_grads",
    )(reading, *parts)


def mix_kernel(tok, *refs):
    parts, mixed, squares = refs[:-2], refs[-2], refs[-1]
    summed = sum(p[...].astype(F32) for p in parts)
    out = (tok[...].astype(F32) + summed).astype(BF16)
    mixed[...] = out
    wide = out.astype(F32)
    squares[...] = jnp.sum(wide * wide, axis=1, keepdims=True)


def run_mix(tokens, parts):
    return pl.pallas_call(
        mix_kernel,
        out_shape=(
            jax.ShapeDtypeStruct(tokens.shape, BF16),
            jax.ShapeDtypeStruct((tokens.shape[0], 1), F32),
        ),
        in_specs=[vmem()] * (len(parts) + 1),
        out_specs=(vmem(), vmem()),
        compiler_params=params(12),
        cost_estimate=cost(MIX_COST),
        name="mixed",
    )(tokens, *parts)


def finish_kernel(slot, back, enc, gain, out, buf, sems):
    copies = []
    for j in range(out.shape[0]):
        cp = pltpu.make_async_copy(back.at[slot[j]], buf.at[j], sems.at[j])
        cp.start()
        copies.append(cp)
    wide = enc[...].astype(F32)
    scale = rms_scale(wide)
    hat = wide * scale
    for cp in copies:
        cp.wait()
    up = gain[...] * buf[...].astype(F32)
    out[...] = (scale * (up - hat * jnp.mean(up * hat, axis=-1, keepdims=True))).astype(BF16)


def run_finish(slot, back, encodings, gain):
    rows = encodings.shape[0]
    return pl.pallas_call(
        finish_kernel,
        out_shape=jax.ShapeDtypeStruct(encodings.shape, BF16),
        in_specs=[smem(), hbm(), vmem(), vmem()],
        out_specs=vmem(),
        scratch_shapes=[pltpu.VMEM(encodings.shape, BF16), pltpu.SemaphoreType.DMA((rows,))],
        compiler_params=params(12),
        cost_estimate=cost(1.9),
        name="d_encodings",
    )(slot, back, encodings, gain.reshape(1, 1, -1))


def shards(
    tokens,
    cotangent,
    gain_dec,
    w_query,
    w_out,
    encodings,
    gain_enc,
    w_key,
    w_value,
    gain_post,
    neighbour_ids,
):
    dp_count = lax.axis_size("dp")
    count = lax.axis_size("mp")
    half = count // 2
    share_cols = tokens.shape[1]
    own_rows, own_tokens, width = encodings.shape
    blocks = neighbour_ids.shape[0]
    readings = blocks * neighbour_ids.shape[1]
    here = lax.axis_index("mp")
    steps = jnp.arange(half, dtype=jnp.int32)
    same = (here - 2 * steps) % count
    src = jnp.concatenate([same, same ^ 1]).astype(jnp.int32)

    chosen = neighbour_ids.reshape(readings)
    owner = chosen // own_rows
    local_row = chosen % own_rows
    slots = jnp.arange(dp_count, dtype=jnp.int32)
    matches = owner[:, None] == slots[None, :]
    wanted = jnp.sum(jnp.where(matches, local_row[:, None] + 1, 0), axis=0) - 1
    reading = jnp.sum(
        jnp.where(matches, jnp.arange(readings, dtype=jnp.int32)[:, None], 0), axis=0
    )
    requested = lax.all_to_all(
        jnp.broadcast_to(wanted[:, None], (dp_count, IDS_WIDTH)),
        "dp",
        split_axis=0,
        concat_axis=0,
        tiled=True,
    )
    serves = requested[:, :1] == jnp.arange(own_rows, dtype=jnp.int32)[None, :]
    slot = jnp.sum(jnp.where(serves, slots[:, None], 0), axis=0)

    tok_own = over_chips(tokens, count)
    outgoing = run_outgoing(requested, run_normed(encodings, gain_enc))
    outgoing, cot_in = lax.optimization_barrier((outgoing, cotangent))
    incoming = lax.all_to_all(outgoing, "dp", split_axis=0, concat_axis=0, tiled=True)
    cot_own = over_chips(cot_in, count)
    q = run_query(src, tok_own + [swap(jnp.stack(tok_own), count)], gain_dec, w_query)
    cot_own, q = lax.optimization_barrier((cot_own, q))
    d = run_back(src, cot_own + [swap(p, count) for p in cot_own], w_out)
    picked = run_pick(owner, incoming).reshape(readings * own_tokens, width)
    row_own = over_chips(picked, count)
    crossed, d = lax.optimization_barrier((row_own[1:], d))
    row_own = [picked] + crossed
    rows = row_own + [swap(p, count) for p in row_own]
    send, keep, att = run_attention(rows, q, d, w_key, w_value, blocks)
    pair = pair_sum(keep, swap(send, count))
    att, pair = lax.optimization_barrier((att, pair))
    parts = pair_shares(pair, count)
    b_send, b_keep = run_branch(src, att, w_out, count)
    b_send, parts = lax.optimization_barrier((b_send, parts))
    b_parts = pair_shares(pair_sum(b_keep, swap(b_send, count)), count)
    back_out = run_place(reading, [p.reshape(readings, own_tokens, width) for p in parts])
    back_in = lax.all_to_all(back_out, "dp", split_axis=0, concat_axis=0, tiled=True)

    mixed, squares = run_mix(tokens, b_parts)
    mixed_wide = mixed.astype(F32)
    squares = squares[:, 0]
    squares = squares + swap(squares, count)
    total = squares
    for k in range(1, half):
        total = total + lax.ppermute(squares, "mp", chip_shift(count, k))
    d_encodings = run_finish(slot, back_in, encodings, gain_enc)
    total, d_encodings = lax.optimization_barrier((total, d_encodings))
    post = lax.rsqrt(total / (share_cols * count) + EPS)[:, None]
    gain_here = lax.dynamic_slice_in_dim(gain_post, here * share_cols, share_cols, 0)
    ffn = (mixed_wide * post * gain_here).astype(BF16)
    return (mixed, ffn, d_encodings)


def solution(mesh):
    in_specs = (
        P("dp", "mp"),
        P("dp", "mp"),
        P(),
        P(None, "mp"),
        P("mp", None),
        P("dp", "mp", None),
        P(),
        P(None, "mp"),
        P(None, "mp"),
        P(),
        P("dp", None),
    )
    out_specs = (P("dp", "mp"), P("dp", "mp"), P("dp", "mp", None))
    return jax.shard_map(shards, mesh=mesh, in_specs=in_specs, out_specs=out_specs, check_vma=False)
```

```python
import jax
import jax.numpy as jnp
from jax import lax
from jax.experimental import pallas as pl
from jax.experimental.pallas import tpu as pltpu
from jax.sharding import PartitionSpec as P

HD = 128
BLOCK = 64
NLEN = 128
NEIGH = 2

EPS = 1e-06
F32 = jnp.float32
BF16 = jnp.bfloat16
IDS_WIDTH = 128
GROUP = 8
MIX_COST = 5
MIB = 1024 * 1024


def rms_scale(values):
    return lax.rsqrt(jnp.mean(values * values, axis=-1, keepdims=True) + EPS)


def params(mib=8):
    return pltpu.CompilerParams(vmem_limit_bytes=mib * MIB)


def cost(micros):
    return pl.CostEstimate(flops=int(micros * 1.1e9), bytes_accessed=0, transcendentals=0)


def vmem():
    return pl.BlockSpec(memory_space=pltpu.VMEM)


def hbm():
    return pl.BlockSpec(memory_space=pltpu.HBM)


def smem():
    return pl.BlockSpec(memory_space=pltpu.SMEM)


def chip_shift(count, k):
    return [(i, (i + 2 * k) % count) for i in range(count)]


def chip_flip(count, flip):
    return [(i, i ^ (2 * flip)) for i in range(count)]


def core_swap(count):
    return [(i, i ^ 1) for i in range(count)]


def over_chips(x, count):
    return [x] + [lax.ppermute(x, "mp", chip_shift(count, k)) for k in range(1, count // 2)]


def swap(x, count):
    return lax.ppermute(x, "mp", core_swap(count))


def pair_kernel(keep, other, *outs):
    for k, out in enumerate(outs):
        out[...] = (keep[k].astype(F32) + other[k].astype(F32)).astype(BF16)


def pair_sum(keep, other):
    return pl.pallas_call(
        pair_kernel,
        out_shape=[jax.ShapeDtypeStruct(keep.shape[1:], BF16)] * keep.shape[0],
        in_specs=[vmem(), vmem()],
        out_specs=[vmem()] * keep.shape[0],
        compiler_params=params(12),
        cost_estimate=cost(0.7),
        name="pair_sums",
    )(keep, other)


def pair_shares(pair, count):
    return [pair[0]] + [
        lax.ppermute(pair[k], "mp", chip_shift(count, -k)) for k in range(1, count // 2)
    ]


def shift_matrix(n, lead, transpose):
    r = lax.broadcasted_iota(jnp.int32, (n, n), 0)
    c = lax.broadcasted_iota(jnp.int32, (n, n), 1)
    hit = (r == c + lead) if transpose else (c == r + lead)
    return jnp.where(hit, 1.0, 0.0).astype(BF16)


def dot(a, b):
    return lax.dot_general(a, b, (((1,), (0,)), ((), ())), preferred_element_type=F32)


def dot_nt(a, b):
    return lax.dot_general(a, b, (((1,), (1,)), ((), ())), preferred_element_type=F32)


def dot_tn(a, b):
    return lax.dot_general(a, b, (((0,), (0,)), ((), ())), preferred_element_type=F32)


def views(count, refs):
    half = count // 2
    return list(refs[:half]) + [refs[half].at[k] for k in range(half)], refs[half + 1 :]


def query_kernel(count, src, *refs):
    pieces, rest = views(count, refs)
    gain, w_hbm, out, w_buf, sems = rest
    share = pieces[0].shape[1]
    copies = []
    for k in range(count):
        start = pl.multiple_of(src[k] * share, share)
        cp = pltpu.make_async_copy(w_hbm.at[pl.ds(start, share), :], w_buf.at[k], sems.at[k])
        cp.start()
        copies.append(cp)
    squares = jnp.zeros((pieces[0].shape[0], 1), F32)
    for k in range(count):
        wide = pieces[k][...].astype(F32)
        squares = squares + jnp.sum(wide * wide, axis=1, keepdims=True)
    scale = lax.rsqrt(squares / (share * count) + EPS)
    acc = jnp.zeros(out.shape, F32)
    for k in range(count):
        g = gain[pl.ds(src[k], 1), :]
        normed = (pieces[k][...].astype(F32) * scale * g).astype(BF16)
        copies[k].wait()
        acc = acc + dot(normed, w_buf[k])
    out[...] = dot(shift_matrix(out.shape[0], BLOCK - 1, False), acc.astype(BF16)).astype(BF16)


def run_query(src, pieces, gain, w_query):
    count = 2 * (len(pieces) - 1)
    rows, share = pieces[0].shape
    cols = w_query.shape[1]
    return pl.pallas_call(
        lambda *r: query_kernel(count, *r),
        out_shape=jax.ShapeDtypeStruct((rows, cols), BF16),
        in_specs=[smem()] + [vmem()] * (len(pieces) + 1) + [hbm()],
        out_specs=vmem(),
        scratch_shapes=[pltpu.VMEM((count, share, cols), BF16), pltpu.SemaphoreType.DMA((count,))],
        compiler_params=params(48),
        cost_estimate=cost(3.4),
        name="queries",
    )(src, *pieces, gain.reshape(count, share), w_query)


def back_kernel(count, src, *refs):
    pieces = refs[:count]
    w_hbm, out, w_buf, sems = refs[count:]
    share = pieces[0].shape[1]
    copies = []
    for k in range(count):
        start = pl.multiple_of(src[k] * share, share)
        cp = pltpu.make_async_copy(w_hbm.at[:, pl.ds(start, share)], w_buf.at[k], sems.at[k])
        cp.start()
        copies.append(cp)
    acc = jnp.zeros(out.shape, F32)
    for k in range(count):
        copies[k].wait()
        acc = acc + dot_nt(pieces[k][...], w_buf[k])
    out[...] = dot(shift_matrix(out.shape[0], BLOCK - 1, False), acc.astype(BF16)).astype(BF16)


def run_back(src, pieces, w_out):
    count = len(pieces)
    rows, share = pieces[0].shape
    cols = w_out.shape[0]
    return pl.pallas_call(
        lambda *r: back_kernel(count, *r),
        out_shape=jax.ShapeDtypeStruct((rows, cols), BF16),
        in_specs=[smem()] + [vmem()] * len(pieces) + [hbm()],
        out_specs=vmem(),
        scratch_shapes=[pltpu.VMEM((count, cols, share), BF16), pltpu.SemaphoreType.DMA((count,))],
        compiler_params=params(48),
        cost_estimate=cost(3.4),
        name="d_attended",
    )(src, *pieces, w_out)


def branch_kernel(count, src, att, w_hbm, send, keep, w_buf, sems):
    share = send.shape[2]
    half = count // 2
    copies = []
    order = list(range(half, count)) + list(range(half))
    for k in order:
        start = pl.multiple_of(src[k] * share, share)
        cp = pltpu.make_async_copy(w_hbm.at[:, pl.ds(start, share)], w_buf.at[k], sems.at[k])
        cp.start()
        copies.append(cp)
    a = dot(shift_matrix(att.shape[0], BLOCK - 1, True), att[...]).astype(BF16)
    for k, cp in zip(order, copies):
        cp.wait()
        out = keep.at[k] if k < half else send.at[k - half]
        out[...] = dot(a, w_buf[k]).astype(BF16)


def run_branch(src, att, w_out, count):
    rows, cols = att.shape
    share = w_out.shape[1] // count
    shape = jax.ShapeDtypeStruct((count // 2, rows, share), BF16)
    return pl.pallas_call(
        lambda *r: branch_kernel(count, *r),
        out_shape=(shape, shape),
        in_specs=[smem(), vmem(), hbm()],
        out_specs=(vmem(), vmem()),
        scratch_shapes=[pltpu.VMEM((count, cols, share), BF16), pltpu.SemaphoreType.DMA((count,))],
        compiler_params=params(48),
        cost_estimate=cost(4),
        name="branches",
    )(src, att, w_out)


def attention_kernel(count, blocks, *refs):
    half = count // 2
    pieces = refs[:count]
    q_ref, d_ref, wk, wv, send, keep, att, mem, keys, values, k_grad, v_grad = refs[count:]
    heads = q_ref.shape[1] // HD
    part = send.shape[1] // blocks
    span = part * count
    scale = HD ** (-0.5)

    def rows(b):
        return slice(b * BLOCK, (b + 1) * BLOCK)

    def ctx(b):
        return slice(b * span, (b + 1) * span)

    def cols(h):
        return slice(h * HD, (h + 1) * HD)

    def softmax(scores):
        scores = scores * scale
        lifted = jnp.exp(scores - jnp.max(scores, axis=-1, keepdims=True))
        return lifted / jnp.sum(lifted, axis=-1, keepdims=True)

    def score_grad(p, dp):
        return (p * (dp - jnp.sum(p * dp, axis=-1, keepdims=True)) * scale).astype(BF16)

    for b in range(blocks):
        for k in range(count):
            mem[b * span + k * part : b * span + (k + 1) * part, :] = pieces[k][
                b * part : (b + 1) * part, :
            ]
    keys[...] = dot(mem[...], wk[...]).astype(BF16)
    values[...] = dot(mem[...], wv[...]).astype(BF16)
    every = [(b, h) for b in range(blocks) for h in range(heads)]
    for start in range(0, len(every), GROUP):
        group = every[start : start + GROUP]
        scores = [dot_nt(q_ref[rows(b), cols(h)], keys[ctx(b), cols(h)]) for b, h in group]
        d_probs = [dot_nt(d_ref[rows(b), cols(h)], values[ctx(b), cols(h)]) for b, h in group]
        probs = [softmax(s) for s in scores]
        weights = [p.astype(BF16) for p in probs]
        d_scores = [score_grad(p, dp) for p, dp in zip(probs, d_probs)]
        for w, ds, (b, h) in zip(weights, d_scores, group):
            att[rows(b), cols(h)] = dot(w, values[ctx(b), cols(h)]).astype(BF16)
            v_grad[ctx(b), cols(h)] = dot_tn(w, d_ref[rows(b), cols(h)]).astype(BF16)
            k_grad[ctx(b), cols(h)] = dot_tn(ds, q_ref[rows(b), cols(h)]).astype(BF16)
    for b in range(blocks):
        terms = (dot_nt(k_grad[ctx(b), :], wk[...]) + dot_nt(v_grad[ctx(b), :], wv[...])).astype(
            BF16
        )
        for k in range(count):
            out = keep.at[k] if k < half else send.at[k - half]
            out[b * part : (b + 1) * part, :] = terms[k * part : (k + 1) * part, :]


def run_attention(pieces, q, d, w_key, w_value, blocks):
    count = len(pieces)
    rows, width = pieces[0].shape
    cols = q.shape[1]
    total = rows * count
    shape = jax.ShapeDtypeStruct((count // 2, rows, width), BF16)
    return pl.pallas_call(
        lambda *r: attention_kernel(count, blocks, *r),
        out_shape=(shape, shape, jax.ShapeDtypeStruct((blocks * BLOCK, cols), BF16)),
        in_specs=[vmem()] * (len(pieces) + 4),
        out_specs=(vmem(), vmem(), vmem()),
        scratch_shapes=[pltpu.VMEM((total, width), BF16)]
        + [pltpu.VMEM((total, cols), BF16)] * 4,
        compiler_params=params(24),
        cost_estimate=cost(9),
        name="attention",
    )(*pieces, q, d, w_key, w_value)


def normed_kernel(enc, gain, out):
    wide = enc[...].astype(F32)
    out[...] = (wide * rms_scale(wide) * gain[...]).astype(BF16)


def run_normed(encodings, gain):
    return pl.pallas_call(
        normed_kernel,
        out_shape=jax.ShapeDtypeStruct(encodings.shape, BF16),
        in_specs=[vmem(), vmem()],
        out_specs=vmem(),
        compiler_params=params(8),
        cost_estimate=cost(0.1),
        name="normed_rows",
    )(encodings, gain.reshape(1, 1, -1))


def outgoing_kernel(req, normed, out):
    for s in range(out.shape[0]):
        out[s] = normed[jnp.maximum(req[s, 0], 0)]


def run_outgoing(requested, normed):
    slots = requested.shape[0]
    return pl.pallas_call(
        outgoing_kernel,
        out_shape=jax.ShapeDtypeStruct((slots,) + normed.shape[1:], BF16),
        in_specs=[smem(), vmem()],
        out_specs=vmem(),
        compiler_params=params(8),
        cost_estimate=cost(0.1),
        name="outgoing_rows",
    )(requested, normed)


def pick_kernel(owner, rows, out, sems):
    copies = []
    for a in range(out.shape[0]):
        cp = pltpu.make_async_copy(rows.at[owner[a]], out.at[a], sems.at[a])
        cp.start()
        copies.append(cp)
    for cp in copies:
        cp.wait()


def run_pick(owner, rows):
    n = owner.shape[0]
    return pl.pallas_call(
        pick_kernel,
        out_shape=jax.ShapeDtypeStruct((n,) + rows.shape[1:], rows.dtype),
        in_specs=[smem(), hbm()],
        out_specs=vmem(),
        scratch_shapes=[pltpu.SemaphoreType.DMA((n,))],
        compiler_params=params(),
        cost_estimate=cost(3.4),
        name="picked_rows",
    )(owner, rows)


def place_kernel(reading, *refs):
    parts, out, total = refs[:-2], refs[-2], refs[-1]
    total[...] = sum(p[...].astype(F32) for p in parts).astype(BF16)
    for s in range(out.shape[0]):
        out[s] = total[reading[s]]


def run_place(reading, parts):
    slots = reading.shape[0]
    shape = parts[0].shape
    return pl.pallas_call(
        place_kernel,
        out_shape=jax.ShapeDtypeStruct((slots,) + shape[1:], BF16),
        in_specs=[smem()] + [vmem()] * len(parts),
        out_specs=vmem(),
        scratch_shapes=[pltpu.VMEM(shape, BF16)],
        compiler_params=params(12),
        cost_estimate=cost(1.7),
        name="placed_grads",
    )(reading, *parts)


def mix_kernel(tok, *refs):
    parts, mixed, squares = refs[:-2], refs[-2], refs[-1]
    summed = sum(p[...].astype(F32) for p in parts)
    out = (tok[...].astype(F32) + summed).astype(BF16)
    mixed[...] = out
    wide = out.astype(F32)
    squares[...] = jnp.sum(wide * wide, axis=1, keepdims=True)


def run_mix(tokens, parts):
    return pl.pallas_call(
        mix_kernel,
        out_shape=(
            jax.ShapeDtypeStruct(tokens.shape, BF16),
            jax.ShapeDtypeStruct((tokens.shape[0], 1), F32),
        ),
        in_specs=[vmem()] * (len(parts) + 1),
        out_specs=(vmem(), vmem()),
        compiler_params=params(12),
        cost_estimate=cost(MIX_COST),
        name="mixed",
    )(tokens, *parts)


def finish_kernel(slot, back, enc, gain, out, buf, sems):
    copies = []
    for j in range(out.shape[0]):
        cp = pltpu.make_async_copy(back.at[slot[j]], buf.at[j], sems.at[j])
        cp.start()
        copies.append(cp)
    wide = enc[...].astype(F32)
    scale = rms_scale(wide)
    hat = wide * scale
    for cp in copies:
        cp.wait()
    up = gain[...] * buf[...].astype(F32)
    out[...] = (scale * (up - hat * jnp.mean(up * hat, axis=-1, keepdims=True))).astype(BF16)


def run_finish(slot, back, encodings, gain):
    rows = encodings.shape[0]
    return pl.pallas_call(
        finish_kernel,
        out_shape=jax.ShapeDtypeStruct(encodings.shape, BF16),
        in_specs=[smem(), hbm(), vmem(), vmem()],
        out_specs=vmem(),
        scratch_shapes=[pltpu.VMEM(encodings.shape, BF16), pltpu.SemaphoreType.DMA((rows,))],
        compiler_params=params(12),
        cost_estimate=cost(1.9),
        name="d_encodings",
    )(slot, back, encodings, gain.reshape(1, 1, -1))


def shards(
    tokens,
    cotangent,
    gain_dec,
    w_query,
    w_out,
    encodings,
    gain_enc,
    w_key,
    w_value,
    gain_post,
    neighbour_ids,
):
    dp_count = lax.axis_size("dp")
    count = lax.axis_size("mp")
    half = count // 2
    share_cols = tokens.shape[1]
    own_rows, own_tokens, width = encodings.shape
    blocks = neighbour_ids.shape[0]
    readings = blocks * neighbour_ids.shape[1]
    here = lax.axis_index("mp")
    steps = jnp.arange(half, dtype=jnp.int32)
    same = (here - 2 * steps) % count
    src = jnp.concatenate([same, same ^ 1]).astype(jnp.int32)

    chosen = neighbour_ids.reshape(readings)
    owner = chosen // own_rows
    local_row = chosen % own_rows
    slots = jnp.arange(dp_count, dtype=jnp.int32)
    matches = owner[:, None] == slots[None, :]
    wanted = jnp.sum(jnp.where(matches, local_row[:, None] + 1, 0), axis=0) - 1
    reading = jnp.sum(
        jnp.where(matches, jnp.arange(readings, dtype=jnp.int32)[:, None], 0), axis=0
    )
    requested = lax.all_to_all(
        jnp.broadcast_to(wanted[:, None], (dp_count, IDS_WIDTH)),
        "dp",
        split_axis=0,
        concat_axis=0,
        tiled=True,
    )
    serves = requested[:, :1] == jnp.arange(own_rows, dtype=jnp.int32)[None, :]
    slot = jnp.sum(jnp.where(serves, slots[:, None], 0), axis=0)

    tok_own = over_chips(tokens, count)
    outgoing = run_outgoing(requested, run_normed(encodings, gain_enc))
    outgoing, cot_in = lax.optimization_barrier((outgoing, cotangent))
    incoming = lax.all_to_all(outgoing, "dp", split_axis=0, concat_axis=0, tiled=True)
    cot_own = over_chips(cot_in, count)
    q = run_query(src, tok_own + [swap(jnp.stack(tok_own), count)], gain_dec, w_query)
    cot_own, q = lax.optimization_barrier((cot_own, q))
    d = run_back(src, cot_own + [swap(p, count) for p in cot_own], w_out)
    picked = run_pick(owner, incoming).reshape(readings * own_tokens, width)
    row_own = over_chips(picked, count)
    crossed, d = lax.optimization_barrier((row_own[1:], d))
    row_own = [picked] + crossed
    rows = row_own + [swap(p, count) for p in row_own]
    send, keep, att = run_attention(rows, q, d, w_key, w_value, blocks)
    pair = pair_sum(keep, swap(send, count))
    att, pair = lax.optimization_barrier((att, pair))
    parts = pair_shares(pair, count)
    b_send, b_keep = run_branch(src, att, w_out, count)
    b_send, parts = lax.optimization_barrier((b_send, parts))
    b_parts = pair_shares(pair_sum(b_keep, swap(b_send, count)), count)
    back_out = run_place(reading, [p.reshape(readings, own_tokens, width) for p in parts])
    back_in = lax.all_to_all(back_out, "dp", split_axis=0, concat_axis=0, tiled=True)

    mixed, squares = run_mix(tokens, b_parts)
    mixed_wide = mixed.astype(F32)
    squares = squares[:, 0]
    d_encodings = run_finish(slot, back_in, encodings, gain_enc)
    total = squares + swap(squares, count)
    for flip in range(1, half, 2):
        total = total + lax.ppermute(total, "mp", chip_flip(count, flip))
    total, d_encodings = lax.optimization_barrier((total, d_encodings))
    post = lax.rsqrt(total / (share_cols * count) + EPS)[:, None]
    gain_here = lax.dynamic_slice_in_dim(gain_post, here * share_cols, share_cols, 0)
    ffn = (mixed_wide * post * gain_here).astype(BF16)
    return (mixed, ffn, d_encodings)


def solution(mesh):
    in_specs = (
        P("dp", "mp"),
        P("dp", "mp"),
        P(),
        P(None, "mp"),
        P("mp", None),
        P("dp", "mp", None),
        P(),
        P(None, "mp"),
        P(None, "mp"),
        P(),
        P("dp", None),
    )
    out_specs = (P("dp", "mp"), P("dp", "mp"), P("dp", "mp", None))
    return jax.shard_map(shards, mesh=mesh, in_specs=in_specs, out_specs=out_specs, check_vma=False)
```

```python
import jax
import jax.numpy as jnp
from jax import lax
from jax.experimental import pallas as pl
from jax.experimental.pallas import tpu as pltpu
from jax.sharding import PartitionSpec as P

HD = 128
BLOCK = 64
NLEN = 128
NEIGH = 2

EPS = 1e-06
F32 = jnp.float32
BF16 = jnp.bfloat16
IDS_WIDTH = 128
GROUP = 8
MIX_COST = 5
MIB = 1024 * 1024


def rms_scale(values):
    return lax.rsqrt(jnp.mean(values * values, axis=-1, keepdims=True) + EPS)


def params(mib=8):
    return pltpu.CompilerParams(vmem_limit_bytes=mib * MIB)


def cost(micros):
    return pl.CostEstimate(flops=int(micros * 1.1e9), bytes_accessed=0, transcendentals=0)


def vmem():
    return pl.BlockSpec(memory_space=pltpu.VMEM)


def hbm():
    return pl.BlockSpec(memory_space=pltpu.HBM)


def smem():
    return pl.BlockSpec(memory_space=pltpu.SMEM)


def chip_shift(count, k):
    return [(i, (i + 2 * k) % count) for i in range(count)]


def chip_flip(count, flip):
    return [(i, i ^ (2 * flip)) for i in range(count)]


def core_swap(count):
    return [(i, i ^ 1) for i in range(count)]


def over_chips(x, count):
    return [x] + [lax.ppermute(x, "mp", chip_shift(count, k)) for k in range(1, count // 2)]


def swap(x, count):
    return lax.ppermute(x, "mp", core_swap(count))


def pair_kernel(keep, other, *outs):
    for k, out in enumerate(outs):
        out[...] = (keep[k].astype(F32) + other[k].astype(F32)).astype(BF16)


def pair_sum(keep, other):
    return pl.pallas_call(
        pair_kernel,
        out_shape=[jax.ShapeDtypeStruct(keep.shape[1:], BF16)] * keep.shape[0],
        in_specs=[vmem(), vmem()],
        out_specs=[vmem()] * keep.shape[0],
        compiler_params=params(12),
        cost_estimate=cost(0.7),
        name="pair_sums",
    )(keep, other)


def pair_shares(pair, count):
    return [pair[0]] + [
        lax.ppermute(pair[k], "mp", chip_shift(count, -k)) for k in range(1, count // 2)
    ]


def shift_matrix(n, lead, transpose):
    r = lax.broadcasted_iota(jnp.int32, (n, n), 0)
    c = lax.broadcasted_iota(jnp.int32, (n, n), 1)
    hit = (r == c + lead) if transpose else (c == r + lead)
    return jnp.where(hit, 1.0, 0.0).astype(BF16)


def dot(a, b):
    return lax.dot_general(a, b, (((1,), (0,)), ((), ())), preferred_element_type=F32)


def dot_nt(a, b):
    return lax.dot_general(a, b, (((1,), (1,)), ((), ())), preferred_element_type=F32)


def dot_tn(a, b):
    return lax.dot_general(a, b, (((0,), (0,)), ((), ())), preferred_element_type=F32)


def views(count, refs):
    half = count // 2
    return list(refs[:half]) + [refs[half].at[k] for k in range(half)], refs[half + 1 :]


def query_kernel(count, src, *refs):
    pieces, rest = views(count, refs)
    gain, w_hbm, out, w_buf, sems = rest
    share = pieces[0].shape[1]
    copies = []
    for k in range(count):
        start = pl.multiple_of(src[k] * share, share)
        cp = pltpu.make_async_copy(w_hbm.at[pl.ds(start, share), :], w_buf.at[k], sems.at[k])
        cp.start()
        copies.append(cp)
    squares = jnp.zeros((pieces[0].shape[0], 1), F32)
    for k in range(count):
        wide = pieces[k][...].astype(F32)
        squares = squares + jnp.sum(wide * wide, axis=1, keepdims=True)
    scale = lax.rsqrt(squares / (share * count) + EPS)
    acc = jnp.zeros(out.shape, F32)
    for k in range(count):
        g = gain[pl.ds(src[k], 1), :]
        normed = (pieces[k][...].astype(F32) * scale * g).astype(BF16)
        copies[k].wait()
        acc = acc + dot(normed, w_buf[k])
    out[...] = dot(shift_matrix(out.shape[0], BLOCK - 1, False), acc.astype(BF16)).astype(BF16)


def run_query(src, pieces, gain, w_query):
    count = 2 * (len(pieces) - 1)
    rows, share = pieces[0].shape
    cols = w_query.shape[1]
    return pl.pallas_call(
        lambda *r: query_kernel(count, *r),
        out_shape=jax.ShapeDtypeStruct((rows, cols), BF16),
        in_specs=[smem()] + [vmem()] * (len(pieces) + 1) + [hbm()],
        out_specs=vmem(),
        scratch_shapes=[pltpu.VMEM((count, share, cols), BF16), pltpu.SemaphoreType.DMA((count,))],
        compiler_params=params(48),
        cost_estimate=cost(3.4),
        name="queries",
    )(src, *pieces, gain.reshape(count, share), w_query)


def back_kernel(count, src, *refs):
    pieces = refs[:count]
    w_hbm, out, w_buf, sems = refs[count:]
    share = pieces[0].shape[1]
    copies = []
    for k in range(count):
        start = pl.multiple_of(src[k] * share, share)
        cp = pltpu.make_async_copy(w_hbm.at[:, pl.ds(start, share)], w_buf.at[k], sems.at[k])
        cp.start()
        copies.append(cp)
    acc = jnp.zeros(out.shape, F32)
    for k in range(count):
        copies[k].wait()
        acc = acc + dot_nt(pieces[k][...], w_buf[k])
    out[...] = dot(shift_matrix(out.shape[0], BLOCK - 1, False), acc.astype(BF16)).astype(BF16)


def run_back(src, pieces, w_out):
    count = len(pieces)
    rows, share = pieces[0].shape
    cols = w_out.shape[0]
    return pl.pallas_call(
        lambda *r: back_kernel(count, *r),
        out_shape=jax.ShapeDtypeStruct((rows, cols), BF16),
        in_specs=[smem()] + [vmem()] * len(pieces) + [hbm()],
        out_specs=vmem(),
        scratch_shapes=[pltpu.VMEM((count, cols, share), BF16), pltpu.SemaphoreType.DMA((count,))],
        compiler_params=params(48),
        cost_estimate=cost(3.4),
        name="d_attended",
    )(src, *pieces, w_out)


def branch_kernel(count, src, att, w_hbm, send, keep, w_buf, sems):
    share = send.shape[2]
    half = count // 2
    copies = []
    order = list(range(half, count)) + list(range(half))
    for k in order:
        start = pl.multiple_of(src[k] * share, share)
        cp = pltpu.make_async_copy(w_hbm.at[:, pl.ds(start, share)], w_buf.at[k], sems.at[k])
        cp.start()
        copies.append(cp)
    a = dot(shift_matrix(att.shape[0], BLOCK - 1, True), att[...]).astype(BF16)
    for k, cp in zip(order, copies):
        cp.wait()
        out = keep.at[k] if k < half else send.at[k - half]
        out[...] = dot(a, w_buf[k]).astype(BF16)


def run_branch(src, att, w_out, count):
    rows, cols = att.shape
    share = w_out.shape[1] // count
    shape = jax.ShapeDtypeStruct((count // 2, rows, share), BF16)
    return pl.pallas_call(
        lambda *r: branch_kernel(count, *r),
        out_shape=(shape, shape),
        in_specs=[smem(), vmem(), hbm()],
        out_specs=(vmem(), vmem()),
        scratch_shapes=[pltpu.VMEM((count, cols, share), BF16), pltpu.SemaphoreType.DMA((count,))],
        compiler_params=params(48),
        cost_estimate=cost(4),
        name="branches",
    )(src, att, w_out)


def attention_kernel(count, blocks, *refs):
    half = count // 2
    pieces = refs[:count]
    q_ref, d_ref, wk, wv, send, keep, att, mem, keys, values, k_grad, v_grad = refs[count:]
    heads = q_ref.shape[1] // HD
    part = send.shape[1] // blocks
    span = part * count
    scale = HD ** (-0.5)

    def rows(b):
        return slice(b * BLOCK, (b + 1) * BLOCK)

    def ctx(b):
        return slice(b * span, (b + 1) * span)

    def cols(h):
        return slice(h * HD, (h + 1) * HD)

    def softmax(scores):
        scores = scores * scale
        lifted = jnp.exp(scores - jnp.max(scores, axis=-1, keepdims=True))
        return lifted / jnp.sum(lifted, axis=-1, keepdims=True)

    def score_grad(p, dp):
        return (p * (dp - jnp.sum(p * dp, axis=-1, keepdims=True)) * scale).astype(BF16)

    for b in range(blocks):
        for k in range(count):
            mem[b * span + k * part : b * span + (k + 1) * part, :] = pieces[k][
                b * part : (b + 1) * part, :
            ]
    keys[...] = dot(mem[...], wk[...]).astype(BF16)
    values[...] = dot(mem[...], wv[...]).astype(BF16)
    every = [(b, h) for b in range(blocks) for h in range(heads)]
    for start in range(0, len(every), GROUP):
        group = every[start : start + GROUP]
        scores = [dot_nt(q_ref[rows(b), cols(h)], keys[ctx(b), cols(h)]) for b, h in group]
        d_probs = [dot_nt(d_ref[rows(b), cols(h)], values[ctx(b), cols(h)]) for b, h in group]
        probs = [softmax(s) for s in scores]
        weights = [p.astype(BF16) for p in probs]
        d_scores = [score_grad(p, dp) for p, dp in zip(probs, d_probs)]
        for w, ds, (b, h) in zip(weights, d_scores, group):
            att[rows(b), cols(h)] = dot(w, values[ctx(b), cols(h)]).astype(BF16)
            v_grad[ctx(b), cols(h)] = dot_tn(w, d_ref[rows(b), cols(h)]).astype(BF16)
            k_grad[ctx(b), cols(h)] = dot_tn(ds, q_ref[rows(b), cols(h)]).astype(BF16)
    for b in range(blocks):
        terms = (dot_nt(k_grad[ctx(b), :], wk[...]) + dot_nt(v_grad[ctx(b), :], wv[...])).astype(
            BF16
        )
        for k in range(count):
            out = keep.at[k] if k < half else send.at[k - half]
            out[b * part : (b + 1) * part, :] = terms[k * part : (k + 1) * part, :]


def run_attention(pieces, q, d, w_key, w_value, blocks):
    count = len(pieces)
    rows, width = pieces[0].shape
    cols = q.shape[1]
    total = rows * count
    shape = jax.ShapeDtypeStruct((count // 2, rows, width), BF16)
    return pl.pallas_call(
        lambda *r: attention_kernel(count, blocks, *r),
        out_shape=(shape, shape, jax.ShapeDtypeStruct((blocks * BLOCK, cols), BF16)),
        in_specs=[vmem()] * (len(pieces) + 4),
        out_specs=(vmem(), vmem(), vmem()),
        scratch_shapes=[pltpu.VMEM((total, width), BF16)]
        + [pltpu.VMEM((total, cols), BF16)] * 4,
        compiler_params=params(24),
        cost_estimate=cost(9),
        name="attention",
    )(*pieces, q, d, w_key, w_value)


def normed_kernel(enc, gain, out):
    wide = enc[...].astype(F32)
    out[...] = (wide * rms_scale(wide) * gain[...]).astype(BF16)


def run_normed(encodings, gain):
    return pl.pallas_call(
        normed_kernel,
        out_shape=jax.ShapeDtypeStruct(encodings.shape, BF16),
        in_specs=[vmem(), vmem()],
        out_specs=vmem(),
        compiler_params=params(8),
        cost_estimate=cost(0.1),
        name="normed_rows",
    )(encodings, gain.reshape(1, 1, -1))


def outgoing_kernel(req, normed, out, sems):
    copies = []
    for s in range(out.shape[0]):
        cp = pltpu.make_async_copy(normed.at[jnp.maximum(req[s, 0], 0)], out.at[s], sems.at[s])
        cp.start()
        copies.append(cp)
    for cp in copies:
        cp.wait()


def run_outgoing(requested, normed):
    slots = requested.shape[0]
    return pl.pallas_call(
        outgoing_kernel,
        out_shape=jax.ShapeDtypeStruct((slots,) + normed.shape[1:], BF16),
        in_specs=[smem(), vmem()],
        out_specs=pl.BlockSpec(memory_space=pl.ANY),
        scratch_shapes=[pltpu.SemaphoreType.DMA((slots,))],
        compiler_params=params(8),
        cost_estimate=cost(0.1),
        name="outgoing_rows",
    )(requested, normed)


def pick_kernel(owner, rows, out, sems):
    copies = []
    for a in range(out.shape[0]):
        cp = pltpu.make_async_copy(rows.at[owner[a]], out.at[a], sems.at[a])
        cp.start()
        copies.append(cp)
    for cp in copies:
        cp.wait()


def run_pick(owner, rows):
    n = owner.shape[0]
    return pl.pallas_call(
        pick_kernel,
        out_shape=jax.ShapeDtypeStruct((n,) + rows.shape[1:], rows.dtype),
        in_specs=[smem(), hbm()],
        out_specs=vmem(),
        scratch_shapes=[pltpu.SemaphoreType.DMA((n,))],
        compiler_params=params(),
        cost_estimate=cost(3.4),
        name="picked_rows",
    )(owner, rows)


def place_kernel(reading, *refs):
    parts, out, total, sems = refs[:-3], refs[-3], refs[-2], refs[-1]
    total[...] = sum(p[...].astype(F32) for p in parts).astype(BF16)
    copies = []
    for s in range(out.shape[0]):
        cp = pltpu.make_async_copy(total.at[reading[s]], out.at[s], sems.at[s])
        cp.start()
        copies.append(cp)
    for cp in copies:
        cp.wait()


def run_place(reading, parts):
    slots = reading.shape[0]
    shape = parts[0].shape
    return pl.pallas_call(
        place_kernel,
        out_shape=jax.ShapeDtypeStruct((slots,) + shape[1:], BF16),
        in_specs=[smem()] + [vmem()] * len(parts),
        out_specs=pl.BlockSpec(memory_space=pl.ANY),
        scratch_shapes=[pltpu.VMEM(shape, BF16), pltpu.SemaphoreType.DMA((slots,))],
        compiler_params=params(12),
        cost_estimate=cost(1.7),
        name="placed_grads",
    )(reading, *parts)


def mix_kernel(tok, *refs):
    parts, mixed, squares = refs[:-2], refs[-2], refs[-1]
    summed = sum(p[...].astype(F32) for p in parts)
    out = (tok[...].astype(F32) + summed).astype(BF16)
    mixed[...] = out
    wide = out.astype(F32)
    squares[...] = jnp.sum(wide * wide, axis=1, keepdims=True)


def run_mix(tokens, parts):
    return pl.pallas_call(
        mix_kernel,
        out_shape=(
            jax.ShapeDtypeStruct(tokens.shape, BF16),
            jax.ShapeDtypeStruct((tokens.shape[0], 1), F32),
        ),
        in_specs=[vmem()] * (len(parts) + 1),
        out_specs=(vmem(), vmem()),
        compiler_params=params(12),
        cost_estimate=cost(MIX_COST),
        name="mixed",
    )(tokens, *parts)


def finish_kernel(slot, back, enc, gain, out, buf, sems):
    copies = []
    for j in range(out.shape[0]):
        cp = pltpu.make_async_copy(back.at[slot[j]], buf.at[j], sems.at[j])
        cp.start()
        copies.append(cp)
    wide = enc[...].astype(F32)
    scale = rms_scale(wide)
    hat = wide * scale
    for cp in copies:
        cp.wait()
    up = gain[...] * buf[...].astype(F32)
    out[...] = (scale * (up - hat * jnp.mean(up * hat, axis=-1, keepdims=True))).astype(BF16)


def run_finish(slot, back, encodings, gain):
    rows = encodings.shape[0]
    return pl.pallas_call(
        finish_kernel,
        out_shape=jax.ShapeDtypeStruct(encodings.shape, BF16),
        in_specs=[smem(), hbm(), vmem(), vmem()],
        out_specs=vmem(),
        scratch_shapes=[pltpu.VMEM(encodings.shape, BF16), pltpu.SemaphoreType.DMA((rows,))],
        compiler_params=params(12),
        cost_estimate=cost(1.9),
        name="d_encodings",
    )(slot, back, encodings, gain.reshape(1, 1, -1))


def shards(
    tokens,
    cotangent,
    gain_dec,
    w_query,
    w_out,
    encodings,
    gain_enc,
    w_key,
    w_value,
    gain_post,
    neighbour_ids,
):
    dp_count = lax.axis_size("dp")
    count = lax.axis_size("mp")
    half = count // 2
    share_cols = tokens.shape[1]
    own_rows, own_tokens, width = encodings.shape
    blocks = neighbour_ids.shape[0]
    readings = blocks * neighbour_ids.shape[1]
    here = lax.axis_index("mp")
    steps = jnp.arange(half, dtype=jnp.int32)
    same = (here - 2 * steps) % count
    src = jnp.concatenate([same, same ^ 1]).astype(jnp.int32)

    chosen = neighbour_ids.reshape(readings)
    owner = chosen // own_rows
    local_row = chosen % own_rows
    slots = jnp.arange(dp_count, dtype=jnp.int32)
    matches = owner[:, None] == slots[None, :]
    wanted = jnp.sum(jnp.where(matches, local_row[:, None] + 1, 0), axis=0) - 1
    reading = jnp.sum(
        jnp.where(matches, jnp.arange(readings, dtype=jnp.int32)[:, None], 0), axis=0
    )
    requested = lax.all_to_all(
        jnp.broadcast_to(wanted[:, None], (dp_count, IDS_WIDTH)),
        "dp",
        split_axis=0,
        concat_axis=0,
        tiled=True,
    )
    serves = requested[:, :1] == jnp.arange(own_rows, dtype=jnp.int32)[None, :]
    slot = jnp.sum(jnp.where(serves, slots[:, None], 0), axis=0)

    tok_own = over_chips(tokens, count)
    outgoing = run_outgoing(requested, run_normed(encodings, gain_enc))
    outgoing, cot_in = lax.optimization_barrier((outgoing, cotangent))
    incoming = lax.all_to_all(outgoing, "dp", split_axis=0, concat_axis=0, tiled=True)
    cot_own = over_chips(cot_in, count)
    q = run_query(src, tok_own + [swap(jnp.stack(tok_own), count)], gain_dec, w_query)
    cot_own, q = lax.optimization_barrier((cot_own, q))
    d = run_back(src, cot_own + [swap(p, count) for p in cot_own], w_out)
    picked = run_pick(owner, incoming).reshape(readings * own_tokens, width)
    row_own = over_chips(picked, count)
    crossed, d = lax.optimization_barrier((row_own[1:], d))
    row_own = [picked] + crossed
    rows = row_own + [swap(p, count) for p in row_own]
    send, keep, att = run_attention(rows, q, d, w_key, w_value, blocks)
    pair = pair_sum(keep, swap(send, count))
    att, pair = lax.optimization_barrier((att, pair))
    parts = pair_shares(pair, count)
    b_send, b_keep = run_branch(src, att, w_out, count)
    b_send, parts = lax.optimization_barrier((b_send, parts))
    b_parts = pair_shares(pair_sum(b_keep, swap(b_send, count)), count)
    back_out = run_place(reading, [p.reshape(readings, own_tokens, width) for p in parts])
    back_in = lax.all_to_all(back_out, "dp", split_axis=0, concat_axis=0, tiled=True)

    mixed, squares = run_mix(tokens, b_parts)
    mixed_wide = mixed.astype(F32)
    squares = squares[:, 0]
    d_encodings = run_finish(slot, back_in, encodings, gain_enc)
    total = squares + swap(squares, count)
    for flip in range(1, half, 2):
        total = total + lax.ppermute(total, "mp", chip_flip(count, flip))
    total, d_encodings = lax.optimization_barrier((total, d_encodings))
    post = lax.rsqrt(total / (share_cols * count) + EPS)[:, None]
    gain_here = lax.dynamic_slice_in_dim(gain_post, here * share_cols, share_cols, 0)
    ffn = (mixed_wide * post * gain_here).astype(BF16)
    return (mixed, ffn, d_encodings)


def solution(mesh):
    in_specs = (
        P("dp", "mp"),
        P("dp", "mp"),
        P(),
        P(None, "mp"),
        P("mp", None),
        P("dp", "mp", None),
        P(),
        P(None, "mp"),
        P(None, "mp"),
        P(),
        P("dp", None),
    )
    out_specs = (P("dp", "mp"), P("dp", "mp"), P("dp", "mp", None))
    return jax.shard_map(shards, mesh=mesh, in_specs=in_specs, out_specs=out_specs, check_vma=False)
```
